32 devices in a mesh: dp: 4 (over x, core), fsdp: 8 (over z, y).
Axes of the slice: x: 2, y: 2, z: 4, core: 2. Of those that a mesh axis runs over, the one named last changes fastest.
Arguments:
- x_short: bfloat16 [32, 256, 1152], P(('dp', 'fsdp')), may hold values from -6 to 6
- x_long: bfloat16 [8192, 1152], P(('dp', 'fsdp')), may hold values from -6 to 6
- short_cond: float32 [32, 1152], P(('dp', 'fsdp')), may hold values from -6 to 6
- long_cond: float32 [8, 1152], P('dp'), may hold values from -6 to 6
- short_heads: int32 [32, 16], P(('dp', 'fsdp')), may hold values 0 or 1
- long_heads: int32 [8, 16], P('dp'), may hold values 0 or 1
- short_groups: int32 [32, 36], P(('dp', 'fsdp')), may hold values 0 or 1
- long_groups: int32 [8, 36], P('dp'), may hold values 0 or 1
- short_keep: int32 [32, 256], P(('dp', 'fsdp')), may hold values 0 or 1
- long_keep: int32 [8192], P(('dp', 'fsdp')), may hold values 0 or 1
- w_ada: bfloat16 [1152, 6912], P('fsdp'), may hold values from -0.1875 to 0.1875
- b_ada: bfloat16 [6912], P('fsdp'), may hold values from -2 to 2
- w_head_router: bfloat16 [1152, 16], P('fsdp'), may hold values from -0.375 to 0.375
- w_group_router: bfloat16 [1152, 36], P('fsdp'), may hold values from -0.375 to 0.375
- w_qkv: bfloat16 [1152, 3456], P('fsdp'), may hold values from -0.1875 to 0.1875
- w_proj: bfloat16 [1152, 1152], P('fsdp'), may hold values from -1.5 to 1.5
- b_proj: bfloat16 [1152], P('fsdp'), may hold values from -2 to 2
- w_fc1: bfloat16 [1152, 4608], P('fsdp'), may hold values from -0.1875 to 0.1875
- b_fc1: bfloat16 [4608], P('fsdp'), may hold values from -2 to 2
- w_fc2: bfloat16 [4608, 1152], P('fsdp'), may hold values from -0.09375 to 0.09375
- b_fc2: bfloat16 [1152], P('fsdp'), may hold values from -2 to 2
- g_short: bfloat16 [32, 256, 1152], P(('dp', 'fsdp')), may hold values from -6 to 6
- g_long: bfloat16 [8192, 1152], P(('dp', 'fsdp')), may hold values from -6 to 6
Outputs:
- y_short: bfloat16 [32, 256, 1152], P(('dp', 'fsdp'))
- y_long: bfloat16 [8192, 1152], P(('dp', 'fsdp'))
- dx_short: bfloat16 [32, 256, 1152], P(('dp', 'fsdp'))
- dx_long: bfloat16 [8192, 1152], P(('dp', 'fsdp'))
- d_short_cond: float32 [32, 1152], P(('dp', 'fsdp'))
- d_long_cond: float32 [8, 1152], P('dp')
- g_w_ada: float32 [1152, 6912], P('fsdp')
- g_b_ada: float32 [6912], P('fsdp')
- g_w_head_router: float32 [1152, 16], P('fsdp')
- g_w_group_router: float32 [1152, 36], P('fsdp')
- g_w_qkv: float32 [1152, 3456], P('fsdp')
- g_w_proj: float32 [1152, 1152], P('fsdp')
- g_b_proj: float32 [1152], P('fsdp')
- g_w_fc1: float32 [1152, 4608], P('fsdp')
- g_b_fc1: float32 [4608], P('fsdp')
- g_w_fc2: float32 [4608, 1152], P('fsdp')
- g_b_fc2: float32 [1152], P('fsdp')
The draws below stay inside these ranges and needn't reach their ends.
All inputs are finite; a program needn't handle non-finite values. No bound on the sum of `short_heads` or of `long_heads` or of `short_groups` or of `long_groups` or of `short_keep` or of `long_keep` on one device may be relied on, other than what follows from the above.
Results may differ from the reference program's by a relative error of at most 0.019.
Values may be sent and summed in bfloat16 or wider, within the bound.
A program may use at most 320 MiB of HBM per device.

```python
import jax
import jax.numpy as jnp
from jax import lax

D = 1152
HEADS = 16
HEAD_DIM = 72
FF = 4608
CHAN = 128
LEN_S = 256
LEN_L = 1024
GROUPS = 36
SHORT_ITEMS = 32
LONG_ITEMS = 8


def set_ends(drawn, stream_key, smallest, high):
    longest = drawn.shape.index(max(drawn.shape))
    spots = []
    for shift in (0, 1):
        where = [jax.random.randint(jax.random.fold_in(stream_key, axis), (), 0, length) for axis, length in enumerate(drawn.shape)]
        where[longest] = (where[longest] + shift) % drawn.shape[longest]
        spots.append(tuple(where))
    return drawn.at[spots[0]].set(smallest).at[spots[1]].set(high)


def steps_of(own_key, dims, shards, least, high):
    factor_of, own = 1.0, jax.random.fold_in(own_key, 6)
    for position, shards_of in shards:
        draws = jnp.exp(jax.random.uniform(jax.random.fold_in(own, position), (shards_of,), jnp.float32, least / len(shards), high / len(shards)))
        factor_of = factor_of * jnp.repeat(draws, dims[position] // shards_of).reshape([-1 if axis == position else 1 for axis in range(len(dims))])
    return factor_of


def noise(stream_key, extent, spread, most, cuts=(), held_as=jnp.bfloat16):
    array = spread * jax.random.normal(stream_key, extent, jnp.float32)
    if cuts:
        array = array * steps_of(stream_key, extent, cuts, -0.22, 0.18)
    return jnp.clip(array, -most, most).astype(held_as)


def setup_inputs(seed: int = 0) -> dict:
    seeds = jax.random.split(jax.random.key(seed), 24)
    return {
        "x_short": noise(seeds[0], (SHORT_ITEMS, LEN_S, D), 1.0, 6.0, ((0, 32),)),
        "x_long": noise(seeds[1], (LONG_ITEMS * LEN_L, D), 1.0, 6.0, ((0, 32),)),
        "short_cond": noise(seeds[2], (SHORT_ITEMS, D), 1.0, 6.0, ((0, 32),), jnp.float32),
        "long_cond": noise(seeds[3], (LONG_ITEMS, D), 1.0, 6.0, ((0, 4),), jnp.float32),
        "short_heads": set_ends((jax.random.randint(seeds[4], (SHORT_ITEMS, HEADS), 0, 4) < 3).astype(jnp.int32), jax.random.fold_in(seeds[4], 1), 0, 1),
        "long_heads": set_ends((jax.random.randint(seeds[5], (LONG_ITEMS, HEADS), 0, 4) < 3).astype(jnp.int32), jax.random.fold_in(seeds[5], 1), 0, 1),
        "short_groups": set_ends((jax.random.randint(seeds[6], (SHORT_ITEMS, GROUPS), 0, 4) < 3).astype(jnp.int32), jax.random.fold_in(seeds[6], 1), 0, 1),
        "long_groups": set_ends((jax.random.randint(seeds[7], (LONG_ITEMS, GROUPS), 0, 4) < 3).astype(jnp.int32), jax.random.fold_in(seeds[7], 1), 0, 1),
        "short_keep": set_ends((jax.random.randint(seeds[8], (SHORT_ITEMS, LEN_S), 0, 4) < 3).astype(jnp.int32), jax.random.fold_in(seeds[8], 1), 0, 1),
        "long_keep": set_ends((jax.random.randint(seeds[9], (LONG_ITEMS * LEN_L,), 0, 4) < 3).astype(jnp.int32), jax.random.fold_in(seeds[9], 1), 0, 1),
        "w_ada": noise(seeds[10], (D, 6 * D), D ** -0.5, 0.1875, ((0, 8),)),
        "b_ada": noise(seeds[11], (6 * D,), 0.3, 2.0, ((0, 8),)),
        "w_head_router": noise(seeds[12], (D, HEADS), (D // 4) ** -0.5, 0.375, ((0, 8),)),
        "w_group_router": noise(seeds[13], (D, GROUPS), (D // 4) ** -0.5, 0.375, ((0, 8),)),
        "w_qkv": noise(seeds[14], (D, 3 * D), D ** -0.5, 0.1875, ((0, 8),)),
        "w_proj": noise(seeds[15], (D, D), (D // 64) ** -0.5, 1.5, ((0, 8),)),
        "b_proj": noise(seeds[16], (D,), 0.3, 2.0, ((0, 8),)),
        "w_fc1": noise(seeds[17], (D, FF), D ** -0.5, 0.1875, ((0, 8),)),
        "b_fc1": noise(seeds[18], (FF,), 0.3, 2.0, ((0, 8),)),
        "w_fc2": noise(seeds[19], (FF, D), FF ** -0.5, 0.09375, ((0, 8),)),
        "b_fc2": noise(seeds[20], (D,), 0.3, 2.0, ((0, 8),)),
        "g_short": noise(seeds[21], (SHORT_ITEMS, LEN_S, D), 1.0, 6.0, ((0, 32),)),
        "g_long": noise(seeds[22], (LONG_ITEMS * LEN_L, D), 1.0, 6.0, ((0, 32),)),
    }


@jax.custom_vjp
def low(v):
    return lax.optimization_barrier(v.astype(jnp.bfloat16)).astype(jnp.float32)

@jax.custom_vjp
def low_back(v):
    return v

def low_keep(v):
    return (low(v), None)

def low_pass(kept, grad):
    return (grad,)

def back_keep(v):
    return (v, None)

def back_low(kept, grad):
    return (low(grad),)
low.defvjp(low_keep, low_pass)
low_back.defvjp(back_keep, back_low)
highest = lax.Precision.HIGHEST

def matmul(left, right):
    return jnp.dot(left, right, precision=highest, preferred_element_type=jnp.float32)

def layer_norm(values):
    average = lax.optimization_barrier(jnp.mean(values, axis=-1, keepdims=True))
    centred = values - average
    variance = lax.optimization_barrier(jnp.mean(centred * centred, axis=-1, keepdims=True))
    return centred * lax.rsqrt(variance + 1e-06)

def conditioning(condition, head_mask, group_mask, w_ada, b_ada, w_head_router, w_group_router):
    activated = low(jax.nn.silu(condition))
    modulation = low_back(matmul(activated, w_ada) + b_ada)
    head_logit = low_back(matmul(activated, w_head_router))
    group_logit = low_back(matmul(activated, w_group_router))
    head_gate = head_mask.astype(jnp.float32) * 2.0 * jax.nn.sigmoid(head_logit)
    group_gate = group_mask.astype(jnp.float32) * 2.0 * jax.nn.sigmoid(group_logit)
    return (modulation, head_gate, group_gate)

def block(tokens, modulation, head_gate, group_gate, keep_rows, w_qkv, w_proj, b_proj, w_fc1, b_fc1, w_fc2, b_fc2):
    shift1, scale1, gate1, shift2, scale2, gate2 = jnp.split(modulation, 6)
    length = tokens.shape[0]
    hidden1 = low(layer_norm(tokens) * (1.0 + scale1) + shift1)
    qkv_rows = low(low_back(matmul(hidden1, w_qkv)))
    queries = qkv_rows[:, :D].reshape(length, HEADS, HEAD_DIM)
    key_rows = qkv_rows[:, D:2 * D].reshape(length, HEADS, HEAD_DIM)
    value_rows = qkv_rows[:, 2 * D:].reshape(length, HEADS, HEAD_DIM)
    scores = low_back(jnp.einsum('qhe,khe->hqk', queries, key_rows, precision=highest) * HEAD_DIM ** (-0.5))
    row_max = lax.optimization_barrier(jnp.max(scores, axis=-1, keepdims=True))
    exponent = jnp.exp(scores - row_max)
    soft_weights = exponent / lax.optimization_barrier(jnp.sum(exponent, axis=-1, keepdims=True))
    head_out = low_back(jnp.einsum('hqk,khe->qhe', low(soft_weights), value_rows, precision=highest))
    attention = low((head_out * head_gate[None, :, None]).reshape(length, D))
    projected = low_back(matmul(attention, w_proj) + b_proj)
    mixed = tokens + gate1 * projected
    hidden2 = low(layer_norm(mixed) * (1.0 + scale2) + shift2)
    up_rows = low_back(matmul(hidden2, w_fc1) + b_fc1)
    activated = low(jax.nn.gelu(up_rows, approximate=True) * jnp.repeat(group_gate, CHAN))
    down_rows = low_back(matmul(activated, w_fc2) + b_fc2)
    return mixed + gate2 * keep_rows[:, None] * down_rows

def reference(x_short, x_long, short_cond, long_cond, short_heads, long_heads, short_groups, long_groups, short_keep, long_keep, w_ada, b_ada, w_head_router, w_group_router, w_qkv, w_proj, b_proj, w_fc1, b_fc1, w_fc2, b_fc2, g_short, g_long):
    weights = tuple((weight.astype(jnp.float32) for weight in (w_ada, b_ada, w_head_router, w_group_router, w_qkv, w_proj, b_proj, w_fc1, b_fc1, w_fc2, b_fc2)))
    short_rows = x_short.astype(jnp.float32)
    long_rows = x_long.astype(jnp.float32).reshape(LONG_ITEMS, LEN_L, D)
    short_flags = short_keep.astype(jnp.float32)
    long_flags = long_keep.astype(jnp.float32).reshape(LONG_ITEMS, LEN_L)

    def forward(short_in, long_in, short_condition, long_condition, weight_set):

        def run(tokens, condition, head_mask, group_mask, keep_rows):
            modulation, head_gate, group_gate = conditioning(condition, head_mask, group_mask, *weight_set[:4])
            return block(tokens, modulation, head_gate, group_gate, keep_rows, *weight_set[4:])
        checked = jax.checkpoint(run)
        short_out = lax.map(lambda item_args: checked(*item_args), (short_in, short_condition, short_heads, short_groups, short_flags))
        long_out = lax.map(lambda item_args: checked(*item_args), (long_in, long_condition, long_heads, long_groups, long_flags))
        return (short_out, long_out)
    (short_out, long_out), pullback = jax.vjp(forward, short_rows, long_rows, short_cond, long_cond, weights)
    cotangents = (g_short.astype(jnp.float32), g_long.astype(jnp.float32).reshape(LONG_ITEMS, LEN_L, D))
    d_short, d_long, d_short_condition, d_long_condition, d_weights = pullback(cotangents)
    return (short_out.astype(jnp.bfloat16), long_out.reshape(LONG_ITEMS * LEN_L, D).astype(jnp.bfloat16), d_short.astype(jnp.bfloat16), d_long.reshape(LONG_ITEMS * LEN_L, D).astype(jnp.bfloat16), d_short_condition, d_long_condition, d_weights[0], d_weights[1], d_weights[2], d_weights[3], d_weights[4], d_weights[5], d_weights[6], d_weights[7], d_weights[8], d_weights[9], d_weights[10])
```

```python
import jax
import jax.numpy as jnp
from jax import lax
from jax.sharding import PartitionSpec as P

CHAN = 128
SPLIT = 4


epsilon = 1e-06


def swap(value, axis, mask):
    pairs = [(source, source ^ mask) for source in range(lax.axis_size(axis))]
    return lax.ppermute(value, axis, pairs)


def place(buffer, block, *where):
    return lax.dynamic_update_slice(buffer, block, where)


def gather_small(rows, axis):
    mask = 1
    while mask < lax.axis_size(axis):
        rows = jnp.concatenate([rows, swap(rows, axis, mask)], 0)
        mask *= 2
    return rows


def gather_blocks(block, y_first):
    half = lax.axis_size("fsdp") // 2
    position = lax.axis_index("fsdp") // 2
    line = jnp.zeros((half,) + block.shape, block.dtype)
    line = place(line, block[None], position, 0, 0)
    for step in range(1, half):
        line = place(line, swap(block, "fsdp", 2 * step)[None], position ^ step, 0, 0)
    held = {(0, 0): line}
    if y_first:
        held[0, 1] = swap(line, "fsdp", 1)
        held[2, 0] = swap(line, "dp", 2)
        held[2, 1] = swap(held[0, 1], "dp", 2)
    else:
        held[2, 0] = swap(line, "dp", 2)
        held[0, 1] = swap(line, "fsdp", 1)
        held[2, 1] = swap(held[2, 0], "fsdp", 1)
    for role, side in list(held):
        held[role ^ 1, side] = swap(held[role, side], "dp", 1)
    return held


def stack_roles(parts, rows):
    role, side = lax.axis_index("dp"), lax.axis_index("fsdp") % 2
    half = lax.axis_size("fsdp") // 2
    width = sum(part[0, 0].shape[2] for part in parts)
    whole = jnp.zeros((4, half, 2, rows, width), jnp.bfloat16)
    offset = 0
    for part in parts:
        for (role_xor, side_xor), line in part.items():
            whole = place(
                whole, line[None, :, None], role ^ role_xor, 0, side ^ side_xor, 0, offset
            )
        offset += part[0, 0].shape[2]
    return whole.reshape(4, half * 2 * rows, width)


def stack_rows(part, rows):
    role, side = lax.axis_index("dp"), lax.axis_index("fsdp") % 2
    half = lax.axis_size("fsdp") // 2
    width = part[0, 0].shape[2]
    whole = jnp.zeros((half, 2, 4, rows, width), jnp.bfloat16)
    for (role_xor, side_xor), line in part.items():
        whole = place(whole, line[:, None, None], 0, side ^ side_xor, role ^ role_xor, 0, 0)
    return whole.reshape(half * 8 * rows, width)


def low(value):
    return value.astype(jnp.bfloat16)


def scatter_blocks(terms, y_first):
    half = lax.axis_size("fsdp") // 2
    position = lax.axis_index("fsdp") // 2
    side = lax.axis_index("fsdp") % 2

    def on_side(value, which):
        return lax.dynamic_index_in_dim(value, which, 1, keepdims=False)

    far = terms[2] + swap(low(terms[3]), "dp", 1).astype(jnp.float32)
    near = terms[0] + swap(low(terms[1]), "dp", 1).astype(jnp.float32)
    if y_first:
        far = on_side(far, side) + swap(low(on_side(far, side ^ 1)), "fsdp", 1)
        near = on_side(near, side) + swap(low(on_side(near, side ^ 1)), "fsdp", 1)
        near = near + swap(low(far), "dp", 2)
    else:
        near = near + swap(low(far), "dp", 2)
        near = on_side(near, side) + swap(low(on_side(near, side ^ 1)), "fsdp", 1)

    def at(index):
        return lax.dynamic_index_in_dim(near, index, 0, keepdims=False)

    total = at(position)
    for step in range(1, half):
        total = total + swap(low(at(position ^ step)), "fsdp", 2 * step)
    return low(total)


def share_roles(block):
    role = lax.axis_index("dp")
    whole = jnp.zeros((4,) + block.shape, jnp.float32)
    whole = place(whole, block[None].astype(jnp.float32), role, 0, 0)
    for step in range(1, 4):
        whole = place(whole, swap(block, "dp", step)[None].astype(jnp.float32), role ^ step, 0, 0)
    return whole


def product(left, right):
    return jnp.dot(left, right, preferred_element_type=jnp.float32)


def product_tn(left, right):
    return lax.dot_general(
        left, right, (((0,), (0,)), ((), ())), preferred_element_type=jnp.float32
    )


def product_nt(left, right):
    return lax.dot_general(
        left, right, (((1,), (1,)), ((), ())), preferred_element_type=jnp.float32
    )


def spread(per_slot, short_count, len_short, quarter_rows):
    width = per_slot.shape[1]
    short_part = jnp.broadcast_to(
        per_slot[:short_count, None, :], (short_count, len_short, width)
    ).reshape(short_count * len_short, width)
    long_part = jnp.broadcast_to(per_slot[short_count:], (quarter_rows, width))
    return jnp.concatenate([short_part, long_part], 0)


def slot_sum(values, short_count, len_short):
    short_rows = short_count * len_short
    short_part = jnp.sum(
        values[:short_rows].reshape((short_count, len_short) + values.shape[1:]), axis=1
    )
    long_part = jnp.sum(values[short_rows:], axis=0, keepdims=True)
    return jnp.concatenate([short_part, long_part], 0)


def norm_parts(values):
    average = jnp.mean(values, axis=-1, keepdims=True)
    centred = values - average
    variance = jnp.mean(centred * centred, axis=-1, keepdims=True)
    inverse = lax.rsqrt(variance + epsilon)
    return (centred * inverse, inverse)


def norm_back(gradient, normed, inverse):
    return inverse * (
        gradient
        - jnp.mean(gradient, axis=-1, keepdims=True)
        - normed * jnp.mean(gradient * normed, axis=-1, keepdims=True)
    )


def silu_grad(values):
    sigmoid_value = jax.nn.sigmoid(values)
    return sigmoid_value * (1.0 + values * (1.0 - sigmoid_value))


def attend(queries, key_rows, value_rows, scaling):
    scores = (
        jnp.einsum("nqhe,nkhe->nhqk", queries, key_rows, preferred_element_type=jnp.float32)
        * scaling
    )
    row_max = jnp.max(scores, axis=-1, keepdims=True)
    exponent = jnp.exp(scores - row_max)
    row_total = jnp.sum(exponent, axis=-1, keepdims=True)
    soft_weights = exponent / row_total
    head_out = jnp.einsum(
        "nhqk,nkhe->nqhe",
        soft_weights.astype(jnp.bfloat16),
        value_rows,
        preferred_element_type=jnp.float32,
    )
    return (head_out, row_max + jnp.log(row_total))


def attend_back(queries, key_rows, value_rows, log_total, d_out, scaling):
    scores = (
        jnp.einsum("nqhe,nkhe->nhqk", queries, key_rows, preferred_element_type=jnp.float32)
        * scaling
    )
    soft_weights = jnp.exp(scores - log_total)
    d_weights = jnp.einsum("nqhe,nkhe->nhqk", d_out, value_rows, preferred_element_type=jnp.float32)
    inner = jnp.sum(soft_weights * d_weights, axis=-1, keepdims=True)
    d_scores = (soft_weights * (d_weights - inner)).astype(jnp.bfloat16)
    d_queries = (
        jnp.einsum("nhqk,nkhe->nqhe", d_scores, key_rows, preferred_element_type=jnp.float32)
        * scaling
    )
    d_keys = (
        jnp.einsum("nhqk,nqhe->nkhe", d_scores, queries, preferred_element_type=jnp.float32)
        * scaling
    )
    d_values = jnp.einsum(
        "nhqk,nqhe->nkhe",
        soft_weights.astype(jnp.bfloat16),
        d_out,
        preferred_element_type=jnp.float32,
    )
    return (d_queries, d_keys, d_values)


def gelu_tanh(values):
    return jax.nn.gelu(values, approximate=True)


def per_device(
    x_short,
    x_long,
    short_cond,
    long_cond,
    short_heads,
    long_heads,
    short_groups,
    long_groups,
    short_keep,
    long_keep,
    w_ada,
    b_ada,
    w_head_router,
    w_group_router,
    w_qkv,
    w_proj,
    b_proj,
    w_fc1,
    b_fc1,
    w_fc2,
    b_fc2,
    g_short,
    g_long,
):
    short_count, len_short, model_width = x_short.shape
    quarter_rows = x_long.shape[0]
    head_count = w_head_router.shape[1]
    head_width = model_width // head_count
    group_count = w_group_router.shape[1]
    slot_count = short_count + 1
    short_rows = short_count * len_short
    row_count = short_rows + quarter_rows
    scaling = head_width ** (-0.5)
    fsdp_index = lax.axis_index("fsdp")
    fsdp_count = lax.axis_size("fsdp")
    role = lax.axis_index("dp")
    group_row = fsdp_index // SPLIT
    first_member = (fsdp_index % SPLIT == 0).astype(jnp.float32)
    group_total = fsdp_count // SPLIT
    half = fsdp_count // 2
    shard_rows = w_qkv.shape[0]
    unit_rows = w_fc2.shape[0] // 4
    first_columns = (model_width // 256 + 1) * 128

    def block_of(matrix, start, width):
        return lax.dynamic_slice_in_dim(matrix, start, width, 1)

    mixed_shard = jnp.concatenate([w_qkv, w_proj], 1)
    first_part = gather_blocks(block_of(mixed_shard, role * model_width, first_columns), True)
    second_part = gather_blocks(
        block_of(mixed_shard, role * model_width + first_columns, model_width - first_columns), False
    )
    attention_full = stack_roles([first_part, second_part], shard_rows)
    fc1_part = gather_blocks(block_of(w_fc1, role * model_width, model_width), True)
    fc2_part = gather_blocks(lax.dynamic_slice_in_dim(w_fc2, role * unit_rows, unit_rows, 0), False)
    short_act = low(jax.nn.silu(short_cond))
    long_act = low(jax.nn.silu(long_cond))
    message = jnp.concatenate([short_act, b_proj[None], b_fc1[None], b_fc2[None]], 1)
    message = gather_small(message, "fsdp")
    members = jnp.arange(fsdp_count) ^ fsdp_index
    act_rows = message[:, :model_width]
    biases = jnp.take(message[:, model_width:], members, axis=0).astype(jnp.float32)
    proj_bias = biases[:, :shard_rows].reshape(-1)
    fc1_bias = biases[:, shard_rows : shard_rows + 4 * shard_rows].reshape(-1)
    fc2_bias = biases[:, 5 * shard_rows :].reshape(-1)
    groups = jnp.arange(group_total) ^ group_row
    item_act = jnp.concatenate([act_rows, jnp.take(long_act, groups, axis=0)], 0)

    def own_columns(rows):
        return lax.dynamic_slice_in_dim(rows, fsdp_index * shard_rows, shard_rows, 1)

    item_columns = own_columns(item_act)
    bias_row = lax.dynamic_update_slice_in_dim(
        jnp.zeros((fsdp_count * b_ada.shape[0],), jnp.float32),
        b_ada.astype(jnp.float32),
        fsdp_index * b_ada.shape[0],
        0,
    )
    partial = jnp.concatenate(
        [
            product(item_columns, w_ada) + bias_row,
            product(item_columns, w_head_router),
            product(item_columns, w_group_router),
        ],
        1,
    )
    short_part, long_part = partial[:fsdp_count], partial[fsdp_count:]
    mask = fsdp_count // 2
    while mask:
        if mask >= SPLIT:
            step = mask // SPLIT
            taken = swap(jnp.concatenate([short_part[mask:], long_part[step:]], 0), "fsdp", mask)
            long_part = long_part[:step] + taken[mask:]
        else:
            taken = swap(jnp.concatenate([short_part[mask:], long_part], 0), "fsdp", mask)
            long_part = long_part + taken[mask:]
        short_part = short_part[:mask] + taken[:mask]
        mask //= 2
    conditioned = jnp.concatenate([short_part, long_part], 0)
    mod_width = 6 * model_width
    modulation = conditioned[:, :mod_width]
    head_sigmoid = jax.nn.sigmoid(conditioned[:, mod_width : mod_width + head_count])
    group_sigmoid = jax.nn.sigmoid(conditioned[:, mod_width + head_count :])
    head_mask = jnp.concatenate(
        [short_heads, lax.dynamic_slice_in_dim(long_heads, group_row, 1, 0)], 0
    ).astype(jnp.float32)
    group_mask = jnp.concatenate(
        [short_groups, lax.dynamic_slice_in_dim(long_groups, group_row, 1, 0)], 0
    ).astype(jnp.float32)
    head_gate = head_mask * 2.0 * head_sigmoid
    group_gate = group_mask * 2.0 * group_sigmoid
    shift1, scale1, gate1, shift2, scale2, gate2 = jnp.split(
        spread(modulation, short_count, len_short, quarter_rows), 6, axis=1
    )
    x_rows = jnp.concatenate([x_short.reshape(short_rows, model_width), x_long], 0).astype(
        jnp.float32
    )
    keep_rows = jnp.concatenate([short_keep.reshape(short_rows), long_keep], 0).astype(jnp.float32)[
        :, None
    ]
    normed1, inverse1 = norm_parts(x_rows)
    hidden1 = low(normed1 * (1.0 + scale1) + shift1)
    q_rows, k_rows, v_rows = (low(product(hidden1, attention_full[part])) for part in range(3))

    def split_heads(rows, count):
        return rows.reshape(count, -1, head_count, head_width)

    own_k, own_v = k_rows[short_rows:], v_rows[short_rows:]
    k_y = swap(own_k, "fsdp", 1)
    v_z = swap(own_v, "fsdp", 2)
    k_far = swap(jnp.concatenate([own_k, k_y], 0), "fsdp", 2)
    v_far = swap(jnp.concatenate([own_v, v_z], 0), "fsdp", 1)
    long_keys = split_heads(jnp.concatenate([own_k, k_y, k_far], 0), 1)
    long_values = split_heads(
        jnp.concatenate([own_v, v_far[:quarter_rows], v_z, v_far[quarter_rows:]], 0), 1
    )
    short_q, short_k, short_v = (
        split_heads(rows[:short_rows], short_count) for rows in (q_rows, k_rows, v_rows)
    )
    short_out, short_log = attend(short_q, short_k, short_v, scaling)
    long_queries = split_heads(q_rows[short_rows:], 1)
    long_out, long_log = attend(long_queries, long_keys, long_values, scaling)
    head_rows = jnp.concatenate(
        [
            short_out.reshape(short_rows, head_count, head_width),
            long_out.reshape(quarter_rows, head_count, head_width),
        ],
        0,
    )
    head_gate_rows = spread(head_gate, short_count, len_short, quarter_rows)[:, :, None]
    attention = low((head_rows * head_gate_rows).reshape(row_count, model_width))
    projected = product(attention, attention_full[3]) + proj_bias
    mixed = x_rows + gate1 * projected
    fc1_full = stack_roles([fc1_part], shard_rows)
    fc2_full = stack_rows(fc2_part, unit_rows)
    fc2_full = fc2_full.reshape(4, -1, model_width)
    normed2, inverse2 = norm_parts(mixed)
    hidden2 = low(normed2 * (1.0 + scale2) + shift2)
    channel_gate = spread(
        jnp.repeat(group_gate, CHAN, axis=1), short_count, len_short, quarter_rows
    )
    gates = jnp.split(channel_gate, 4, axis=1)
    gelus, pulls, activated = [], [], []
    down_rows = fc2_bias
    for part in range(4):
        up_rows = product(hidden2, fc1_full[part]) + fc1_bias.reshape(4, -1)[part]
        gelu_value, gelu_pull = jax.vjp(gelu_tanh, up_rows)
        gelus.append(gelu_value)
        pulls.append(gelu_pull)
        activated.append(low(gelu_value * gates[part]))
        down_rows = down_rows + product(activated[part], fc2_full[part])
    out_rows = mixed + gate2 * keep_rows * down_rows
    y_short = low(out_rows[:short_rows].reshape(x_short.shape))
    y_long = low(out_rows[short_rows:])
    gradient = jnp.concatenate([g_short.reshape(short_rows, model_width), g_long], 0).astype(
        jnp.float32
    )
    d_down = low(gradient * gate2 * keep_rows)
    slot_gate2 = slot_sum(gradient * keep_rows * down_rows, short_count, len_short)
    grad_fc2 = jnp.concatenate([low(product_tn(part, d_down)) for part in activated], 0)
    grad_fc2 = grad_fc2.reshape(half, 2, 4, unit_rows, model_width)
    fc2_terms = [
        lax.dynamic_index_in_dim(grad_fc2, role ^ step, 2, keepdims=False) for step in range(4)
    ]
    fc2_block = scatter_blocks(fc2_terms, False)
    g_w_fc2 = share_roles(fc2_block).reshape(4 * unit_rows, model_width)
    d_ups, d_groups = [], []
    d_hidden2 = 0.0
    for part in range(4):
        d_activated = product_nt(d_down, fc2_full[part])
        d_channel = slot_sum(d_activated * gelus[part], short_count, len_short)
        d_groups.append(jnp.sum(d_channel.reshape(slot_count, -1, CHAN), axis=-1))
        d_ups.append(low(pulls[part](d_activated * gates[part])[0]))
        d_hidden2 = d_hidden2 + product_nt(d_ups[part], fc1_full[part])
    d_group = jnp.concatenate(d_groups, 1)
    up_stack = jnp.stack(d_ups)

    def role_term(left, right):
        return product_tn(left, right).reshape(half, 2, shard_rows, -1)

    fc1_terms = [
        role_term(hidden2, lax.dynamic_index_in_dim(up_stack, role ^ step, 0, keepdims=False))
        for step in range(4)
    ]
    fc1_block = scatter_blocks(fc1_terms, True)
    g_w_fc1 = share_roles(fc1_block).transpose(1, 0, 2).reshape(shard_rows, -1)
    slot_shift2 = slot_sum(d_hidden2, short_count, len_short)
    slot_scale2 = slot_sum(d_hidden2 * normed2, short_count, len_short)
    d_mixed = gradient + norm_back(d_hidden2 * (1.0 + scale2), normed2, inverse2)
    d_projected = low(d_mixed * gate1)
    slot_gate1 = slot_sum(d_mixed * projected, short_count, len_short)
    d_attention = product_nt(d_projected, attention_full[3]).reshape(
        row_count, head_count, head_width
    )
    d_head = slot_sum(jnp.sum(d_attention * head_rows, axis=-1), short_count, len_short)
    d_heads = low(d_attention * head_gate_rows)
    bias_grad = jnp.concatenate(
        [jnp.sum(d_projected, axis=0, dtype=jnp.float32)]
        + [jnp.sum(d_up, axis=0, dtype=jnp.float32) for d_up in d_ups]
        + [jnp.sum(d_down, axis=0, dtype=jnp.float32)]
    )[None]
    for axis in ("fsdp", "dp"):
        mask = 1
        while mask < lax.axis_size(axis):
            bias_grad = bias_grad + swap(bias_grad, axis, mask)
            mask *= 2
    bias_grad = bias_grad[0]

    def own_bias(start, count):
        return lax.dynamic_slice_in_dim(bias_grad, start + fsdp_index * count, count, 0)

    g_b_proj = own_bias(0, shard_rows)
    g_b_fc1 = own_bias(model_width, 4 * shard_rows)
    g_b_fc2 = own_bias(5 * model_width, shard_rows)
    long_dq, long_dk, long_dv = attend_back(
        long_queries, long_keys, long_values, long_log, split_heads(d_heads[short_rows:], 1), scaling
    )
    dk = long_dk.reshape(SPLIT, quarter_rows, model_width)
    dv = long_dv.reshape(SPLIT, quarter_rows, model_width)
    dk_near = dk[:2] + swap(low(dk[2:]), "fsdp", 2)
    own_dk = dk_near[0] + swap(low(dk_near[1]), "fsdp", 1)
    dv_sent = swap(low(jnp.stack([dv[1], dv[3]])), "fsdp", 1)
    dv_near = jnp.stack([dv[0], dv[2]]) + dv_sent
    own_dv = dv_near[0] + swap(low(dv_near[1]), "fsdp", 2)
    short_dq, short_dk, short_dv = attend_back(
        short_q, short_k, short_v, short_log, split_heads(d_heads[:short_rows], short_count), scaling
    )

    def join(short_rows_part, long_rows_part):
        return low(
            jnp.concatenate(
                [
                    short_rows_part.reshape(short_rows, model_width),
                    long_rows_part.reshape(quarter_rows, model_width),
                ],
                0,
            )
        )

    dq_rows, dk_rows, dv_rows = join(short_dq, long_dq), join(short_dk, own_dk), join(short_dv, own_dv)
    right_stack = jnp.stack([dq_rows, dk_rows, dv_rows, d_projected])
    left_stack = jnp.stack([hidden1, attention])
    attention_terms = []
    for step in range(4):
        which = role ^ step
        right = lax.dynamic_index_in_dim(right_stack, which, 0, keepdims=False)
        left = lax.dynamic_index_in_dim(left_stack, which // 3, 0, keepdims=False)
        attention_terms.append(role_term(left, right))
    attention_block = jnp.concatenate(
        [
            scatter_blocks([term[..., :first_columns] for term in attention_terms], True),
            scatter_blocks([term[..., first_columns:] for term in attention_terms], False),
        ],
        1,
    )
    attention_grad = share_roles(attention_block)
    g_w_qkv = attention_grad[:3].transpose(1, 0, 2).reshape(shard_rows, -1)
    g_w_proj = attention_grad[3]
    d_hidden1 = (
        product_nt(dq_rows, attention_full[0])
        + product_nt(dk_rows, attention_full[1])
        + product_nt(dv_rows, attention_full[2])
    )
    slot_shift1 = slot_sum(d_hidden1, short_count, len_short)
    slot_scale1 = slot_sum(d_hidden1 * normed1, short_count, len_short)
    d_rows = d_mixed + norm_back(d_hidden1 * (1.0 + scale1), normed1, inverse1)
    dx_short = low(d_rows[:short_rows].reshape(x_short.shape))
    dx_long = low(d_rows[short_rows:])
    d_head_logit = d_head * head_mask * 2.0 * head_sigmoid * (1.0 - head_sigmoid)
    d_group_logit = d_group * group_mask * 2.0 * group_sigmoid * (1.0 - group_sigmoid)
    d_conditioned = jnp.concatenate(
        [
            slot_shift1,
            slot_scale1,
            slot_gate1,
            slot_shift2,
            slot_scale2,
            slot_gate2,
            d_head_logit,
            d_group_logit,
        ],
        1,
    )
    long_sum = d_conditioned[short_count:]
    for mask in (1, 2):
        long_sum = long_sum + swap(long_sum, "fsdp", mask)
    own_rows = low(jnp.concatenate([d_conditioned[:short_count], long_sum], 0))[None]
    member_rows = gather_small(own_rows, "fsdp")
    ordered = jnp.take(member_rows, members, axis=0)
    d_items = jnp.concatenate([ordered[:, 0], ordered[::SPLIT, 1]], 0)
    d_silu = (
        product_nt(d_items[:, :mod_width], w_ada)
        + product_nt(d_items[:, mod_width : mod_width + head_count], w_head_router)
        + product_nt(d_items[:, mod_width + head_count :], w_group_router)
    )
    d_silu = jnp.take(gather_small(d_silu[None], "fsdp"), members, axis=0)
    d_silu = d_silu.transpose(1, 0, 2).reshape(-1, model_width)
    d_short_cond = lax.dynamic_slice_in_dim(d_silu, fsdp_index, 1, 0) * silu_grad(short_cond)
    d_long_cond = d_silu[fsdp_count:] * silu_grad(long_cond)
    replicas = jnp.arange(lax.axis_size("dp")) ^ role
    factors = jnp.take(gather_small(d_items[None], "dp"), replicas, axis=0)
    factors = factors.reshape(-1, factors.shape[2])
    ordered_act = jnp.concatenate([jnp.take(act_rows, members, axis=0), long_act], 0)
    act_factors = jnp.take(gather_small(own_columns(ordered_act)[None], "dp"), replicas, axis=0)
    act_factors = act_factors.reshape(-1, shard_rows)
    g_w_ada = product_tn(act_factors, factors[:, :mod_width])
    g_w_head_router = product_tn(act_factors, factors[:, mod_width : mod_width + head_count])
    g_w_group_router = product_tn(act_factors, factors[:, mod_width + head_count :])
    g_b_ada = lax.dynamic_slice_in_dim(
        jnp.sum(factors[:, :mod_width].astype(jnp.float32), axis=0),
        fsdp_index * b_ada.shape[0],
        b_ada.shape[0],
        0,
    )
    return (
        y_short,
        y_long,
        dx_short,
        dx_long,
        d_short_cond,
        d_long_cond,
        g_w_ada,
        g_b_ada,
        g_w_head_router,
        g_w_group_router,
        g_w_qkv,
        g_w_proj,
        g_b_proj,
        g_w_fc1,
        g_b_fc1,
        g_w_fc2,
        g_b_fc2,
    )


def solution(mesh):
    return jax.shard_map(
        per_device,
        mesh=mesh,
        in_specs=(
            P(("dp", "fsdp"), None, None),
            P(("dp", "fsdp"), None),
            P(("dp", "fsdp"), None),
            P("dp", None),
            P(("dp", "fsdp"), None),
            P("dp", None),
            P(("dp", "fsdp"), None),
            P("dp", None),
            P(("dp", "fsdp"), None),
            P(("dp", "fsdp")),
            P("fsdp", None),
            P("fsdp"),
            P("fsdp", None),
            P("fsdp", None),
            P("fsdp", None),
            P("fsdp", None),
            P("fsdp"),
            P("fsdp", None),
            P("fsdp"),
            P("fsdp", None),
            P("fsdp"),
            P(("dp", "fsdp"), None, None),
            P(("dp", "fsdp"), None),
        ),
        out_specs=(
            P(("dp", "fsdp"), None, None),
            P(("dp", "fsdp"), None),
            P(("dp", "fsdp"), None, None),
            P(("dp", "fsdp"), None),
            P(("dp", "fsdp"), None),
            P("dp", None),
            P("fsdp", None),
            P("fsdp"),
            P("fsdp", None),
            P("fsdp", None),
            P("fsdp", None),
            P("fsdp", None),
            P("fsdp"),
            P("fsdp", None),
            P("fsdp"),
            P("fsdp", None),
            P("fsdp"),
        ),
        check_vma=False,
    )
```

```python
import functools
import math

import jax
import jax.numpy as jnp
from jax import lax
from jax.experimental import pallas as pl
from jax.experimental.pallas import tpu as pltpu
from jax.sharding import PartitionSpec as P

CHAN = 128
SPLIT = 4


epsilon = 1e-06


def swap(value, axis, mask):
    pairs = [(source, source ^ mask) for source in range(lax.axis_size(axis))]
    return lax.ppermute(value, axis, pairs)


def low(value):
    return value.astype(jnp.bfloat16)


def packed(parts, unit):
    flat = jnp.concatenate([part.reshape(-1) for part in parts])
    return jnp.pad(flat, (0, -flat.size % (unit * 128))).reshape(-1, 128)


def unpacked(rows, shapes):
    lead = rows.shape[:-2]
    flat = rows.reshape(lead + (-1,))
    parts, start = [], 0
    for shape in shapes:
        size = math.prod(shape)
        parts.append(flat[..., start : start + size].reshape(lead + shape))
        start += size
    return parts


MESH_IDS = pl.DeviceIdType.MESH
VMEM_BYTES = 60 * 1024 * 1024


def flipped(value, step, size):
    total, bit = 0, 1
    while bit < size:
        digit = (value // bit) % 2
        total = total + bit * ((digit + 1) % 2 if step & bit else digit)
        bit *= 2
    return total


def greet(peers):
    barrier = pltpu.get_barrier_semaphore()
    for peer in peers:
        pl.semaphore_signal(barrier, inc=1, device_id=peer, device_id_type=MESH_IDS)
    pl.semaphore_wait(barrier, len(peers))


def remote(source, target, send_sem, recv_sem, peer):
    return pltpu.make_async_remote_copy(
        src_ref=source,
        dst_ref=target,
        send_sem=send_sem,
        recv_sem=recv_sem,
        device_id=peer,
        device_id_type=MESH_IDS,
    )


def exchange_kernel(axis, size, spread_out, rows_ref, out_ref, send_sem, recv_sem):
    me = lax.axis_index(axis)
    greet([{axis: (me + step) % size} for step in range(1, size)])

    def piece(target):
        return rows_ref.at[target] if spread_out else rows_ref

    sent = []
    for step in range(1, size):
        peer = (me + step) % size
        copy = remote(
            piece(peer), out_ref.at[me], send_sem.at[step], recv_sem.at[size - step], {axis: peer}
        )
        copy.start()
        sent.append(copy)
    out_ref[me] = rows_ref[me] if spread_out else rows_ref[...]
    for step in range(1, size):
        peer = (me + step) % size
        remote(
            piece(peer), out_ref.at[peer], send_sem.at[step], recv_sem.at[step], {axis: peer}
        ).wait_recv()
    for copy in sent:
        copy.wait_send()


def exchange(rows, axis, spread_out, number):
    size = lax.axis_size(axis)
    block = rows.shape[1:] if spread_out else rows.shape
    return pl.pallas_call(
        functools.partial(exchange_kernel, axis, size, spread_out),
        out_shape=jax.ShapeDtypeStruct((size,) + block, rows.dtype),
        in_specs=[pl.BlockSpec(memory_space=pltpu.VMEM)],
        out_specs=pl.BlockSpec(memory_space=pltpu.VMEM),
        scratch_shapes=[pltpu.SemaphoreType.DMA((size,)), pltpu.SemaphoreType.DMA((size,))],
        compiler_params=pltpu.CompilerParams(
            collective_id=number, has_side_effects=True, vmem_limit_bytes=VMEM_BYTES
        ),
        name=f"exchange{number}",
    )(rows)


class Place:
    def __init__(self, half):
        self.half = half
        self.role = lax.axis_index("dp")
        shard = lax.axis_index("fsdp")
        self.line, self.side = shard // 2, shard % 2
        self.other_side = (self.side + 1) % 2
        self.roles = [flipped(self.role, step, 4) for step in range(4)]
        self.lines = [flipped(self.line, step, half) for step in range(half)]
        self.sides = [self.side, self.other_side]
        self.across = {"dp": self.roles[2]}
        self.beside = {"fsdp": self.line * 2 + self.other_side}
        self.core = {"dp": self.roles[1]}
        self.along = [{"fsdp": line * 2 + self.side} for line in self.lines]

    def greet(self, also=()):
        greet([self.across, self.beside, self.core] + self.along[1:] + list(also))


def cut(rows):
    first = (rows // 2 + 15) // 16 * 16
    return [(0, first), (first, rows - first)]


class GatherUnit:
    def __init__(self, at, piece, out, by_shard, start, count, side_first, send_sem, recv_sem):
        self.at, self.piece, self.out, self.by_shard = at, piece, out, by_shard
        self.rows = pl.ds(start, count)
        self.side_first, self.send_sem, self.recv_sem = side_first, send_sem, recv_sem
        self.sent = []

    def view(self, role, line, side):
        if self.by_shard:
            return self.out.at[line, side, role, self.rows]
        return self.out.at[role, line, side, self.rows]

    def send(self, number, source, target, peer):
        copy = remote(source, target, self.send_sem.at[number], self.recv_sem.at[number], peer)
        copy.start()
        self.sent.append(copy)

    def got(self, number, target):
        remote(
            target, target, self.send_sem.at[number], self.recv_sem.at[number], self.at.core
        ).wait_recv()

    def numbers(self):
        half = self.at.half
        return half, 2 * half, 3 * half, 3 * half + 1

    def begin(self):
        at = self.at
        own = self.piece.at[self.rows]
        target = self.view(at.role, at.line, at.side)
        for step in range(1, at.half):
            self.send(step, own, target, at.along[step])
        self.fan(0, own, target)

    def fan(self, step, source, target):
        beside, across, _, _ = self.numbers()
        self.send(beside + step, source, target, self.at.beside)
        self.send(across + step, source, target, self.at.across)

    def line_step(self, step):
        at = self.at
        view = self.view(at.role, at.lines[step], at.side)
        self.got(step, view)
        self.fan(step, view, view)

    def second(self):
        at, every = self.at, slice(None)
        beside, across, second, core = self.numbers()
        for step in range(at.half):
            if self.side_first:
                self.got(beside + step, self.view(at.role, at.lines[step], at.other_side))
            else:
                self.got(across + step, self.view(at.roles[2], at.lines[step], at.side))
        own = self.view(at.role, every, at.side)
        if self.side_first:
            view = self.view(at.role, every, at.other_side)
            self.send(second, view, view, at.across)
        else:
            view = self.view(at.roles[2], every, at.side)
            self.send(second, view, view, at.beside)
        self.send(core, own, own, at.core)
        self.send(core + 1, view, view, at.core)

    def third(self):
        at, every = self.at, slice(None)
        beside, across, second, core = self.numbers()
        for step in range(at.half):
            if self.side_first:
                self.got(across + step, self.view(at.roles[2], at.lines[step], at.side))
            else:
                self.got(beside + step, self.view(at.role, at.lines[step], at.other_side))
        if self.side_first:
            view = self.view(at.roles[2], every, at.side)
        else:
            view = self.view(at.role, every, at.other_side)
        self.send(core + 2, view, view, at.core)
        last = self.view(at.roles[2], every, at.other_side)
        self.got(second, last)
        self.send(core + 3, last, last, at.core)

    def finish(self):
        at, every = self.at, slice(None)
        core = self.numbers()[3]
        near, far = at.roles[1], at.roles[3]
        views = [
            self.view(near, every, at.side),
            self.view(near, every, at.other_side),
            self.view(far, every, at.side),
            self.view(far, every, at.other_side),
        ]
        if not self.side_first:
            views[1], views[2] = views[2], views[1]
        for step, view in enumerate(views):
            self.got(core + step, view)
        for copy in self.sent:
            copy.wait_send()


def gather_kernel(half, by_shard, *refs):
    count = len(by_shard)
    pieces, outs = refs[:count], refs[count : 2 * count]
    send_sem, recv_sem, local_sem = refs[2 * count :]
    at = Place(half)
    at.greet()
    pairs, local = [], []
    for matrix in range(count):
        rows = pieces[matrix].shape[0]
        pairs.append(
            [
                GatherUnit(
                    at,
                    pieces[matrix],
                    outs[matrix],
                    by_shard[matrix],
                    start,
                    size,
                    part == 0,
                    send_sem.at[2 * matrix + part],
                    recv_sem.at[2 * matrix + part],
                )
                for part, (start, size) in enumerate(cut(rows))
            ]
        )
        target = outs[matrix]
        if by_shard[matrix]:
            target = target.at[at.line, at.side, at.role]
        else:
            target = target.at[at.role, at.line, at.side]
        copy = pltpu.make_async_copy(pieces[matrix], target, local_sem.at[matrix])
        copy.start()
        local.append(copy)
    for unit in pairs[0]:
        unit.begin()
    for copy in local:
        copy.wait()
    for matrix in range(count + 1):
        if matrix < count:
            for step in range(1, half):
                for unit in pairs[matrix]:
                    unit.line_step(step)
            if matrix + 1 < count:
                for unit in pairs[matrix + 1]:
                    unit.begin()
            for unit in pairs[matrix]:
                unit.second()
        if matrix:
            for unit in pairs[matrix - 1]:
                unit.third()
    for pair in pairs:
        for unit in pair:
            unit.finish()


def gather(pieces, by_shard, number):
    half = lax.axis_size("fsdp") // 2
    count = len(pieces)
    units = 2 * count
    any_space = pl.BlockSpec(memory_space=pl.ANY)
    shapes = []
    for piece, rows_first in zip(pieces, by_shard):
        lead = (half, 2, 4) if rows_first else (4, half, 2)
        shapes.append(jax.ShapeDtypeStruct(lead + piece.shape, piece.dtype))
    return pl.pallas_call(
        functools.partial(gather_kernel, half, by_shard),
        out_shape=shapes,
        in_specs=[pl.BlockSpec(memory_space=pltpu.VMEM)] * count,
        out_specs=[any_space] * count,
        scratch_shapes=[
            pltpu.SemaphoreType.DMA((units, 3 * half + 5)),
            pltpu.SemaphoreType.DMA((units, 3 * half + 5)),
            pltpu.SemaphoreType.DMA((count,)),
        ],
        compiler_params=pltpu.CompilerParams(
            collective_id=number, has_side_effects=True, vmem_limit_bytes=VMEM_BYTES
        ),
        name=f"gather{number}",
    )(*pieces)


def accumulate(target, source):
    rows = target.shape[0]
    chunk = 16 if rows % 16 == 0 else rows

    def step(index, carry):
        place_of = pl.ds(pl.multiple_of(index * chunk, chunk), chunk)
        total = target[place_of].astype(jnp.float32) + source[place_of].astype(jnp.float32)
        target[place_of] = total.astype(target.dtype)
        return carry

    lax.fori_loop(0, rows // chunk, step, 0)


class ScatterUnit:
    def __init__(self, at, terms, out, start, count, across_first, send_sem, recv_sem, buffers):
        self.at, self.terms, self.out = at, terms, out
        self.rows = pl.ds(start, count)
        self.across_first, self.send_sem, self.recv_sem = across_first, send_sem, recv_sem
        self.core_buf, self.first_buf, self.last_buf, self.line_buf = buffers
        self.sent = []
        half = at.half
        self.base_first, self.base_last = 4, 6
        self.base_line, self.base_share = 6 + half, 6 + 2 * half
        self.first_peer = at.across if across_first else at.beside
        self.last_peer = at.beside if across_first else at.across

    def own_terms(self, first, last, core):
        role_step, side_step = (first, last) if self.across_first else (last, first)
        role = self.at.roles[2 * role_step + core]
        return self.terms.at[role, :, self.at.sides[side_step], self.rows]

    def send(self, number, source, target, peer):
        copy = remote(source, target, self.send_sem.at[number], self.recv_sem.at[number], peer)
        copy.start()
        self.sent.append(copy)

    def got(self, number, target):
        remote(
            target, target, self.send_sem.at[number], self.recv_sem.at[number], self.at.core
        ).wait_recv()

    def add_lines(self, target, source):
        def step(line, carry):
            accumulate(target.at[line], source.at[line])
            return carry

        lax.fori_loop(0, self.at.half, step, 0)

    def begin(self):
        for first in (1, 0):
            for last in (1, 0):
                self.send(
                    2 * first + last,
                    self.own_terms(first, last, 1),
                    self.core_buf.at[first, last],
                    self.at.core,
                )

    def paired(self, first, last):
        buffer = self.core_buf.at[first, last]
        self.got(2 * first + last, buffer)
        self.add_lines(buffer, self.own_terms(first, last, 0))
        if first:
            self.send(self.base_first + last, buffer, self.first_buf.at[last], self.first_peer)

    def joined(self, last):
        buffer = self.first_buf.at[last]
        self.got(self.base_first + last, buffer)
        self.add_lines(buffer, self.core_buf.at[0, last])
        if last:
            for step in list(range(self.at.half - 1, 0, -1)) + [0]:
                line = self.at.lines[step]
                self.send(
                    self.base_last + step, buffer.at[line], self.last_buf.at[line], self.last_peer
                )

    def lined(self, step):
        line = self.at.lines[step]
        block = self.last_buf.at[line]
        self.got(self.base_last + step, block)
        accumulate(block, self.first_buf.at[0, line])
        if step:
            self.send(self.base_line + step, block, self.line_buf.at[step], self.at.along[step])

    def end(self):
        at = self.at
        own = self.last_buf.at[at.line]
        for step in range(1, at.half):
            self.got(self.base_line + step, self.line_buf.at[step])
            accumulate(own, self.line_buf.at[step])
        self.out[at.role, self.rows] = own[...]
        target = self.out.at[at.role, self.rows]
        for step in (1, 2, 3):
            self.send(self.base_share + step, own, target, {"dp": at.roles[step]})

    def finish(self):
        for step in (1, 2, 3):
            self.got(self.base_share + step, self.out.at[self.at.roles[step], self.rows])
        for copy in self.sent:
            copy.wait_send()


def scatter_program(pairs, begun=False):
    half = pairs[0][0].at.half
    for pair in pairs:
        for unit in pair:
            unit.begin()
    stages = [
        [lambda unit: unit.paired(1, 1), lambda unit: unit.paired(1, 0)],
        [lambda unit: unit.paired(0, 1), lambda unit: unit.paired(0, 0)],
        [lambda unit: unit.joined(1), lambda unit: unit.joined(0)],
        [lambda unit, step=step: unit.lined(step) for step in list(range(half - 1, 0, -1)) + [0]],
        [lambda unit: unit.end()],
    ]
    for turn in range(len(stages) + len(pairs) - 1):
        for index, pair in reversed(list(enumerate(pairs))):
            if 0 <= turn - index < len(stages):
                for action in stages[turn - index]:
                    for unit in pair:
                        action(unit)
    for pair in pairs:
        for unit in pair:
            unit.finish()


def scatter_buffers(half, rows, columns):
    shapes = []
    for _, size in cut(rows):
        for lead in ((2, 2, half), (2, half), (half,), (half,)):
            shapes.append(pltpu.VMEM(lead + (size, columns), jnp.bfloat16))
    return shapes


def scatter_kernel(half, layout, *refs):
    inputs = sum(layout)
    ins, outs = refs[:inputs], refs[inputs : inputs + len(layout)]
    rest = refs[inputs + len(layout) :]
    terms, rest = rest[: len(layout)], rest[len(layout) :]
    send_sem, recv_sem, local_sem, buffers = rest[0], rest[1], rest[2], rest[3:]
    at = Place(half)
    local, taken = [], 0
    for matrix, many in enumerate(layout):
        for role in range(4):
            source = ins[taken + role] if many == 4 else ins[taken].at[:, :, role]
            copy = pltpu.make_async_copy(
                source, terms[matrix].at[role], local_sem.at[4 * matrix + role]
            )
            copy.start()
            local.append(copy)
        taken += many
    at.greet([{"dp": at.roles[3]}])
    for copy in local:
        copy.wait()
    pairs = []
    for matrix in range(len(layout)):
        pairs.append(
            [
                ScatterUnit(
                    at,
                    terms[matrix],
                    outs[matrix],
                    start,
                    size,
                    part == 0,
                    send_sem.at[2 * matrix + part],
                    recv_sem.at[2 * matrix + part],
                    buffers[4 * (2 * matrix + part) : 4 * (2 * matrix + part) + 4],
                )
                for part, (start, size) in enumerate(cut(terms[matrix].shape[3]))
            ]
        )
    scatter_program(pairs)


def scatter(gradients, number):
    half = lax.axis_size("fsdp") // 2
    layout = tuple(len(gradient) for gradient in gradients)
    flat = [block for gradient in gradients for block in gradient]
    rows, columns = flat[0].shape[-2:]
    count = len(layout)
    scratch = [pltpu.VMEM((4, half, 2, rows, columns), jnp.bfloat16)] * count
    scratch += [pltpu.SemaphoreType.DMA((2 * count, 2 * half + 10))] * 2
    scratch += [pltpu.SemaphoreType.DMA((4 * count,))]
    for _ in range(count):
        scratch += scatter_buffers(half, rows, columns)
    return pl.pallas_call(
        functools.partial(scatter_kernel, half, layout),
        out_shape=[jax.ShapeDtypeStruct((4, rows, columns), jnp.bfloat16)] * count,
        in_specs=[pl.BlockSpec(memory_space=pl.ANY)] * len(flat),
        out_specs=[pl.BlockSpec(memory_space=pltpu.VMEM)] * count,
        scratch_shapes=scratch,
        compiler_params=pltpu.CompilerParams(
            collective_id=number, has_side_effects=True, vmem_limit_bytes=VMEM_BYTES
        ),
        name=f"scatter{number}",
    )(*flat)


def product(left, right):
    return jnp.dot(left, right, preferred_element_type=jnp.float32)


def product_tn(left, right):
    return lax.dot_general(
        left, right, (((0,), (0,)), ((), ())), preferred_element_type=jnp.float32
    )


def product_nt(left, right):
    return lax.dot_general(
        left, right, (((1,), (1,)), ((), ())), preferred_element_type=jnp.float32
    )


def spread(per_slot, short_count, len_short, quarter_rows):
    width = per_slot.shape[1]
    short_part = jnp.broadcast_to(
        per_slot[:short_count, None, :], (short_count, len_short, width)
    ).reshape(short_count * len_short, width)
    long_part = jnp.broadcast_to(per_slot[short_count:], (quarter_rows, width))
    return jnp.concatenate([short_part, long_part], 0)


def slot_sum(values, short_count, len_short):
    short_rows = short_count * len_short
    short_part = jnp.sum(
        values[:short_rows].reshape((short_count, len_short) + values.shape[1:]), axis=1
    )
    long_part = jnp.sum(values[short_rows:], axis=0, keepdims=True)
    return jnp.concatenate([short_part, long_part], 0)


def norm_parts(values):
    average = jnp.mean(values, axis=-1, keepdims=True)
    centred = values - average
    variance = jnp.mean(centred * centred, axis=-1, keepdims=True)
    inverse = lax.rsqrt(variance + epsilon)
    return (centred * inverse, inverse)


def norm_back(gradient, normed, inverse):
    return inverse * (
        gradient
        - jnp.mean(gradient, axis=-1, keepdims=True)
        - normed * jnp.mean(gradient * normed, axis=-1, keepdims=True)
    )


def silu_grad(values):
    sigmoid_value = jax.nn.sigmoid(values)
    return sigmoid_value * (1.0 + values * (1.0 - sigmoid_value))


def attend(queries, key_rows, value_rows, scaling):
    scores = (
        jnp.einsum("nqhe,nkhe->nhqk", queries, key_rows, preferred_element_type=jnp.float32)
        * scaling
    )
    row_max = jnp.max(scores, axis=-1, keepdims=True)
    exponent = jnp.exp(scores - row_max)
    row_total = jnp.sum(exponent, axis=-1, keepdims=True)
    soft_weights = exponent / row_total
    head_out = jnp.einsum(
        "nhqk,nkhe->nqhe",
        soft_weights.astype(jnp.bfloat16),
        value_rows,
        preferred_element_type=jnp.float32,
    )
    return (head_out, row_max + jnp.log(row_total))


def attend_back(queries, key_rows, value_rows, log_total, d_out, scaling):
    scores = (
        jnp.einsum("nqhe,nkhe->nhqk", queries, key_rows, preferred_element_type=jnp.float32)
        * scaling
    )
    soft_weights = jnp.exp(scores - log_total)
    d_weights = jnp.einsum("nqhe,nkhe->nhqk", d_out, value_rows, preferred_element_type=jnp.float32)
    inner = jnp.sum(soft_weights * d_weights, axis=-1, keepdims=True)
    d_scores = (soft_weights * (d_weights - inner)).astype(jnp.bfloat16)
    d_queries = (
        jnp.einsum("nhqk,nkhe->nqhe", d_scores, key_rows, preferred_element_type=jnp.float32)
        * scaling
    )
    d_keys = (
        jnp.einsum("nhqk,nqhe->nkhe", d_scores, queries, preferred_element_type=jnp.float32)
        * scaling
    )
    d_values = jnp.einsum(
        "nhqk,nqhe->nkhe",
        soft_weights.astype(jnp.bfloat16),
        d_out,
        preferred_element_type=jnp.float32,
    )
    return (d_queries, d_keys, d_values)


def gelu_tanh(values):
    return jax.nn.gelu(values, approximate=True)


def per_device(
    x_short,
    x_long,
    short_cond,
    long_cond,
    short_heads,
    long_heads,
    short_groups,
    long_groups,
    short_keep,
    long_keep,
    w_ada,
    b_ada,
    w_head_router,
    w_group_router,
    w_qkv,
    w_proj,
    b_proj,
    w_fc1,
    b_fc1,
    w_fc2,
    b_fc2,
    g_short,
    g_long,
):
    short_count, len_short, model_width = x_short.shape
    quarter_rows = x_long.shape[0]
    head_count = w_head_router.shape[1]
    head_width = model_width // head_count
    group_count = w_group_router.shape[1]
    slot_count = short_count + 1
    short_rows = short_count * len_short
    row_count = short_rows + quarter_rows
    scaling = head_width ** (-0.5)
    fsdp_index = lax.axis_index("fsdp")
    fsdp_count = lax.axis_size("fsdp")
    role = lax.axis_index("dp")
    group_row = fsdp_index // SPLIT
    half = fsdp_count // 2
    shard_rows = w_qkv.shape[0]
    unit_rows = w_fc2.shape[0] // 4
    short_act = low(jax.nn.silu(short_cond))
    long_act = low(jax.nn.silu(long_cond))
    message = exchange(packed([short_act, b_proj, b_fc1, b_fc2], 16), "fsdp", False, 0)
    act_rows, proj_bias, fc1_bias, fc2_bias = unpacked(
        message, [(model_width,), b_proj.shape, b_fc1.shape, b_fc2.shape]
    )
    proj_bias, fc1_bias, fc2_bias = (
        bias.reshape(-1).astype(jnp.float32) for bias in (proj_bias, fc1_bias, fc2_bias)
    )
    item_act = jnp.concatenate([act_rows, long_act], 0)
    item_columns = lax.dynamic_slice_in_dim(item_act, fsdp_index * shard_rows, shard_rows, 1)
    bias_row = lax.dynamic_update_slice_in_dim(
        jnp.zeros((fsdp_count * b_ada.shape[0],), jnp.float32),
        b_ada.astype(jnp.float32),
        fsdp_index * b_ada.shape[0],
        0,
    )
    partial = jnp.concatenate(
        [
            product(item_columns, w_ada) + bias_row,
            product(item_columns, w_head_router),
            product(item_columns, w_group_router),
        ],
        1,
    )
    width = partial.shape[1]
    for_device = jnp.stack(
        [partial[:fsdp_count], jnp.repeat(partial[fsdp_count:], SPLIT, axis=0)], 1
    ).reshape(fsdp_count, -1)
    for_device = jnp.pad(for_device, ((0, 0), (0, -for_device.shape[1] % 1024)))
    shares = exchange(for_device.reshape(fsdp_count, -1, 128), "fsdp", True, 1)
    conditioned = unpacked(jnp.sum(shares, axis=0), [(2, width)])[0]
    mixed_shard = jnp.concatenate([w_qkv, w_proj], 1)
    attention_piece = lax.dynamic_slice_in_dim(mixed_shard, role * model_width, model_width, 1)
    (attention_full,) = gather([attention_piece], (False,), 2)
    attention_full = attention_full.reshape(4, -1, model_width)
    mod_width = 6 * model_width
    modulation = conditioned[:, :mod_width]
    head_sigmoid = jax.nn.sigmoid(conditioned[:, mod_width : mod_width + head_count])
    group_sigmoid = jax.nn.sigmoid(conditioned[:, mod_width + head_count :])
    head_mask = jnp.concatenate(
        [short_heads, lax.dynamic_slice_in_dim(long_heads, group_row, 1, 0)], 0
    ).astype(jnp.float32)
    group_mask = jnp.concatenate(
        [short_groups, lax.dynamic_slice_in_dim(long_groups, group_row, 1, 0)], 0
    ).astype(jnp.float32)
    head_gate = head_mask * 2.0 * head_sigmoid
    group_gate = group_mask * 2.0 * group_sigmoid
    shift1, scale1, gate1, shift2, scale2, gate2 = jnp.split(
        spread(modulation, short_count, len_short, quarter_rows), 6, axis=1
    )
    x_rows = jnp.concatenate([x_short.reshape(short_rows, model_width), x_long], 0).astype(
        jnp.float32
    )
    keep_rows = jnp.concatenate([short_keep.reshape(short_rows), long_keep], 0).astype(jnp.float32)[
        :, None
    ]
    normed1, inverse1 = norm_parts(x_rows)
    hidden1 = low(normed1 * (1.0 + scale1) + shift1)
    q_rows, k_rows, v_rows = (low(product(hidden1, attention_full[part])) for part in range(3))

    fc1_piece = lax.dynamic_slice_in_dim(w_fc1, role * model_width, model_width, 1)
    fc2_piece = lax.dynamic_slice_in_dim(w_fc2, role * unit_rows, unit_rows, 0)
    q_rows, k_rows, v_rows, fc1_piece, fc2_piece = lax.optimization_barrier(
        (q_rows, k_rows, v_rows, fc1_piece, fc2_piece)
    )
    fc1_full, fc2_full = gather([fc1_piece, fc2_piece], (False, True), 3)

    def split_heads(rows, count):
        return rows.reshape(count, -1, head_count, head_width)

    own_k, own_v = k_rows[short_rows:], v_rows[short_rows:]
    k_y = swap(own_k, "fsdp", 1)
    v_z = swap(own_v, "fsdp", 2)
    k_far = swap(jnp.concatenate([own_k, k_y], 0), "fsdp", 2)
    v_far = swap(jnp.concatenate([own_v, v_z], 0), "fsdp", 1)
    long_keys = split_heads(jnp.concatenate([own_k, k_y, k_far], 0), 1)
    long_values = split_heads(
        jnp.concatenate([own_v, v_far[:quarter_rows], v_z, v_far[quarter_rows:]], 0), 1
    )
    short_q, short_k, short_v = (
        split_heads(rows[:short_rows], short_count) for rows in (q_rows, k_rows, v_rows)
    )
    short_out, short_log = attend(short_q, short_k, short_v, scaling)
    long_queries = split_heads(q_rows[short_rows:], 1)
    long_out, long_log = attend(long_queries, long_keys, long_values, scaling)
    head_rows = jnp.concatenate(
        [
            short_out.reshape(short_rows, head_count, head_width),
            long_out.reshape(quarter_rows, head_count, head_width),
        ],
        0,
    )
    head_gate_rows = spread(head_gate, short_count, len_short, quarter_rows)[:, :, None]
    attention = low((head_rows * head_gate_rows).reshape(row_count, model_width))
    projected = product(attention, attention_full[3]) + proj_bias
    mixed = x_rows + gate1 * projected
    fc1_full = fc1_full.reshape(4, -1, model_width)
    fc2_full = fc2_full.reshape(4, -1, model_width)
    normed2, inverse2 = norm_parts(mixed)
    hidden2 = low(normed2 * (1.0 + scale2) + shift2)
    channel_gate = spread(
        jnp.repeat(group_gate, CHAN, axis=1), short_count, len_short, quarter_rows
    )
    gates = jnp.split(channel_gate, 4, axis=1)
    gelus, pulls, activated = [], [], []
    down_rows = fc2_bias
    for part in range(4):
        up_rows = product(hidden2, fc1_full[part]) + fc1_bias.reshape(4, -1)[part]
        gelu_value, gelu_pull = jax.vjp(gelu_tanh, up_rows)
        gelus.append(gelu_value)
        pulls.append(gelu_pull)
        activated.append(low(gelu_value * gates[part]))
        down_rows = down_rows + product(activated[part], fc2_full[part])
    out_rows = mixed + gate2 * keep_rows * down_rows
    y_short = low(out_rows[:short_rows].reshape(x_short.shape))
    y_long = low(out_rows[short_rows:])
    gradient = jnp.concatenate([g_short.reshape(short_rows, model_width), g_long], 0).astype(
        jnp.float32
    )
    d_down = low(gradient * gate2 * keep_rows)
    slot_gate2 = slot_sum(gradient * keep_rows * down_rows, short_count, len_short)
    grad_fc2 = jnp.concatenate([low(product_tn(part, d_down)) for part in activated], 0)
    grad_fc2 = grad_fc2.reshape(half, 2, 4, unit_rows, model_width)
    d_ups, d_groups = [], []
    d_hidden2 = 0.0
    for part in range(4):
        d_activated = product_nt(d_down, fc2_full[part])
        d_channel = slot_sum(d_activated * gelus[part], short_count, len_short)
        d_groups.append(jnp.sum(d_channel.reshape(slot_count, -1, CHAN), axis=-1))
        d_ups.append(low(pulls[part](d_activated * gates[part])[0]))
        d_hidden2 = d_hidden2 + product_nt(d_ups[part], fc1_full[part])
    d_group = jnp.concatenate(d_groups, 1)

    def blocks(grad):
        return low(grad).reshape(half, 2, shard_rows, model_width)

    fc1_sum, fc2_sum = scatter(
        [[blocks(product_tn(hidden2, d_up)) for d_up in d_ups], [grad_fc2]], 4
    )
    g_w_fc1 = fc1_sum.transpose(1, 0, 2).reshape(shard_rows, -1).astype(jnp.float32)
    g_w_fc2 = fc2_sum.reshape(-1, model_width).astype(jnp.float32)
    slot_shift2 = slot_sum(d_hidden2, short_count, len_short)
    slot_scale2 = slot_sum(d_hidden2 * normed2, short_count, len_short)
    d_mixed = gradient + norm_back(d_hidden2 * (1.0 + scale2), normed2, inverse2)
    d_projected = low(d_mixed * gate1)
    slot_gate1 = slot_sum(d_mixed * projected, short_count, len_short)
    d_attention = product_nt(d_projected, attention_full[3]).reshape(
        row_count, head_count, head_width
    )
    d_head = slot_sum(jnp.sum(d_attention * head_rows, axis=-1), short_count, len_short)
    d_heads = low(d_attention * head_gate_rows)
    bias_grad = jnp.concatenate(
        [jnp.sum(d_projected, axis=0, dtype=jnp.float32)]
        + [jnp.sum(d_up, axis=0, dtype=jnp.float32) for d_up in d_ups]
        + [jnp.sum(d_down, axis=0, dtype=jnp.float32)]
    )
    long_dq, long_dk, long_dv = attend_back(
        long_queries, long_keys, long_values, long_log, split_heads(d_heads[short_rows:], 1), scaling
    )
    dk = long_dk.reshape(SPLIT, quarter_rows, model_width)
    dv = long_dv.reshape(SPLIT, quarter_rows, model_width)
    dk_near = dk[:2] + swap(low(dk[2:]), "fsdp", 2)
    own_dk = dk_near[0] + swap(low(dk_near[1]), "fsdp", 1)
    dv_sent = swap(low(jnp.stack([dv[1], dv[3]])), "fsdp", 1)
    dv_near = jnp.stack([dv[0], dv[2]]) + dv_sent
    own_dv = dv_near[0] + swap(low(dv_near[1]), "fsdp", 2)
    short_dq, short_dk, short_dv = attend_back(
        short_q, short_k, short_v, short_log, split_heads(d_heads[:short_rows], short_count), scaling
    )

    def join(short_rows_part, long_rows_part):
        return low(
            jnp.concatenate(
                [
                    short_rows_part.reshape(short_rows, model_width),
                    long_rows_part.reshape(quarter_rows, model_width),
                ],
                0,
            )
        )

    dq_rows, dk_rows, dv_rows = join(short_dq, long_dq), join(short_dk, own_dk), join(short_dv, own_dv)
    (attention_sum,) = scatter(
        [
            [
                blocks(product_tn(hidden1, dq_rows)),
                blocks(product_tn(hidden1, dk_rows)),
                blocks(product_tn(hidden1, dv_rows)),
                blocks(product_tn(attention, d_projected)),
            ]
        ],
        5,
    )
    g_w_qkv = attention_sum[:3].transpose(1, 0, 2).reshape(shard_rows, -1).astype(jnp.float32)
    g_w_proj = attention_sum[3].astype(jnp.float32)
    d_hidden1 = (
        product_nt(dq_rows, attention_full[0])
        + product_nt(dk_rows, attention_full[1])
        + product_nt(dv_rows, attention_full[2])
    )
    slot_shift1 = slot_sum(d_hidden1, short_count, len_short)
    slot_scale1 = slot_sum(d_hidden1 * normed1, short_count, len_short)
    d_rows = d_mixed + norm_back(d_hidden1 * (1.0 + scale1), normed1, inverse1)
    dx_short = low(d_rows[:short_rows].reshape(x_short.shape))
    dx_long = low(d_rows[short_rows:])
    d_head_logit = d_head * head_mask * 2.0 * head_sigmoid * (1.0 - head_sigmoid)
    d_group_logit = d_group * group_mask * 2.0 * group_sigmoid * (1.0 - group_sigmoid)
    d_conditioned = jnp.concatenate(
        [
            slot_shift1,
            slot_scale1,
            slot_gate1,
            slot_shift2,
            slot_scale2,
            slot_gate2,
            d_head_logit,
            d_group_logit,
        ],
        1,
    )
    member_rows = exchange(packed([low(d_conditioned), low(bias_grad)], 16), "fsdp", False, 6)
    member_rows, bias_rows = unpacked(member_rows, [(2, width), bias_grad.shape])
    long_sum = jnp.sum(
        member_rows[:, 1].astype(jnp.float32).reshape(-1, SPLIT, width), axis=1
    )
    d_items = jnp.concatenate([member_rows[:, 0], low(long_sum)], 0)
    group_bias = jnp.sum(bias_rows.astype(jnp.float32), axis=0)
    d_silu = (
        product_nt(d_items[:, :mod_width], w_ada)
        + product_nt(d_items[:, mod_width : mod_width + head_count], w_head_router)
        + product_nt(d_items[:, mod_width + head_count :], w_group_router)
    )
    d_silu = unpacked(exchange(packed([d_silu], 8), "fsdp", False, 7), [d_silu.shape])[0]
    d_silu = d_silu.transpose(1, 0, 2).reshape(-1, model_width)
    d_short_cond = lax.dynamic_slice_in_dim(d_silu, fsdp_index, 1, 0) * silu_grad(short_cond)
    d_long_cond = d_silu[fsdp_count:] * silu_grad(long_cond)
    replicas = exchange(packed([d_items, low(group_bias), item_columns], 16), "dp", False, 8)
    factors, bias_rows, act_factors = unpacked(
        replicas, [d_items.shape, group_bias.shape, item_columns.shape]
    )
    factors, act_factors = factors.reshape(-1, width), act_factors.reshape(-1, shard_rows)
    g_w_ada = product_tn(act_factors, factors[:, :mod_width])
    g_w_head_router = product_tn(act_factors, factors[:, mod_width : mod_width + head_count])
    g_w_group_router = product_tn(act_factors, factors[:, mod_width + head_count :])
    g_b_ada = lax.dynamic_slice_in_dim(
        jnp.sum(factors[:, :mod_width].astype(jnp.float32), axis=0),
        fsdp_index * b_ada.shape[0],
        b_ada.shape[0],
        0,
    )
    bias_sum = jnp.sum(bias_rows.astype(jnp.float32), axis=0)

    def own_bias(start, count):
        return lax.dynamic_slice_in_dim(bias_sum, start + fsdp_index * count, count, 0)

    g_b_proj = own_bias(0, shard_rows)
    g_b_fc1 = own_bias(model_width, 4 * shard_rows)
    g_b_fc2 = own_bias(5 * model_width, shard_rows)
    return (
        y_short,
        y_long,
        dx_short,
        dx_long,
        d_short_cond,
        d_long_cond,
        g_w_ada,
        g_b_ada,
        g_w_head_router,
        g_w_group_router,
        g_w_qkv,
        g_w_proj,
        g_b_proj,
        g_w_fc1,
        g_b_fc1,
        g_w_fc2,
        g_b_fc2,
    )


def solution(mesh):
    return jax.shard_map(
        per_device,
        mesh=mesh,
        in_specs=(
            P(("dp", "fsdp"), None, None),
            P(("dp", "fsdp"), None),
            P(("dp", "fsdp"), None),
            P("dp", None),
            P(("dp", "fsdp"), None),
            P("dp", None),
            P(("dp", "fsdp"), None),
            P("dp", None),
            P(("dp", "fsdp"), None),
            P(("dp", "fsdp")),
            P("fsdp", None),
            P("fsdp"),
            P("fsdp", None),
            P("fsdp", None),
            P("fsdp", None),
            P("fsdp", None),
            P("fsdp"),
            P("fsdp", None),
            P("fsdp"),
            P("fsdp", None),
            P("fsdp"),
            P(("dp", "fsdp"), None, None),
            P(("dp", "fsdp"), None),
        ),
        out_specs=(
            P(("dp", "fsdp"), None, None),
            P(("dp", "fsdp"), None),
            P(("dp", "fsdp"), None, None),
            P(("dp", "fsdp"), None),
            P(("dp", "fsdp"), None),
            P("dp", None),
            P("fsdp", None),
            P("fsdp"),
            P("fsdp", None),
            P("fsdp", None),
            P("fsdp", None),
            P("fsdp", None),
            P("fsdp"),
            P("fsdp", None),
            P("fsdp"),
            P("fsdp", None),
            P("fsdp"),
        ),
        check_vma=False,
    )
```

```python
import functools
import math

import jax
import jax.numpy as jnp
from jax import lax
from jax.experimental import pallas as pl
from jax.experimental.pallas import tpu as pltpu
from jax.sharding import PartitionSpec as P

CHAN = 128
SPLIT = 4


epsilon = 1e-06


def low(value):
    return value.astype(jnp.bfloat16)


def packed(parts, unit):
    flat = jnp.concatenate([part.reshape(-1) for part in parts])
    return jnp.pad(flat, (0, -flat.size % (unit * 128))).reshape(-1, 128)


def unpacked(rows, shapes):
    lead = rows.shape[:-2]
    flat = rows.reshape(lead + (-1,))
    parts, start = [], 0
    for shape in shapes:
        size = math.prod(shape)
        parts.append(flat[..., start : start + size].reshape(lead + shape))
        start += size
    return parts


MESH_IDS = pl.DeviceIdType.MESH
VMEM_BYTES = 67_000_000
BY_ROLE, BY_SHARD, BY_COLUMN = range(3)


def flipped(value, step, size):
    total, bit = 0, 1
    while bit < size:
        digit = (value // bit) % 2
        total = total + bit * ((digit + 1) % 2 if step & bit else digit)
        bit *= 2
    return total


def greet(peers):
    barrier = pltpu.get_barrier_semaphore()
    for peer in peers:
        pl.semaphore_signal(barrier, inc=1, device_id=peer, device_id_type=MESH_IDS)
    pl.semaphore_wait(barrier, len(peers))


def remote(source, target, send_sem, recv_sem, peer):
    return pltpu.make_async_remote_copy(
        src_ref=source,
        dst_ref=target,
        send_sem=send_sem,
        recv_sem=recv_sem,
        device_id=peer,
        device_id_type=MESH_IDS,
    )


def exchange_kernel(axis, size, spread_out, rows_ref, out_ref, send_sem, recv_sem):
    me = lax.axis_index(axis)
    greet([{axis: (me + step) % size} for step in range(1, size)])

    def piece(target):
        return rows_ref.at[target] if spread_out else rows_ref

    sent = []
    for step in range(1, size):
        peer = (me + step) % size
        copy = remote(
            piece(peer), out_ref.at[me], send_sem.at[step], recv_sem.at[size - step], {axis: peer}
        )
        copy.start()
        sent.append(copy)
    out_ref[me] = rows_ref[me] if spread_out else rows_ref[...]
    for step in range(1, size):
        peer = (me + step) % size
        remote(
            piece(peer), out_ref.at[peer], send_sem.at[step], recv_sem.at[step], {axis: peer}
        ).wait_recv()
    for copy in sent:
        copy.wait_send()


def exchange(rows, axis, spread_out, number):
    size = lax.axis_size(axis)
    block = rows.shape[1:] if spread_out else rows.shape
    return pl.pallas_call(
        functools.partial(exchange_kernel, axis, size, spread_out),
        out_shape=jax.ShapeDtypeStruct((size,) + block, rows.dtype),
        in_specs=[pl.BlockSpec(memory_space=pltpu.VMEM)],
        out_specs=pl.BlockSpec(memory_space=pltpu.VMEM),
        scratch_shapes=[pltpu.SemaphoreType.DMA((size,)), pltpu.SemaphoreType.DMA((size,))],
        compiler_params=pltpu.CompilerParams(
            collective_id=number, has_side_effects=True, vmem_limit_bytes=VMEM_BYTES
        ),
        name=f"exchange{number}",
    )(rows)


class Place:
    def __init__(self, half):
        self.half = half
        self.role = lax.axis_index("dp")
        shard = lax.axis_index("fsdp")
        self.line, self.side = shard // 2, shard % 2
        self.other_side = (self.side + 1) % 2
        self.roles = [flipped(self.role, step, 4) for step in range(4)]
        self.lines = [flipped(self.line, step, half) for step in range(half)]
        self.sides = [self.side, self.other_side]
        self.across = {"dp": self.roles[2]}
        self.beside = {"fsdp": self.line * 2 + self.other_side}
        self.core = {"dp": self.roles[1]}
        self.along = [{"fsdp": line * 2 + self.side} for line in self.lines]

    def greet(self, also=()):
        greet([self.across, self.beside, self.core] + self.along[1:] + list(also))


def cut(rows):
    first = (rows // 2 + 15) // 16 * 16
    return [(0, first), (first, rows - first)]


def block_view(ref, layout, role, line, side, rows):
    if layout == BY_SHARD:
        return ref.at[line, side, role, rows]
    if layout == BY_ROLE:
        return ref.at[role, line, side, rows]
    width = ref.shape[-1] // 4
    return ref.at[line, side, rows, pl.ds(pl.multiple_of(role * width, 128), width)]


def whole_shape(layout, half, rows, columns):
    lead = {BY_ROLE: (4, half, 2), BY_SHARD: (half, 2, 4), BY_COLUMN: (half, 2)}[layout]
    return lead + (rows, 4 * columns if layout == BY_COLUMN else columns)


class GatherUnit:
    def __init__(self, at, piece, out, layout, start, count, side_first, send_sem, recv_sem):
        self.at, self.piece, self.out, self.layout = at, piece, out, layout
        self.rows = pl.ds(start, count)
        self.side_first, self.send_sem, self.recv_sem = side_first, send_sem, recv_sem
        self.sent = []

    def view(self, role, line, side):
        return block_view(self.out, self.layout, role, line, side, self.rows)

    def send(self, number, make):
        self.sent.append((number, make))
        self.copy_of(number, make).start()

    def copy_of(self, number, make):
        source, target, peer = make()
        return remote(source, target, self.send_sem.at[number], self.recv_sem.at[number], peer)

    def got(self, number, target):
        remote(
            target, target, self.send_sem.at[number], self.recv_sem.at[number], self.at.core
        ).wait_recv()

    def numbers(self):
        half = self.at.half
        return half, 2 * half, 3 * half, 3 * half + 1

    def begin(self):
        at = self.at

        def own_to(peer):
            return lambda: (
                self.piece.at[self.rows], self.view(at.role, at.line, at.side), peer
            )

        beside, across, _, _ = self.numbers()
        for step in range(1, at.half):
            self.send(step, own_to(at.along[step]))
        self.send(beside, own_to(at.beside))
        self.send(across, own_to(at.across))

    def pass_on(self, number, peer, *where):
        self.send(number, lambda: (self.view(*where), self.view(*where), peer))

    def line_step(self, step):
        at = self.at
        where = (at.role, at.lines[step], at.side)
        self.got(step, self.view(*where))
        beside, across, _, _ = self.numbers()
        self.pass_on(beside + step, at.beside, *where)
        self.pass_on(across + step, at.across, *where)

    def second(self):
        at, every = self.at, slice(None)
        beside, across, second, core = self.numbers()
        for step in range(at.half):
            if self.side_first:
                self.got(beside + step, self.view(at.role, at.lines[step], at.other_side))
            else:
                self.got(across + step, self.view(at.roles[2], at.lines[step], at.side))
        if self.side_first:
            where = (at.role, every, at.other_side)
            self.pass_on(second, at.across, *where)
        else:
            where = (at.roles[2], every, at.side)
            self.pass_on(second, at.beside, *where)
        self.pass_on(core, at.core, at.role, every, at.side)
        self.pass_on(core + 1, at.core, *where)

    def third(self):
        at, every = self.at, slice(None)
        beside, across, second, core = self.numbers()
        for step in range(at.half):
            if self.side_first:
                self.got(across + step, self.view(at.roles[2], at.lines[step], at.side))
            else:
                self.got(beside + step, self.view(at.role, at.lines[step], at.other_side))
        if self.side_first:
            self.pass_on(core + 2, at.core, at.roles[2], every, at.side)
        else:
            self.pass_on(core + 2, at.core, at.role, every, at.other_side)
        last = (at.roles[2], every, at.other_side)
        self.got(second, self.view(*last))
        self.pass_on(core + 3, at.core, *last)

    def finish(self):
        at, every = self.at, slice(None)
        core = self.numbers()[3]
        near, far = at.roles[1], at.roles[3]
        views = [
            self.view(near, every, at.side),
            self.view(near, every, at.other_side),
            self.view(far, every, at.side),
            self.view(far, every, at.other_side),
        ]
        if not self.side_first:
            views[1], views[2] = views[2], views[1]
        for step, view in enumerate(views):
            self.got(core + step, view)
        for number, make in self.sent:
            self.copy_of(number, make).wait_send()


def gather_start(at, layouts, pieces, outs, send_sem, recv_sem, local_sem):
    pairs, local = [], []
    for matrix, layout in enumerate(layouts):
        rows = pieces[matrix].shape[0]
        pairs.append(
            [
                GatherUnit(
                    at,
                    pieces[matrix],
                    outs[matrix],
                    layout,
                    start,
                    size,
                    part == 0,
                    send_sem.at[2 * matrix + part],
                    recv_sem.at[2 * matrix + part],
                )
                for part, (start, size) in enumerate(cut(rows))
            ]
        )

        def make(matrix=matrix, layout=layout, rows=rows):
            target = block_view(outs[matrix], layout, at.role, at.line, at.side, pl.ds(0, rows))
            return pltpu.make_async_copy(pieces[matrix], target, local_sem.at[matrix])

        make().start()
        local.append(make)
    for unit in pairs[0]:
        unit.begin()
    return pairs, local


def gather_actions(pairs, local):
    half, count = pairs[0][0].at.half, len(pairs)
    actions = []

    def each(pair, name, *given):
        def act():
            for unit in pair:
                getattr(unit, name)(*given)

        actions.append(act)

    def settle():
        for make in local:
            make().wait()

    actions.append(settle)
    for matrix in range(count + 1):
        if matrix < count:
            for step in range(1, half):
                each(pairs[matrix], "line_step", step)
            if matrix + 1 < count:
                each(pairs[matrix + 1], "begin")
            each(pairs[matrix], "second")
        if matrix:
            each(pairs[matrix - 1], "third")
    for pair in pairs:
        each(pair, "finish")
    return actions


def gather_scratch(count, half):
    return [
        pltpu.SemaphoreType.DMA((2 * count, 3 * half + 5)),
        pltpu.SemaphoreType.DMA((2 * count, 3 * half + 5)),
        pltpu.SemaphoreType.DMA((count,)),
    ]


def gather_kernel(half, layouts, *refs):
    count = len(layouts)
    at = Place(half)
    at.greet()
    pairs, local = gather_start(
        at, layouts, refs[:count], refs[count : 2 * count], *refs[2 * count :]
    )
    for action in gather_actions(pairs, local):
        action()


def gather(pieces, layouts, number):
    half = lax.axis_size("fsdp") // 2
    count = len(pieces)
    return pl.pallas_call(
        functools.partial(gather_kernel, half, layouts),
        out_shape=[
            jax.ShapeDtypeStruct(whole_shape(layout, half, *piece.shape), piece.dtype)
            for piece, layout in zip(pieces, layouts)
        ],
        in_specs=[pl.BlockSpec(memory_space=pltpu.VMEM)] * count,
        out_specs=[pl.BlockSpec(memory_space=pl.ANY)] * count,
        scratch_shapes=gather_scratch(count, half),
        compiler_params=pltpu.CompilerParams(
            collective_id=number, has_side_effects=True, vmem_limit_bytes=VMEM_BYTES
        ),
        name=f"gather{number}",
    )(*pieces)


def accumulate(target, source):
    rows = target.shape[0]
    chunk = 16 if rows % 16 == 0 else rows

    def step(index, carry):
        place_of = pl.ds(pl.multiple_of(index * chunk, chunk), chunk)
        target[place_of] = target[place_of] + source[place_of]
        return carry

    lax.fori_loop(0, rows // chunk, step, 0)


class ScatterUnit:
    def __init__(self, at, terms, out, layout, start, count, across_first, sems, buffers):
        self.at, self.terms, self.out, self.layout = at, terms, out, layout
        self.rows = pl.ds(start, count)
        self.across_first = across_first
        self.send_sem, self.recv_sem, self.stage_sem = sems
        self.core_buf, self.first_buf, self.last_buf, self.line_buf, self.stage = buffers
        self.sent = []
        half = at.half
        self.base_first, self.base_last = 4, 6
        self.base_line, self.base_share = 6 + half, 6 + 2 * half
        self.first_peer = at.across if across_first else at.beside
        self.last_peer = at.beside if across_first else at.across

    def own_terms(self, first, last, core):
        role_step, side_step = (first, last) if self.across_first else (last, first)
        role = self.at.roles[2 * role_step + core]
        return block_view(
            self.terms, self.layout, role, slice(None), self.at.sides[side_step], self.rows
        )

    def out_view(self, role):
        if self.layout == BY_COLUMN:
            width = self.out.shape[1] // 4
            return self.out.at[self.rows, pl.ds(pl.multiple_of(role * width, 128), width)]
        return self.out.at[role, self.rows]

    def send(self, number, make):
        self.sent.append((number, make))
        self.copy_of(number, make).start()

    def copy_of(self, number, make):
        source, target, peer = make()
        return remote(source, target, self.send_sem.at[number], self.recv_sem.at[number], peer)

    def got(self, number, target):
        remote(
            target, target, self.send_sem.at[number], self.recv_sem.at[number], self.at.core
        ).wait_recv()

    def add_lines(self, target, source):
        def step(line, carry):
            accumulate(target.at[line], source.at[line])
            return carry

        lax.fori_loop(0, self.at.half, step, 0)

    def begin(self):
        for first in (1, 0):
            for last in (1, 0):
                self.send(
                    2 * first + last,
                    lambda first=first, last=last: (
                        self.own_terms(first, last, 1), self.core_buf.at[first, last], self.at.core
                    ),
                )

    def paired(self, first, last):
        buffer = self.core_buf.at[first, last]
        load = pltpu.make_async_copy(self.own_terms(first, last, 0), self.stage, self.stage_sem)
        load.start()
        self.got(2 * first + last, buffer)
        load.wait()
        self.add_lines(buffer, self.stage)
        if first:
            self.send(
                self.base_first + last,
                lambda: (
                    self.core_buf.at[first, last], self.first_buf.at[last], self.first_peer
                ),
            )

    def joined(self, last):
        buffer = self.first_buf.at[last]
        self.got(self.base_first + last, buffer)
        self.add_lines(buffer, self.core_buf.at[0, last])
        if last:
            for step in list(range(self.at.half - 1, 0, -1)) + [0]:
                self.send(
                    self.base_last + step,
                    lambda line=self.at.lines[step]: (
                        self.first_buf.at[last, line], self.last_buf.at[line], self.last_peer
                    ),
                )

    def lined(self, step):
        line = self.at.lines[step]
        block = self.last_buf.at[line]
        self.got(self.base_last + step, block)
        accumulate(block, self.first_buf.at[0, line])
        if step:
            self.send(
                self.base_line + step,
                lambda: (self.last_buf.at[line], self.line_buf.at[step], self.at.along[step]),
            )

    def end(self):
        at = self.at
        own = self.last_buf.at[at.line]
        for step in range(1, at.half):
            self.got(self.base_line + step, self.line_buf.at[step])
            accumulate(own, self.line_buf.at[step])
        target = self.out_view(at.role)
        target[...] = own[...]
        for step in (1, 2, 3):
            self.send(
                self.base_share + step,
                lambda step=step: (
                    self.last_buf.at[at.line], self.out_view(at.role), {"dp": at.roles[step]}
                ),
            )

    def finish(self):
        for step in (1, 2, 3):
            self.got(self.base_share + step, self.out_view(self.at.roles[step]))
        for number, make in self.sent:
            self.copy_of(number, make).wait_send()


def scatter_actions(pairs):
    half = pairs[0][0].at.half
    steps = list(range(half - 1, 0, -1)) + [0]
    stages = [
        [("paired", 1, 1), ("paired", 1, 0)],
        [("paired", 0, 1), ("paired", 0, 0)],
        [("joined", 1), ("joined", 0)],
        [("lined", step) for step in steps],
        [("end",)],
    ]
    actions = []

    def each(pair, name, *given):
        def act():
            for unit in pair:
                getattr(unit, name)(*given)

        actions.append(act)

    for turn in range(len(stages) + len(pairs) - 1):
        for index, pair in reversed(list(enumerate(pairs))):
            if 0 <= turn - index < len(stages):
                for call in stages[turn - index]:
                    each(pair, *call)
    for pair in pairs:
        each(pair, "finish")
    return actions


def scatter_start(at, layouts, terms, outs, scratch):
    sems, buffers = scratch[:3], scratch[3:]
    pairs = []
    for matrix, layout in enumerate(layouts):
        pair = []
        for part, (start, size) in enumerate(cut(terms[matrix].shape[-2])):
            unit = 2 * matrix + part
            pair.append(
                ScatterUnit(
                    at,
                    terms[matrix],
                    outs[matrix],
                    layout,
                    start,
                    size,
                    part == 0,
                    [sem.at[unit] for sem in sems],
                    buffers[5 * unit : 5 * unit + 5],
                )
            )
        pairs.append(pair)
    for pair in pairs:
        for unit in pair:
            unit.begin()
    return pairs


def scatter_scratch(count, half, rows, columns):
    scratch = [pltpu.SemaphoreType.DMA((2 * count, 2 * half + 10))] * 2
    scratch += [pltpu.SemaphoreType.DMA((2 * count,))]
    for _ in range(count):
        for _, size in cut(rows):
            for lead in ((2, 2, half), (2, half), (half,), (half,), (half,)):
                scratch.append(pltpu.VMEM(lead + (size, columns), jnp.bfloat16))
    return scratch


def scatter_outs(layouts, rows, columns):
    return [
        jax.ShapeDtypeStruct(
            (rows, 4 * columns) if layout == BY_COLUMN else (4, rows, columns), jnp.bfloat16
        )
        for layout in layouts
    ]


def roles_kernel(half, *refs):
    ins, out, terms, local_sem, scratch = refs[:4], refs[4], refs[5], refs[6], refs[7:]
    at = Place(half)
    local = []
    for role in range(4):
        copy = pltpu.make_async_copy(ins[role], terms.at[role], local_sem.at[role])
        copy.start()
        local.append(copy)
    at.greet([{"dp": at.roles[3]}])
    for copy in local:
        copy.wait()
    pairs = scatter_start(at, (BY_ROLE,), [terms], [out], scratch)
    for action in scatter_actions(pairs):
        action()


def scatter_roles(gradients, number):
    half = lax.axis_size("fsdp") // 2
    rows, columns = gradients[0].shape[-2:]
    return pl.pallas_call(
        functools.partial(roles_kernel, half),
        out_shape=scatter_outs((BY_ROLE,), rows, columns)[0],
        in_specs=[pl.BlockSpec(memory_space=pl.ANY)] * 4,
        out_specs=pl.BlockSpec(memory_space=pltpu.VMEM),
        scratch_shapes=[
            pltpu.VMEM((4, half, 2, rows, columns), jnp.bfloat16),
            pltpu.SemaphoreType.DMA((4,)),
        ]
        + scatter_scratch(1, half, rows, columns),
        compiler_params=pltpu.CompilerParams(
            collective_id=number, has_side_effects=True, vmem_limit_bytes=VMEM_BYTES
        ),
        name=f"scatter{number}",
    )(*gradients)


def head_window(head, width, columns):
    tile = jnp.minimum(head * width // 128, columns // 128 - 2)
    lane = lax.broadcasted_iota(jnp.int32, (1, 256), 1) + tile * 128
    inside = jnp.logical_and(lane >= head * width, lane < (head + 1) * width)
    return pl.ds(pl.multiple_of(tile * 128, 128), 256), jnp.where(inside, 1.0, 0.0)


def dot_nt(left, right):
    return lax.dot_general(
        left, right, (((1,), (1,)), ((), ())), preferred_element_type=jnp.float32
    )


def dot_tn(left, right):
    return lax.dot_general(
        left, right, (((0,), (0,)), ((), ())), preferred_element_type=jnp.float32
    )


def attend_head(head, width, q_ref, k_ref, v_ref, o_ref, log_ref):
    scaling = width ** (-0.5)
    window, inside = head_window(head, width, q_ref.shape[1])
    queries = q_ref[:, window] * inside.astype(jnp.bfloat16)
    scores = dot_nt(queries, k_ref[:, window]) * scaling
    row_max = jnp.max(scores, axis=-1, keepdims=True)
    exponent = jnp.exp(scores - row_max)
    row_total = jnp.sum(exponent, axis=-1, keepdims=True)
    weights = (exponent * (1.0 / row_total)).astype(jnp.bfloat16)
    result = jnp.dot(weights, v_ref[:, window], preferred_element_type=jnp.float32)
    o_ref[:, window] += result * inside
    lane = lax.broadcasted_iota(jnp.int32, (1, log_ref.shape[1]), 1)
    log_ref[...] = jnp.where(lane == head, row_max + jnp.log(row_total), log_ref[...])


def attend_back_head(head, width, q_ref, k_ref, v_ref, g_ref, log_ref, dq_ref, dk_ref, dv_ref):
    scaling = width ** (-0.5)
    window, inside = head_window(head, width, q_ref.shape[1])
    inside_low = inside.astype(jnp.bfloat16)
    queries, grads = q_ref[:, window] * inside_low, g_ref[:, window] * inside_low
    key_rows = k_ref[:, window]
    lane = lax.broadcasted_iota(jnp.int32, (1, log_ref.shape[1]), 1)
    log_total = jnp.sum(jnp.where(lane == head, log_ref[...], 0.0), axis=-1, keepdims=True)
    weights = jnp.exp(dot_nt(queries, key_rows) * scaling - log_total)
    dv_ref[:, window] += dot_tn(weights.astype(jnp.bfloat16), grads)
    d_weights = dot_nt(grads, v_ref[:, window])
    inner = jnp.sum(weights * d_weights, axis=-1, keepdims=True)
    d_scores = (weights * (d_weights - inner)).astype(jnp.bfloat16)
    dq_ref[:, window] += jnp.dot(d_scores, key_rows, preferred_element_type=jnp.float32) * (
        inside * scaling
    )
    dk_ref[:, window] += dot_tn(d_scores, queries) * scaling


def run_heads(head_count, attend_one, actions):
    spread_over = {}
    for index, action in enumerate(actions):
        spread_over.setdefault(index * head_count // len(actions), []).append(action)

    def step(head, carry):
        attend_one(head)
        for when, group in spread_over.items():

            @pl.when(head == when)
            def _(group=group):
                for action in group:
                    action()

        return carry

    lax.fori_loop(0, head_count, step, 0)


def forward_kernel(half, layouts, heads, *refs):
    count = len(layouts)
    q_ref, k_ref, v_ref = refs[:3]
    pieces = refs[3 : 3 + count]
    o_ref, log_ref, keys, values = refs[3 + count : 7 + count]
    outs = refs[7 + count : 7 + 2 * count]
    send_sem, recv_sem = refs[7 + 2 * count : 9 + 2 * count]
    at = Place(half)
    width = q_ref.shape[1] // heads
    rows = keys.shape[0] // 4
    short = q_ref.shape[0] - rows
    own = pl.ds(short, rows)
    beside, along = at.beside, at.along[1]

    def quarter(buffer, index):
        return buffer.at[pl.ds(index * rows, rows)]

    at.greet()
    sent = []

    def send(number, source, target, peer):
        copy = remote(source, target, send_sem.at[number], recv_sem.at[number], peer)
        copy.start()
        sent.append(copy)

    def got(number, target):
        remote(target, target, send_sem.at[number], recv_sem.at[number], along).wait_recv()

    send(0, k_ref.at[own], quarter(keys, 1), beside)
    send(1, v_ref.at[own], quarter(values, 2), along)
    send(2, v_ref.at[own], quarter(values, 1), beside)
    send(3, k_ref.at[own], quarter(keys, 2), along)
    pairs, local = gather_start(at, layouts, pieces, outs, *refs[9 + 2 * count :])
    quarter(keys, 0)[...] = k_ref[own]
    quarter(values, 0)[...] = v_ref[own]
    o_ref[...] = jnp.zeros_like(o_ref)
    log_ref[...] = jnp.zeros_like(log_ref)

    def pass_on():
        got(0, quarter(keys, 1))
        send(4, quarter(keys, 1), quarter(keys, 3), along)
        got(1, quarter(values, 2))
        send(5, quarter(values, 2), quarter(values, 3), beside)

    actions = gather_actions(pairs, local)
    early = 1 + (half - 1)
    first = pl.ds(0, short)
    run_heads(
        heads,
        lambda head: attend_head(
            head,
            width,
            q_ref.at[first],
            k_ref.at[first],
            v_ref.at[first],
            o_ref.at[first],
            log_ref.at[first],
        ),
        [lambda: None, lambda: None, lambda: None] + actions[:early],
    )
    pass_on()
    for action in actions[early : early + 2]:
        action()
    got(2, quarter(values, 1))
    got(3, quarter(keys, 2))
    got(4, quarter(keys, 3))
    got(5, quarter(values, 3))
    run_heads(
        heads,
        lambda head: attend_head(
            head, width, q_ref.at[own], keys, values, o_ref.at[own], log_ref.at[own]
        ),
        actions[early + 2 : -count],
    )
    for action in actions[-count:]:
        action()
    for copy in sent:
        copy.wait_send()


def attention_forward(q_rows, k_rows, v_rows, pieces, layouts, heads, rows, number):
    half = lax.axis_size("fsdp") // 2
    count = len(pieces)
    vmem, hbm = pl.BlockSpec(memory_space=pltpu.VMEM), pl.BlockSpec(memory_space=pl.ANY)
    total, columns = q_rows.shape
    outs = [
        jax.ShapeDtypeStruct((total, columns), jnp.float32),
        jax.ShapeDtypeStruct((total, 128), jnp.float32),
        jax.ShapeDtypeStruct((4 * rows, columns), jnp.bfloat16),
        jax.ShapeDtypeStruct((4 * rows, columns), jnp.bfloat16),
    ] + [
        jax.ShapeDtypeStruct(whole_shape(layout, half, *piece.shape), piece.dtype)
        for piece, layout in zip(pieces, layouts)
    ]
    return pl.pallas_call(
        functools.partial(forward_kernel, half, layouts, heads),
        out_shape=outs,
        in_specs=[vmem] * (3 + count),
        out_specs=[vmem] * 4 + [hbm] * count,
        scratch_shapes=[pltpu.SemaphoreType.DMA((6,)), pltpu.SemaphoreType.DMA((6,))]
        + gather_scratch(count, half),
        compiler_params=pltpu.CompilerParams(
            collective_id=number, has_side_effects=True, vmem_limit_bytes=VMEM_BYTES
        ),
        name=f"attention{number}",
    )(q_rows, k_rows, v_rows, *pieces)


def backward_kernel(half, layouts, heads, *refs):
    count = len(layouts)
    q_ref, k_ref, v_ref, g_ref, log_ref, keys, values = refs[:7]
    terms = refs[7 : 7 + count]
    dq_out, dk_out, dv_out = refs[7 + count : 10 + count]
    outs = refs[10 + count : 10 + 2 * count]
    rest = refs[10 + 2 * count :]
    dq, dk, dv, wide, wide_got, slim, slim_got, send_sem, recv_sem = rest[:9]
    at = Place(half)
    width = q_ref.shape[1] // heads
    rows = keys.shape[0] // 4
    short = q_ref.shape[0] - rows
    own, first = pl.ds(short, rows), pl.ds(0, short)
    beside, along = at.beside, at.along[1]
    at.greet([{"dp": at.roles[3]}])
    pairs = scatter_start(at, layouts, terms, outs, rest[9:])
    actions = scatter_actions(pairs)
    dq[...] = jnp.zeros_like(dq)
    dk[...] = jnp.zeros_like(dk)
    dv[...] = jnp.zeros_like(dv)
    sent = []

    def send(number, source, target, peer):
        copy = remote(source, target, send_sem.at[number], recv_sem.at[number], peer)
        copy.start()
        sent.append(copy)

    def got(number, target):
        remote(target, target, send_sem.at[number], recv_sem.at[number], along).wait_recv()

    def quarter(index):
        return pl.ds(index * rows, rows)

    split = 2 * len(actions) // 5
    run_heads(
        heads,
        lambda head: attend_back_head(
            head,
            width,
            q_ref.at[own],
            keys,
            values,
            g_ref.at[own],
            log_ref.at[own],
            dq.at[own],
            dk,
            dv,
        ),
        actions[:split],
    )
    for part, (source, index) in enumerate([(dk, 2), (dk, 3), (dv, 1), (dv, 3)]):
        wide[part] = source[quarter(index)].astype(jnp.bfloat16)
    send(0, wide.at[pl.ds(0, 2)], wide_got.at[pl.ds(0, 2)], along)
    send(1, wide.at[pl.ds(2, 2)], wide_got.at[pl.ds(2, 2)], beside)
    short_dk, short_dv = dk.at[pl.ds(2 * rows, short)], dv.at[pl.ds(rows, short)]
    short_dk[...] = jnp.zeros_like(short_dk)
    short_dv[...] = jnp.zeros_like(short_dv)
    run_heads(
        heads,
        lambda head: attend_back_head(
            head,
            width,
            q_ref.at[first],
            k_ref.at[first],
            v_ref.at[first],
            g_ref.at[first],
            log_ref.at[first],
            dq.at[first],
            short_dk,
            short_dv,
        ),
        actions[split : split + 2],
    )
    dq_out[...] = dq[...].astype(jnp.bfloat16)
    dk_out[first] = short_dk[...].astype(jnp.bfloat16)
    dv_out[first] = short_dv[...].astype(jnp.bfloat16)
    got(0, wide_got.at[pl.ds(0, 2)])
    slim[0] = (dk[quarter(1)] + wide_got[1].astype(jnp.float32)).astype(jnp.bfloat16)
    send(2, slim.at[0], slim_got.at[0], beside)
    got(1, wide_got.at[pl.ds(2, 2)])
    slim[1] = (dv[quarter(2)] + wide_got[3].astype(jnp.float32)).astype(jnp.bfloat16)
    send(3, slim.at[1], slim_got.at[1], along)
    for action in actions[split + 2 : -count]:
        action()
    got(2, slim_got.at[0])
    total = dk[quarter(0)] + wide_got[0].astype(jnp.float32) + slim_got[0].astype(jnp.float32)
    dk_out[own] = total.astype(jnp.bfloat16)
    got(3, slim_got.at[1])
    total = dv[quarter(0)] + wide_got[2].astype(jnp.float32) + slim_got[1].astype(jnp.float32)
    dv_out[own] = total.astype(jnp.bfloat16)
    for action in actions[-count:]:
        action()
    for copy in sent:
        copy.wait_send()


def attention_backward(rows_in, keys, values, gradients, layouts, heads, rows, columns, number):
    half = lax.axis_size("fsdp") // 2
    count = len(gradients)
    vmem, hbm = pl.BlockSpec(memory_space=pltpu.VMEM), pl.BlockSpec(memory_space=pl.ANY)
    total, model_width = rows_in[0].shape
    quarter_rows = keys.shape[0] // 4
    low_rows = jax.ShapeDtypeStruct((total, model_width), jnp.bfloat16)
    return pl.pallas_call(
        functools.partial(backward_kernel, half, layouts, heads),
        out_shape=[low_rows] * 3 + scatter_outs(layouts, rows, columns),
        in_specs=[vmem] * 7 + [hbm] * count,
        out_specs=[vmem] * (3 + count),
        scratch_shapes=[
            pltpu.VMEM((total, model_width), jnp.float32),
            pltpu.VMEM((4 * quarter_rows, model_width), jnp.float32),
            pltpu.VMEM((4 * quarter_rows, model_width), jnp.float32),
            pltpu.VMEM((4, quarter_rows, model_width), jnp.bfloat16),
            pltpu.VMEM((4, quarter_rows, model_width), jnp.bfloat16),
            pltpu.VMEM((2, quarter_rows, model_width), jnp.bfloat16),
            pltpu.VMEM((2, quarter_rows, model_width), jnp.bfloat16),
            pltpu.SemaphoreType.DMA((4,)),
            pltpu.SemaphoreType.DMA((4,)),
        ]
        + scatter_scratch(count, half, rows, columns),
        compiler_params=pltpu.CompilerParams(
            collective_id=number, has_side_effects=True, vmem_limit_bytes=VMEM_BYTES
        ),
        name=f"attention{number}",
    )(*rows_in, keys, values, *gradients)


def product(left, right):
    return jnp.dot(left, right, preferred_element_type=jnp.float32)


def product_tn(left, right):
    return lax.dot_general(
        left, right, (((0,), (0,)), ((), ())), preferred_element_type=jnp.float32
    )


def product_nt(left, right):
    return lax.dot_general(
        left, right, (((1,), (1,)), ((), ())), preferred_element_type=jnp.float32
    )


def spread(per_slot, short_count, len_short, quarter_rows):
    width = per_slot.shape[1]
    short_part = jnp.broadcast_to(
        per_slot[:short_count, None, :], (short_count, len_short, width)
    ).reshape(short_count * len_short, width)
    long_part = jnp.broadcast_to(per_slot[short_count:], (quarter_rows, width))
    return jnp.concatenate([short_part, long_part], 0)


def slot_sum(values, short_count, len_short):
    short_rows = short_count * len_short
    short_part = jnp.sum(
        values[:short_rows].reshape((short_count, len_short) + values.shape[1:]), axis=1
    )
    long_part = jnp.sum(values[short_rows:], axis=0, keepdims=True)
    return jnp.concatenate([short_part, long_part], 0)


def norm_parts(values):
    average = jnp.mean(values, axis=-1, keepdims=True)
    centred = values - average
    variance = jnp.mean(centred * centred, axis=-1, keepdims=True)
    inverse = lax.rsqrt(variance + epsilon)
    return (centred * inverse, inverse)


def norm_back(gradient, normed, inverse):
    return inverse * (
        gradient
        - jnp.mean(gradient, axis=-1, keepdims=True)
        - normed * jnp.mean(gradient * normed, axis=-1, keepdims=True)
    )


def silu_grad(values):
    sigmoid_value = jax.nn.sigmoid(values)
    return sigmoid_value * (1.0 + values * (1.0 - sigmoid_value))


def gelu_tanh(values):
    return jax.nn.gelu(values, approximate=True)


def per_device(
    x_short,
    x_long,
    short_cond,
    long_cond,
    short_heads,
    long_heads,
    short_groups,
    long_groups,
    short_keep,
    long_keep,
    w_ada,
    b_ada,
    w_head_router,
    w_group_router,
    w_qkv,
    w_proj,
    b_proj,
    w_fc1,
    b_fc1,
    w_fc2,
    b_fc2,
    g_short,
    g_long,
):
    short_count, len_short, model_width = x_short.shape
    quarter_rows = x_long.shape[0]
    head_count = w_head_router.shape[1]
    head_width = model_width // head_count
    group_count = w_group_router.shape[1]
    slot_count = short_count + 1
    short_rows = short_count * len_short
    row_count = short_rows + quarter_rows
    fsdp_index = lax.axis_index("fsdp")
    fsdp_count = lax.axis_size("fsdp")
    role = lax.axis_index("dp")
    group_row = fsdp_index // SPLIT
    half = fsdp_count // 2
    shard_rows = w_qkv.shape[0]
    unit_rows = w_fc2.shape[0] // 4
    short_act = low(jax.nn.silu(short_cond))
    long_act = low(jax.nn.silu(long_cond))
    message = exchange(packed([short_act, b_proj, b_fc1, b_fc2], 16), "fsdp", False, 0)
    act_rows, proj_bias, fc1_bias, fc2_bias = unpacked(
        message, [(model_width,), b_proj.shape, b_fc1.shape, b_fc2.shape]
    )
    proj_bias, fc1_bias, fc2_bias = (
        bias.reshape(-1).astype(jnp.float32) for bias in (proj_bias, fc1_bias, fc2_bias)
    )
    item_act = jnp.concatenate([act_rows, long_act], 0)
    item_columns = lax.dynamic_slice_in_dim(item_act, fsdp_index * shard_rows, shard_rows, 1)
    bias_row = lax.dynamic_update_slice_in_dim(
        jnp.zeros((fsdp_count * b_ada.shape[0],), jnp.float32),
        b_ada.astype(jnp.float32),
        fsdp_index * b_ada.shape[0],
        0,
    )
    partial = jnp.concatenate(
        [
            product(item_columns, w_ada) + bias_row,
            product(item_columns, w_head_router),
            product(item_columns, w_group_router),
        ],
        1,
    )
    width = partial.shape[1]
    for_device = jnp.stack(
        [partial[:fsdp_count], jnp.repeat(partial[fsdp_count:], SPLIT, axis=0)], 1
    ).reshape(fsdp_count, -1)
    for_device = jnp.pad(for_device, ((0, 0), (0, -for_device.shape[1] % 1024)))
    shares = exchange(for_device.reshape(fsdp_count, -1, 128), "fsdp", True, 1)
    conditioned = unpacked(jnp.sum(shares, axis=0), [(2, width)])[0]
    mixed_shard = jnp.concatenate([w_qkv, w_proj], 1)
    attention_piece = lax.dynamic_slice_in_dim(mixed_shard, role * model_width, model_width, 1)
    (attention_full,) = gather([attention_piece], (BY_ROLE,), 2)
    attention_full = attention_full.reshape(4, -1, model_width)
    mod_width = 6 * model_width
    modulation = conditioned[:, :mod_width]
    head_sigmoid = jax.nn.sigmoid(conditioned[:, mod_width : mod_width + head_count])
    group_sigmoid = jax.nn.sigmoid(conditioned[:, mod_width + head_count :])
    head_mask = jnp.concatenate(
        [short_heads, lax.dynamic_slice_in_dim(long_heads, group_row, 1, 0)], 0
    ).astype(jnp.float32)
    group_mask = jnp.concatenate(
        [short_groups, lax.dynamic_slice_in_dim(long_groups, group_row, 1, 0)], 0
    ).astype(jnp.float32)
    head_gate = head_mask * 2.0 * head_sigmoid
    group_gate = group_mask * 2.0 * group_sigmoid
    shift1, scale1, gate1, shift2, scale2, gate2 = jnp.split(
        spread(modulation, short_count, len_short, quarter_rows), 6, axis=1
    )
    x_rows = jnp.concatenate([x_short.reshape(short_rows, model_width), x_long], 0).astype(
        jnp.float32
    )
    keep_rows = jnp.concatenate([short_keep.reshape(short_rows), long_keep], 0).astype(jnp.float32)[
        :, None
    ]
    normed1, inverse1 = norm_parts(x_rows)
    hidden1 = low(normed1 * (1.0 + scale1) + shift1)
    q_rows, k_rows, v_rows = (low(product(hidden1, attention_full[part])) for part in range(3))

    fc1_piece = lax.dynamic_slice_in_dim(w_fc1, role * model_width, model_width, 1)
    fc2_piece = lax.dynamic_slice_in_dim(w_fc2, role * unit_rows, unit_rows, 0)
    head_rows, log_rows, keys, values, fc1_full, fc2_full = attention_forward(
        q_rows,
        k_rows,
        v_rows,
        [fc1_piece, fc2_piece],
        (BY_COLUMN, BY_SHARD),
        head_count,
        quarter_rows,
        3,
    )
    head_rows = head_rows.reshape(row_count, head_count, head_width)
    head_gate_rows = spread(head_gate, short_count, len_short, quarter_rows)[:, :, None]
    attention = low((head_rows * head_gate_rows).reshape(row_count, model_width))
    projected = product(attention, attention_full[3]) + proj_bias
    mixed = x_rows + gate1 * projected
    fc1_full = fc1_full.reshape(model_width, -1)
    fc2_full = fc2_full.reshape(-1, model_width)
    normed2, inverse2 = norm_parts(mixed)
    hidden2 = low(normed2 * (1.0 + scale2) + shift2)
    channel_gate = spread(
        jnp.repeat(group_gate, CHAN, axis=1), short_count, len_short, quarter_rows
    )
    up_rows = product(hidden2, fc1_full) + fc1_bias
    gelu_value, gelu_pull = jax.vjp(gelu_tanh, up_rows)
    activated = low(gelu_value * channel_gate)
    down_rows = product(activated, fc2_full) + fc2_bias
    out_rows = mixed + gate2 * keep_rows * down_rows
    y_short = low(out_rows[:short_rows].reshape(x_short.shape))
    y_long = low(out_rows[short_rows:])
    gradient = jnp.concatenate([g_short.reshape(short_rows, model_width), g_long], 0).astype(
        jnp.float32
    )
    d_down = low(gradient * gate2 * keep_rows)
    slot_gate2 = slot_sum(gradient * keep_rows * down_rows, short_count, len_short)
    grad_fc2 = low(product_tn(activated, d_down)).reshape(half, 2, 4, unit_rows, model_width)
    d_activated = product_nt(d_down, fc2_full)
    d_channel = slot_sum(d_activated * gelu_value, short_count, len_short)
    d_group = jnp.sum(d_channel.reshape(slot_count, group_count, CHAN), axis=-1)
    d_up = low(gelu_pull(d_activated * channel_gate)[0])
    grad_fc1 = low(product_tn(hidden2, d_up)).reshape(half, 2, shard_rows, -1)
    d_hidden2 = product_nt(d_up, fc1_full)

    def blocks(grad):
        return low(grad).reshape(half, 2, shard_rows, model_width)

    slot_shift2 = slot_sum(d_hidden2, short_count, len_short)
    slot_scale2 = slot_sum(d_hidden2 * normed2, short_count, len_short)
    d_mixed = gradient + norm_back(d_hidden2 * (1.0 + scale2), normed2, inverse2)
    d_projected = low(d_mixed * gate1)
    slot_gate1 = slot_sum(d_mixed * projected, short_count, len_short)
    d_attention = product_nt(d_projected, attention_full[3]).reshape(
        row_count, head_count, head_width
    )
    d_head = slot_sum(jnp.sum(d_attention * head_rows, axis=-1), short_count, len_short)
    d_heads = low(d_attention * head_gate_rows)
    bias_grad = jnp.concatenate(
        [jnp.sum(part, axis=0, dtype=jnp.float32) for part in (d_projected, d_up, d_down)]
    )
    dq_rows, dk_rows, dv_rows, fc1_sum, fc2_sum = attention_backward(
        [q_rows, k_rows, v_rows, d_heads.reshape(row_count, model_width), log_rows],
        keys,
        values,
        [grad_fc1, grad_fc2],
        (BY_COLUMN, BY_SHARD),
        head_count,
        shard_rows,
        model_width,
        4,
    )
    g_w_fc1 = fc1_sum.astype(jnp.float32)
    g_w_fc2 = fc2_sum.reshape(-1, model_width).astype(jnp.float32)
    attention_sum = scatter_roles(
        [
            blocks(product_tn(hidden1, dq_rows)),
            blocks(product_tn(hidden1, dk_rows)),
            blocks(product_tn(hidden1, dv_rows)),
            blocks(product_tn(attention, d_projected)),
        ],
        5,
    )
    g_w_qkv = attention_sum[:3].transpose(1, 0, 2).reshape(shard_rows, -1).astype(jnp.float32)
    g_w_proj = attention_sum[3].astype(jnp.float32)
    d_hidden1 = (
        product_nt(dq_rows, attention_full[0])
        + product_nt(dk_rows, attention_full[1])
        + product_nt(dv_rows, attention_full[2])
    )
    slot_shift1 = slot_sum(d_hidden1, short_count, len_short)
    slot_scale1 = slot_sum(d_hidden1 * normed1, short_count, len_short)
    d_rows = d_mixed + norm_back(d_hidden1 * (1.0 + scale1), normed1, inverse1)
    dx_short = low(d_rows[:short_rows].reshape(x_short.shape))
    dx_long = low(d_rows[short_rows:])
    d_head_logit = d_head * head_mask * 2.0 * head_sigmoid * (1.0 - head_sigmoid)
    d_group_logit = d_group * group_mask * 2.0 * group_sigmoid * (1.0 - group_sigmoid)
    d_conditioned = jnp.concatenate(
        [
            slot_shift1,
            slot_scale1,
            slot_gate1,
            slot_shift2,
            slot_scale2,
            slot_gate2,
            d_head_logit,
            d_group_logit,
        ],
        1,
    )
    member_rows = exchange(packed([low(d_conditioned), low(bias_grad)], 16), "fsdp", False, 6)
    member_rows, bias_rows = unpacked(member_rows, [(2, width), bias_grad.shape])
    long_sum = jnp.sum(
        member_rows[:, 1].astype(jnp.float32).reshape(-1, SPLIT, width), axis=1
    )
    d_items = jnp.concatenate([member_rows[:, 0], low(long_sum)], 0)
    group_bias = jnp.sum(bias_rows.astype(jnp.float32), axis=0)
    d_silu = (
        product_nt(d_items[:, :mod_width], w_ada)
        + product_nt(d_items[:, mod_width : mod_width + head_count], w_head_router)
        + product_nt(d_items[:, mod_width + head_count :], w_group_router)
    )
    d_silu = unpacked(exchange(packed([d_silu], 8), "fsdp", False, 7), [d_silu.shape])[0]
    d_silu = d_silu.transpose(1, 0, 2).reshape(-1, model_width)
    d_short_cond = lax.dynamic_slice_in_dim(d_silu, fsdp_index, 1, 0) * silu_grad(short_cond)
    d_long_cond = d_silu[fsdp_count:] * silu_grad(long_cond)
    replicas = exchange(packed([d_items, low(group_bias), item_columns], 16), "dp", False, 8)
    factors, bias_rows, act_factors = unpacked(
        replicas, [d_items.shape, group_bias.shape, item_columns.shape]
    )
    factors, act_factors = factors.reshape(-1, width), act_factors.reshape(-1, shard_rows)
    g_w_ada = product_tn(act_factors, factors[:, :mod_width])
    g_w_head_router = product_tn(act_factors, factors[:, mod_width : mod_width + head_count])
    g_w_group_router = product_tn(act_factors, factors[:, mod_width + head_count :])
    g_b_ada = lax.dynamic_slice_in_dim(
        jnp.sum(factors[:, :mod_width].astype(jnp.float32), axis=0),
        fsdp_index * b_ada.shape[0],
        b_ada.shape[0],
        0,
    )
    bias_sum = jnp.sum(bias_rows.astype(jnp.float32), axis=0)

    def own_bias(start, count):
        return lax.dynamic_slice_in_dim(bias_sum, start + fsdp_index * count, count, 0)

    g_b_proj = own_bias(0, shard_rows)
    g_b_fc1 = own_bias(model_width, 4 * shard_rows)
    g_b_fc2 = own_bias(5 * model_width, shard_rows)
    return (
        y_short,
        y_long,
        dx_short,
        dx_long,
        d_short_cond,
        d_long_cond,
        g_w_ada,
        g_b_ada,
        g_w_head_router,
        g_w_group_router,
        g_w_qkv,
        g_w_proj,
        g_b_proj,
        g_w_fc1,
        g_b_fc1,
        g_w_fc2,
        g_b_fc2,
    )


def solution(mesh):
    return jax.shard_map(
        per_device,
        mesh=mesh,
        in_specs=(
            P(("dp", "fsdp"), None, None),
            P(("dp", "fsdp"), None),
            P(("dp", "fsdp"), None),
            P("dp", None),
            P(("dp", "fsdp"), None),
            P("dp", None),
            P(("dp", "fsdp"), None),
            P("dp", None),
            P(("dp", "fsdp"), None),
            P(("dp", "fsdp")),
            P("fsdp", None),
            P("fsdp"),
            P("fsdp", None),
            P("fsdp", None),
            P("fsdp", None),
            P("fsdp", None),
            P("fsdp"),
            P("fsdp", None),
            P("fsdp"),
            P("fsdp", None),
            P("fsdp"),
            P(("dp", "fsdp"), None, None),
            P(("dp", "fsdp"), None),
        ),
        out_specs=(
            P(("dp", "fsdp"), None, None),
            P(("dp", "fsdp"), None),
            P(("dp", "fsdp"), None, None),
            P(("dp", "fsdp"), None),
            P(("dp", "fsdp"), None),
            P("dp", None),
            P("fsdp", None),
            P("fsdp"),
            P("fsdp", None),
            P("fsdp", None),
            P("fsdp", None),
            P("fsdp", None),
            P("fsdp"),
            P("fsdp", None),
            P("fsdp"),
            P("fsdp", None),
            P("fsdp"),
        ),
        check_vma=False,
    )
```

```python
import functools
import math

import jax
import jax.numpy as jnp
from jax import lax
from jax.experimental import pallas as pl
from jax.experimental.pallas import tpu as pltpu
from jax.sharding import PartitionSpec as P

CHAN = 128
SPLIT = 4


epsilon = 1e-06


def low(value):
    return value.astype(jnp.bfloat16)


def packed(parts, unit):
    flat = jnp.concatenate([part.reshape(-1) for part in parts])
    return jnp.pad(flat, (0, -flat.size % (unit * 128))).reshape(-1, 128)


def unpacked(rows, shapes):
    lead = rows.shape[:-2]
    flat = rows.reshape(lead + (-1,))
    parts, start = [], 0
    for shape in shapes:
        size = math.prod(shape)
        parts.append(flat[..., start : start + size].reshape(lead + shape))
        start += size
    return parts


MESH_IDS = pl.DeviceIdType.MESH
VMEM_BYTES = 67_000_000
BY_ROLE, BY_SHARD, BY_COLUMN = range(3)


def flipped(value, step, size):
    total, bit = 0, 1
    while bit < size:
        digit = (value // bit) % 2
        total = total + bit * ((digit + 1) % 2 if step & bit else digit)
        bit *= 2
    return total


def greet(peers):
    barrier = pltpu.get_barrier_semaphore()
    for peer in peers:
        pl.semaphore_signal(barrier, inc=1, device_id=peer, device_id_type=MESH_IDS)
    pl.semaphore_wait(barrier, len(peers))


def remote(source, target, send_sem, recv_sem, peer):
    return pltpu.make_async_remote_copy(
        src_ref=source,
        dst_ref=target,
        send_sem=send_sem,
        recv_sem=recv_sem,
        device_id=peer,
        device_id_type=MESH_IDS,
    )


def exchange_kernel(axis, size, spread_out, rows_ref, out_ref, send_sem, recv_sem):
    me = lax.axis_index(axis)
    greet([{axis: (me + step) % size} for step in range(1, size)])

    def piece(target):
        return rows_ref.at[target] if spread_out else rows_ref

    sent = []
    for step in range(1, size):
        peer = (me + step) % size
        copy = remote(
            piece(peer), out_ref.at[me], send_sem.at[step], recv_sem.at[size - step], {axis: peer}
        )
        copy.start()
        sent.append(copy)
    out_ref[me] = rows_ref[me] if spread_out else rows_ref[...]
    for step in range(1, size):
        peer = (me + step) % size
        remote(
            piece(peer), out_ref.at[peer], send_sem.at[step], recv_sem.at[step], {axis: peer}
        ).wait_recv()
    for copy in sent:
        copy.wait_send()


def exchange(rows, axis, spread_out, number):
    size = lax.axis_size(axis)
    block = rows.shape[1:] if spread_out else rows.shape
    return pl.pallas_call(
        functools.partial(exchange_kernel, axis, size, spread_out),
        out_shape=jax.ShapeDtypeStruct((size,) + block, rows.dtype),
        in_specs=[pl.BlockSpec(memory_space=pltpu.VMEM)],
        out_specs=pl.BlockSpec(memory_space=pltpu.VMEM),
        scratch_shapes=[pltpu.SemaphoreType.DMA((size,)), pltpu.SemaphoreType.DMA((size,))],
        compiler_params=pltpu.CompilerParams(
            collective_id=number, has_side_effects=True, vmem_limit_bytes=VMEM_BYTES
        ),
        name=f"exchange{number}",
    )(rows)


class Place:
    def __init__(self, half):
        self.half = half
        self.role = lax.axis_index("dp")
        shard = lax.axis_index("fsdp")
        self.shard = shard
        self.line, self.side = shard // 2, shard % 2
        self.other_side = (self.side + 1) % 2
        self.roles = [flipped(self.role, step, 4) for step in range(4)]
        self.lines = [flipped(self.line, step, half) for step in range(half)]
        self.sides = [self.side, self.other_side]
        self.across = {"dp": self.roles[2]}
        self.beside = {"fsdp": self.line * 2 + self.other_side}
        self.core = {"dp": self.roles[1]}
        self.along = [{"fsdp": line * 2 + self.side} for line in self.lines]

    def greet(self, every_shard=False):
        if every_shard:
            shards = [{"fsdp": (self.shard + step) % (2 * self.half)} for step in range(1, 2 * self.half)]
        else:
            shards = [self.beside] + self.along[1:]
        greet([self.across, self.core] + shards)


class Message:
    def __init__(self, at, rows, out, spread_out, send_sem, recv_sem):
        self.at, self.rows, self.out, self.spread_out = at, rows, out, spread_out
        self.send_sem, self.recv_sem, self.sent = send_sem, recv_sem, []
        self.size = 2 * at.half

    def slot(self, shard):
        return self.out.at[shard] if self.spread_out else self.out.at[self.at.role, shard]

    def send(self, number, recv_number, source, target, peer):
        copy = remote(source, target, self.send_sem.at[number], self.recv_sem.at[recv_number], peer)
        copy.start()
        self.sent.append(copy)

    def got(self, number, target):
        remote(
            target, target, self.send_sem.at[number], self.recv_sem.at[number], self.at.core
        ).wait_recv()

    def begin(self):
        me = self.at.shard
        for step in range(1, self.size):
            peer = (me + step) % self.size
            source = self.rows.at[peer] if self.spread_out else self.rows
            self.send(step, self.size - step, source, self.slot(me), {"fsdp": peer})
        self.slot(me)[...] = self.rows[me] if self.spread_out else self.rows[...]

    def arrive(self):
        for step in range(1, self.size):
            self.got(step, self.slot((self.at.shard + step) % self.size))
        if not self.spread_out:
            own = self.out.at[self.at.role]
            self.send(self.size, self.size, own, own, self.at.across)
            self.send(self.size + 1, self.size + 1, own, own, self.at.core)

    def finish(self):
        if not self.spread_out:
            far = self.out.at[self.at.roles[2]]
            self.got(self.size, far)
            self.send(self.size + 2, self.size + 2, far, far, self.at.core)
            self.got(self.size + 1, self.out.at[self.at.roles[1]])
            self.got(self.size + 2, self.out.at[self.at.roles[3]])
        for copy in self.sent:
            copy.wait_send()


def message_scratch(half):
    return [pltpu.SemaphoreType.DMA((2 * half + 3,)), pltpu.SemaphoreType.DMA((2 * half + 3,))]

def cut(rows):
    first = (rows // 2 + 15) // 16 * 16
    return [(0, first), (first, rows - first)]


def block_view(ref, layout, role, line, side, rows):
    if layout == BY_SHARD:
        return ref.at[line, side, role, rows]
    if layout == BY_ROLE:
        return ref.at[role, line, side, rows]
    width = ref.shape[-1] // 4
    return ref.at[line, side, rows, pl.ds(pl.multiple_of(role * width, 128), width)]


def whole_shape(layout, half, rows, columns):
    lead = {BY_ROLE: (4, half, 2), BY_SHARD: (half, 2, 4), BY_COLUMN: (half, 2)}[layout]
    return lead + (rows, 4 * columns if layout == BY_COLUMN else columns)


class GatherUnit:
    def __init__(self, at, piece, out, layout, start, count, side_first, send_sem, recv_sem):
        self.at, self.piece, self.out, self.layout = at, piece, out, layout
        self.rows = pl.ds(start, count)
        self.side_first, self.send_sem, self.recv_sem = side_first, send_sem, recv_sem
        self.sent = []

    def view(self, role, line, side):
        return block_view(self.out, self.layout, role, line, side, self.rows)

    def send(self, number, make):
        self.sent.append((number, make))
        self.copy_of(number, make).start()

    def copy_of(self, number, make):
        source, target, peer = make()
        return remote(source, target, self.send_sem.at[number], self.recv_sem.at[number], peer)

    def got(self, number, target):
        remote(
            target, target, self.send_sem.at[number], self.recv_sem.at[number], self.at.core
        ).wait_recv()

    def numbers(self):
        half = self.at.half
        return half, 2 * half, 3 * half, 3 * half + 1

    def begin(self):
        at = self.at

        def own_to(peer):
            return lambda: (
                self.piece.at[self.rows], self.view(at.role, at.line, at.side), peer
            )

        beside, across, _, _ = self.numbers()
        for step in range(1, at.half):
            self.send(step, own_to(at.along[step]))
        self.send(beside, own_to(at.beside))
        self.send(across, own_to(at.across))

    def pass_on(self, number, peer, *where):
        self.send(number, lambda: (self.view(*where), self.view(*where), peer))

    def line_step(self, step):
        at = self.at
        where = (at.role, at.lines[step], at.side)
        self.got(step, self.view(*where))
        beside, across, _, _ = self.numbers()
        self.pass_on(beside + step, at.beside, *where)
        self.pass_on(across + step, at.across, *where)

    def second(self):
        at, every = self.at, slice(None)
        beside, across, second, core = self.numbers()
        for step in range(at.half):
            if self.side_first:
                self.got(beside + step, self.view(at.role, at.lines[step], at.other_side))
            else:
                self.got(across + step, self.view(at.roles[2], at.lines[step], at.side))
        if self.side_first:
            where = (at.role, every, at.other_side)
            self.pass_on(second, at.across, *where)
        else:
            where = (at.roles[2], every, at.side)
            self.pass_on(second, at.beside, *where)
        self.pass_on(core, at.core, at.role, every, at.side)
        self.pass_on(core + 1, at.core, *where)

    def third(self):
        at, every = self.at, slice(None)
        beside, across, second, core = self.numbers()
        for step in range(at.half):
            if self.side_first:
                self.got(across + step, self.view(at.roles[2], at.lines[step], at.side))
            else:
                self.got(beside + step, self.view(at.role, at.lines[step], at.other_side))
        if self.side_first:
            self.pass_on(core + 2, at.core, at.roles[2], every, at.side)
        else:
            self.pass_on(core + 2, at.core, at.role, every, at.other_side)
        last = (at.roles[2], every, at.other_side)
        self.got(second, self.view(*last))
        self.pass_on(core + 3, at.core, *last)

    def finish(self):
        at, every = self.at, slice(None)
        core = self.numbers()[3]
        near, far = at.roles[1], at.roles[3]
        views = [
            self.view(near, every, at.side),
            self.view(near, every, at.other_side),
            self.view(far, every, at.side),
            self.view(far, every, at.other_side),
        ]
        if not self.side_first:
            views[1], views[2] = views[2], views[1]
        for step, view in enumerate(views):
            self.got(core + step, view)
        for number, make in self.sent:
            self.copy_of(number, make).wait_send()


def gather_start(at, layouts, orders, pieces, outs, send_sem, recv_sem, local_sem):
    pairs, local = [], []
    for matrix, layout in enumerate(layouts):
        rows = pieces[matrix].shape[0]
        pairs.append(
            [
                GatherUnit(
                    at,
                    pieces[matrix],
                    outs[matrix],
                    layout,
                    start,
                    size,
                    orders[matrix][part],
                    send_sem.at[2 * matrix + part],
                    recv_sem.at[2 * matrix + part],
                )
                for part, (start, size) in enumerate(cut(rows))
            ]
        )

        def make(matrix=matrix, layout=layout, rows=rows):
            target = block_view(outs[matrix], layout, at.role, at.line, at.side, pl.ds(0, rows))
            return pltpu.make_async_copy(pieces[matrix], target, local_sem.at[matrix])

        make().start()
        local.append(make)
    for unit in pairs[0]:
        unit.begin()
    return pairs, local


def gather_actions(pairs, local):
    half, count = pairs[0][0].at.half, len(pairs)
    actions = []

    def each(pair, name, *given):
        def act():
            for unit in pair:
                getattr(unit, name)(*given)

        actions.append(act)

    def settle():
        for make in local:
            make().wait()

    actions.append(settle)
    for matrix in range(count + 1):
        if matrix < count:
            for step in range(1, half):
                each(pairs[matrix], "line_step", step)
            if matrix + 1 < count:
                each(pairs[matrix + 1], "begin")
            each(pairs[matrix], "second")
        if matrix:
            each(pairs[matrix - 1], "third")
    for pair in pairs:
        each(pair, "finish")
    return actions


def gather_scratch(count, half):
    return [
        pltpu.SemaphoreType.DMA((2 * count, 3 * half + 5)),
        pltpu.SemaphoreType.DMA((2 * count, 3 * half + 5)),
        pltpu.SemaphoreType.DMA((count,)),
    ]


def gather_kernel(half, layouts, orders, *refs):
    count = len(layouts)
    at = Place(half)
    rows, out = refs[count], refs[2 * count + 1]
    scratch = refs[2 * count + 2 :]
    message = Message(at, rows, out, True, *scratch[:2])
    at.greet(True)
    message.begin()
    pairs, local = gather_start(
        at, layouts, orders, refs[:count], refs[count + 1 : 2 * count + 1], *scratch[2:]
    )
    for action in gather_actions(pairs, local):
        action()
    message.arrive()
    message.finish()


def gather(pieces, layouts, orders, rows, number):
    half = lax.axis_size("fsdp") // 2
    count = len(pieces)
    vmem, hbm = pl.BlockSpec(memory_space=pltpu.VMEM), pl.BlockSpec(memory_space=pl.ANY)
    return pl.pallas_call(
        functools.partial(gather_kernel, half, layouts, orders),
        out_shape=[
            jax.ShapeDtypeStruct(whole_shape(layout, half, *piece.shape), piece.dtype)
            for piece, layout in zip(pieces, layouts)
        ]
        + [jax.ShapeDtypeStruct(rows.shape, rows.dtype)],
        in_specs=[vmem] * (count + 1),
        out_specs=[hbm] * count + [vmem],
        scratch_shapes=message_scratch(half) + gather_scratch(count, half),
        compiler_params=pltpu.CompilerParams(
            collective_id=number, has_side_effects=True, vmem_limit_bytes=VMEM_BYTES
        ),
        name=f"gather{number}",
    )(*pieces, rows)


def accumulate(target, source):
    rows = target.shape[0]
    chunk = 16 if rows % 16 == 0 else rows

    def step(index, carry):
        place_of = pl.ds(pl.multiple_of(index * chunk, chunk), chunk)
        target[place_of] = target[place_of] + source[place_of]
        return carry

    lax.fori_loop(0, rows // chunk, step, 0)


class ScatterUnit:
    def __init__(self, at, terms, out, layout, start, count, across_first, sems, buffers):
        self.at, self.terms, self.out, self.layout = at, terms, out, layout
        self.rows = pl.ds(start, count)
        self.across_first = across_first
        self.send_sem, self.recv_sem, self.stage_sem = sems
        self.core_buf, self.first_buf, self.last_buf, self.line_buf, self.stage = buffers
        self.sent = []
        half = at.half
        self.base_first, self.base_last = 4, 6
        self.base_line, self.base_share = 6 + half, 6 + 2 * half
        self.first_peer = at.across if across_first else at.beside
        self.last_peer = at.beside if across_first else at.across

    def own_terms(self, first, last, core):
        role_step, side_step = (first, last) if self.across_first else (last, first)
        role = self.at.roles[2 * role_step + core]
        return block_view(
            self.terms, self.layout, role, slice(None), self.at.sides[side_step], self.rows
        )

    def out_view(self, role):
        if self.layout == BY_COLUMN:
            width = self.out.shape[1] // 4
            return self.out.at[self.rows, pl.ds(pl.multiple_of(role * width, 128), width)]
        return self.out.at[role, self.rows]

    def send(self, number, make):
        self.sent.append((number, make))
        self.copy_of(number, make).start()

    def copy_of(self, number, make):
        source, target, peer = make()
        return remote(source, target, self.send_sem.at[number], self.recv_sem.at[number], peer)

    def got(self, number, target):
        remote(
            target, target, self.send_sem.at[number], self.recv_sem.at[number], self.at.core
        ).wait_recv()

    def add_lines(self, target, source):
        def step(line, carry):
            accumulate(target.at[line], source.at[line])
            return carry

        lax.fori_loop(0, self.at.half, step, 0)

    def begin(self):
        for first in (1, 0):
            for last in (1, 0):
                self.send(
                    2 * first + last,
                    lambda first=first, last=last: (
                        self.own_terms(first, last, 1), self.core_buf.at[first, last], self.at.core
                    ),
                )

    def paired(self, first, last):
        buffer = self.core_buf.at[first, last]
        load = pltpu.make_async_copy(self.own_terms(first, last, 0), self.stage, self.stage_sem)
        load.start()
        self.got(2 * first + last, buffer)
        load.wait()
        self.add_lines(buffer, self.stage)
        if first:
            self.send(
                self.base_first + last,
                lambda: (
                    self.core_buf.at[first, last], self.first_buf.at[last], self.first_peer
                ),
            )

    def joined(self, last):
        buffer = self.first_buf.at[last]
        self.got(self.base_first + last, buffer)
        self.add_lines(buffer, self.core_buf.at[0, last])
        if last:
            for step in list(range(self.at.half - 1, 0, -1)) + [0]:
                self.send(
                    self.base_last + step,
                    lambda line=self.at.lines[step]: (
                        self.first_buf.at[last, line], self.last_buf.at[line], self.last_peer
                    ),
                )

    def lined(self, step):
        line = self.at.lines[step]
        block = self.last_buf.at[line]
        self.got(self.base_last + step, block)
        accumulate(block, self.first_buf.at[0, line])
        if step:
            self.send(
                self.base_line + step,
                lambda: (self.last_buf.at[line], self.line_buf.at[step], self.at.along[step]),
            )

    def end(self):
        at = self.at
        own = self.last_buf.at[at.line]
        for step in range(1, at.half):
            self.got(self.base_line + step, self.line_buf.at[step])
            accumulate(own, self.line_buf.at[step])
        target = self.out_view(at.role)
        target[...] = own[...]
        for step in (2, 1):
            self.send(
                self.base_share + step,
                lambda step=step: (
                    self.last_buf.at[at.line], self.out_view(at.role), {"dp": at.roles[step]}
                ),
            )

    def finish(self):
        roles = self.at.roles
        self.got(self.base_share + 2, self.out_view(roles[2]))
        self.send(
            self.base_share + 3,
            lambda: (self.out_view(roles[2]), self.out_view(roles[2]), self.at.core),
        )

    def close(self):
        for step in (1, 3):
            self.got(self.base_share + step, self.out_view(self.at.roles[step]))
        for number, make in self.sent:
            self.copy_of(number, make).wait_send()


def scatter_actions(pairs):
    half = pairs[0][0].at.half
    steps = list(range(half - 1, 0, -1)) + [0]
    stages = [
        [("paired", 1, 1), ("paired", 1, 0)],
        [("paired", 0, 1), ("paired", 0, 0)],
        [("joined", 1), ("joined", 0)],
        [("lined", step) for step in steps],
        [("end",)],
    ]
    actions = []

    def each(pair, name, *given):
        def act():
            for unit in pair:
                getattr(unit, name)(*given)

        actions.append(act)

    for turn in range(len(stages) + len(pairs) - 1):
        for index, pair in reversed(list(enumerate(pairs))):
            if 0 <= turn - index < len(stages):
                for call in stages[turn - index]:
                    each(pair, *call)
    for name in ("finish", "close"):
        for pair in pairs:
            each(pair, name)
    return actions


def scatter_start(at, layouts, orders, terms, outs, scratch):
    sems, buffers = scratch[:3], scratch[3:]
    pairs = []
    for matrix, layout in enumerate(layouts):
        pair = []
        for part, (start, size) in enumerate(cut(terms[matrix].shape[-2])):
            unit = 2 * matrix + part
            pair.append(
                ScatterUnit(
                    at,
                    terms[matrix],
                    outs[matrix],
                    layout,
                    start,
                    size,
                    orders[matrix][part],
                    [sem.at[unit] for sem in sems],
                    buffers[5 * unit : 5 * unit + 5],
                )
            )
        pairs.append(pair)
    for pair in pairs:
        for unit in pair:
            unit.begin()
    return pairs


def scatter_scratch(count, half, rows, columns):
    scratch = [pltpu.SemaphoreType.DMA((2 * count, 2 * half + 10))] * 2
    scratch += [pltpu.SemaphoreType.DMA((2 * count,))]
    for _ in range(count):
        for _, size in cut(rows):
            for lead in ((2, 2, half), (2, half), (half,), (half,), (half,)):
                scratch.append(pltpu.VMEM(lead + (size, columns), jnp.bfloat16))
    return scratch


def scatter_outs(layouts, rows, columns):
    return [
        jax.ShapeDtypeStruct(
            (rows, 4 * columns) if layout == BY_COLUMN else (4, rows, columns), jnp.bfloat16
        )
        for layout in layouts
    ]


def roles_kernel(half, order, *refs):
    ins, rows, out, rows_out = refs[:6], refs[6], refs[7], refs[8]
    left, right, terms, local_sem = refs[9:13]
    scratch = refs[13:]
    at = Place(half)
    local = []
    for index in range(6):
        target = left.at[index] if index < 2 else right.at[index - 2]
        copy = pltpu.make_async_copy(ins[index], target, local_sem.at[index])
        copy.start()
        local.append(copy)
    message = Message(at, rows, rows_out, False, *scratch[:2])
    at.greet(True)
    message.begin()
    for copy in local:
        copy.wait()
    shard_rows, columns = terms.shape[3:]
    chunks = 3
    width = columns // chunks

    def product_of(role, chunk):
        window = pl.ds(pl.multiple_of(chunk * width, 128), width)
        result = dot_tn(left[role // 3], right[role, :, window]).astype(jnp.bfloat16)
        for shard in range(2 * half):
            terms[role, shard // 2, shard % 2, :, window] = result[
                shard * shard_rows : (shard + 1) * shard_rows
            ]

    def two_roles(first, second):
        def step(index, carry):
            role = jnp.where(index < chunks, first, second)
            product_of(role, index % chunks)
            return carry

        lax.fori_loop(0, 2 * chunks, step, 0)

    two_roles(at.roles[3], at.roles[1])
    pairs = scatter_start(at, (BY_ROLE,), (order,), [terms], [out], scratch[2:])
    two_roles(at.roles[2], at.roles[0])
    actions = scatter_actions(pairs)
    for action in actions[:5]:
        action()
    message.arrive()
    for action in actions[5:]:
        action()
    message.finish()


def scatter_products(lefts, rights, order, message, number):
    half = lax.axis_size("fsdp") // 2
    model_width = lefts[0].shape[1]
    rows, columns = model_width // (2 * half), rights[0].shape[1]
    vmem, hbm = pl.BlockSpec(memory_space=pltpu.VMEM), pl.BlockSpec(memory_space=pl.ANY)
    return pl.pallas_call(
        functools.partial(roles_kernel, half, order),
        out_shape=scatter_outs((BY_ROLE,), rows, columns)
        + [jax.ShapeDtypeStruct((4, 2 * half) + message.shape, message.dtype)],
        in_specs=[hbm] * 6 + [vmem],
        out_specs=[vmem] * 2,
        scratch_shapes=[
            pltpu.VMEM((2,) + lefts[0].shape, jnp.bfloat16),
            pltpu.VMEM((4,) + rights[0].shape, jnp.bfloat16),
            pltpu.VMEM((4, half, 2, rows, columns), jnp.bfloat16),
            pltpu.SemaphoreType.DMA((6,)),
        ]
        + message_scratch(half)
        + scatter_scratch(1, half, rows, columns),
        compiler_params=pltpu.CompilerParams(
            collective_id=number, has_side_effects=True, vmem_limit_bytes=VMEM_BYTES
        ),
        name=f"scatter{number}",
    )(*lefts, *rights, message)


def head_window(head, width, columns):
    tile = jnp.minimum(head * width // 128, columns // 128 - 2)
    lane = lax.broadcasted_iota(jnp.int32, (1, 256), 1) + tile * 128
    inside = jnp.logical_and(lane >= head * width, lane < (head + 1) * width)
    return pl.ds(pl.multiple_of(tile * 128, 128), 256), jnp.where(inside, 1.0, 0.0)


def dot_nt(left, right):
    return lax.dot_general(
        left, right, (((1,), (1,)), ((), ())), preferred_element_type=jnp.float32
    )


def dot_tn(left, right):
    return lax.dot_general(
        left, right, (((0,), (0,)), ((), ())), preferred_element_type=jnp.float32
    )


def attend_head(head, width, q_ref, k_ref, v_ref, o_ref, log_ref):
    scaling = width ** (-0.5)
    window, inside = head_window(head, width, q_ref.shape[1])
    queries = q_ref[:, window] * inside.astype(jnp.bfloat16)
    scores = dot_nt(queries, k_ref[:, window]) * scaling
    row_max = jnp.max(scores, axis=-1, keepdims=True)
    exponent = jnp.exp(scores - row_max)
    row_total = jnp.sum(exponent, axis=-1, keepdims=True)
    weights = (exponent * (1.0 / row_total)).astype(jnp.bfloat16)
    result = jnp.dot(weights, v_ref[:, window], preferred_element_type=jnp.float32)
    o_ref[:, window] += result * inside
    lane = lax.broadcasted_iota(jnp.int32, (1, log_ref.shape[1]), 1)
    log_ref[...] = jnp.where(lane == head, row_max + jnp.log(row_total), log_ref[...])


def attend_back_head(head, width, q_ref, k_ref, v_ref, g_ref, log_ref, dq_ref, dk_ref, dv_ref):
    scaling = width ** (-0.5)
    window, inside = head_window(head, width, q_ref.shape[1])
    inside_low = inside.astype(jnp.bfloat16)
    queries, grads = q_ref[:, window] * inside_low, g_ref[:, window] * inside_low
    key_rows = k_ref[:, window]
    lane = lax.broadcasted_iota(jnp.int32, (1, log_ref.shape[1]), 1)
    log_total = jnp.sum(jnp.where(lane == head, log_ref[...], 0.0), axis=-1, keepdims=True)
    weights = jnp.exp(dot_nt(queries, key_rows) * scaling - log_total)
    dv_ref[:, window] += dot_tn(weights.astype(jnp.bfloat16), grads)
    d_weights = dot_nt(grads, v_ref[:, window])
    inner = jnp.sum(weights * d_weights, axis=-1, keepdims=True)
    d_scores = (weights * (d_weights - inner)).astype(jnp.bfloat16)
    dq_ref[:, window] += jnp.dot(d_scores, key_rows, preferred_element_type=jnp.float32) * (
        inside * scaling
    )
    dk_ref[:, window] += dot_tn(d_scores, queries) * scaling


def run_heads(head_count, attend_one, actions):
    spread_over = {}
    for index, action in enumerate(actions):
        spread_over.setdefault(index * head_count // len(actions), []).append(action)

    def step(head, carry):
        attend_one(head)
        for when, group in spread_over.items():

            @pl.when(head == when)
            def _(group=group):
                for action in group:
                    action()

        return carry

    lax.fori_loop(0, head_count, step, 0)


def forward_kernel(half, layouts, orders, heads, *refs):
    count = len(layouts)
    q_ref, k_ref, v_ref = refs[:3]
    pieces = refs[3 : 3 + count]
    o_ref, log_ref, keys, values = refs[3 + count : 7 + count]
    outs = refs[7 + count : 7 + 2 * count]
    send_sem, recv_sem = refs[7 + 2 * count : 9 + 2 * count]
    at = Place(half)
    width = q_ref.shape[1] // heads
    rows = keys.shape[0] // 4
    short = q_ref.shape[0] - rows
    own = pl.ds(short, rows)
    beside, along = at.beside, at.along[1]

    def quarter(buffer, index):
        return buffer.at[pl.ds(index * rows, rows)]

    at.greet()
    sent = []

    def send(number, source, target, peer):
        copy = remote(source, target, send_sem.at[number], recv_sem.at[number], peer)
        copy.start()
        sent.append(copy)

    def got(number, target):
        remote(target, target, send_sem.at[number], recv_sem.at[number], along).wait_recv()

    send(0, k_ref.at[own], quarter(keys, 1), beside)
    send(1, v_ref.at[own], quarter(values, 2), along)
    send(2, v_ref.at[own], quarter(values, 1), beside)
    send(3, k_ref.at[own], quarter(keys, 2), along)
    pairs, local = gather_start(
        at, layouts, orders, pieces, outs, *refs[9 + 2 * count :]
    )
    quarter(keys, 0)[...] = k_ref[own]
    quarter(values, 0)[...] = v_ref[own]
    o_ref[...] = jnp.zeros_like(o_ref)
    log_ref[...] = jnp.zeros_like(log_ref)

    def pass_on():
        got(0, quarter(keys, 1))
        send(4, quarter(keys, 1), quarter(keys, 3), along)
        got(1, quarter(values, 2))
        send(5, quarter(values, 2), quarter(values, 3), beside)

    actions = gather_actions(pairs, local)
    early = 1 + (half - 1)
    first = pl.ds(0, short)
    run_heads(
        heads,
        lambda head: attend_head(
            head,
            width,
            q_ref.at[first],
            k_ref.at[first],
            v_ref.at[first],
            o_ref.at[first],
            log_ref.at[first],
        ),
        [lambda: None, lambda: None, lambda: None] + actions[:early],
    )
    pass_on()
    for action in actions[early : early + 2]:
        action()
    got(2, quarter(values, 1))
    got(3, quarter(keys, 2))
    got(4, quarter(keys, 3))
    got(5, quarter(values, 3))
    run_heads(
        heads,
        lambda head: attend_head(
            head, width, q_ref.at[own], keys, values, o_ref.at[own], log_ref.at[own]
        ),
        actions[early + 2 : -count],
    )
    for action in actions[-count:]:
        action()
    for copy in sent:
        copy.wait_send()


def attention_forward(q_rows, k_rows, v_rows, pieces, layouts, orders, heads, rows, number):
    half = lax.axis_size("fsdp") // 2
    count = len(pieces)
    vmem, hbm = pl.BlockSpec(memory_space=pltpu.VMEM), pl.BlockSpec(memory_space=pl.ANY)
    total, columns = q_rows.shape
    outs = [
        jax.ShapeDtypeStruct((total, columns), jnp.float32),
        jax.ShapeDtypeStruct((total, 128), jnp.float32),
        jax.ShapeDtypeStruct((4 * rows, columns), jnp.bfloat16),
        jax.ShapeDtypeStruct((4 * rows, columns), jnp.bfloat16),
    ] + [
        jax.ShapeDtypeStruct(whole_shape(layout, half, *piece.shape), piece.dtype)
        for piece, layout in zip(pieces, layouts)
    ]
    return pl.pallas_call(
        functools.partial(forward_kernel, half, layouts, orders, heads),
        out_shape=outs,
        in_specs=[vmem] * (3 + count),
        out_specs=[vmem] * 4 + [hbm] * count,
        scratch_shapes=[pltpu.SemaphoreType.DMA((6,)), pltpu.SemaphoreType.DMA((6,))]
        + gather_scratch(count, half),
        compiler_params=pltpu.CompilerParams(
            collective_id=number, has_side_effects=True, vmem_limit_bytes=VMEM_BYTES
        ),
        name=f"attention{number}",
    )(q_rows, k_rows, v_rows, *pieces)


def backward_kernel(half, layouts, orders, heads, *refs):
    count = len(layouts)
    q_ref, k_ref, v_ref, g_ref, log_ref, keys, values = refs[:7]
    terms = refs[7 : 7 + count]
    dq_out, dk_out, dv_out = refs[7 + count : 10 + count]
    outs = refs[10 + count : 10 + 2 * count]
    rest = refs[10 + 2 * count :]
    dq, dk, dv, wide, wide_got, slim, slim_got, send_sem, recv_sem = rest[:9]
    at = Place(half)
    width = q_ref.shape[1] // heads
    rows = keys.shape[0] // 4
    short = q_ref.shape[0] - rows
    own, first = pl.ds(short, rows), pl.ds(0, short)
    beside, along = at.beside, at.along[1]
    at.greet()
    pairs = scatter_start(at, layouts, orders, terms, outs, rest[9:])
    actions = scatter_actions(pairs)
    dq[...] = jnp.zeros_like(dq)
    dk[...] = jnp.zeros_like(dk)
    dv[...] = jnp.zeros_like(dv)
    sent = []

    def send(number, source, target, peer):
        copy = remote(source, target, send_sem.at[number], recv_sem.at[number], peer)
        copy.start()
        sent.append(copy)

    def got(number, target):
        remote(target, target, send_sem.at[number], recv_sem.at[number], along).wait_recv()

    def quarter(index):
        return pl.ds(index * rows, rows)

    split = 2 * len(actions) // 5
    run_heads(
        heads,
        lambda head: attend_back_head(
            head,
            width,
            q_ref.at[own],
            keys,
            values,
            g_ref.at[own],
            log_ref.at[own],
            dq.at[own],
            dk,
            dv,
        ),
        actions[:split],
    )
    for part, (source, index) in enumerate([(dk, 2), (dk, 3), (dv, 1), (dv, 3)]):
        wide[part] = source[quarter(index)].astype(jnp.bfloat16)
    send(0, wide.at[pl.ds(0, 2)], wide_got.at[pl.ds(0, 2)], along)
    send(1, wide.at[pl.ds(2, 2)], wide_got.at[pl.ds(2, 2)], beside)
    short_dk, short_dv = dk.at[pl.ds(2 * rows, short)], dv.at[pl.ds(rows, short)]
    short_dk[...] = jnp.zeros_like(short_dk)
    short_dv[...] = jnp.zeros_like(short_dv)
    run_heads(
        heads,
        lambda head: attend_back_head(
            head,
            width,
            q_ref.at[first],
            k_ref.at[first],
            v_ref.at[first],
            g_ref.at[first],
            log_ref.at[first],
            dq.at[first],
            short_dk,
            short_dv,
        ),
        actions[split : split + 2],
    )
    dq_out[...] = dq[...].astype(jnp.bfloat16)
    dk_out[first] = short_dk[...].astype(jnp.bfloat16)
    dv_out[first] = short_dv[...].astype(jnp.bfloat16)
    got(0, wide_got.at[pl.ds(0, 2)])
    slim[0] = (dk[quarter(1)] + wide_got[1].astype(jnp.float32)).astype(jnp.bfloat16)
    send(2, slim.at[0], slim_got.at[0], beside)
    got(1, wide_got.at[pl.ds(2, 2)])
    slim[1] = (dv[quarter(2)] + wide_got[3].astype(jnp.float32)).astype(jnp.bfloat16)
    send(3, slim.at[1], slim_got.at[1], along)
    for action in actions[split + 2 : -2 * count]:
        action()
    got(2, slim_got.at[0])
    total = dk[quarter(0)] + wide_got[0].astype(jnp.float32) + slim_got[0].astype(jnp.float32)
    dk_out[own] = total.astype(jnp.bfloat16)
    got(3, slim_got.at[1])
    total = dv[quarter(0)] + wide_got[2].astype(jnp.float32) + slim_got[1].astype(jnp.float32)
    dv_out[own] = total.astype(jnp.bfloat16)
    for action in actions[-2 * count :]:
        action()
    for copy in sent:
        copy.wait_send()


def attention_backward(
    rows_in, keys, values, gradients, layouts, orders, heads, rows, columns, number
):
    half = lax.axis_size("fsdp") // 2
    count = len(gradients)
    vmem, hbm = pl.BlockSpec(memory_space=pltpu.VMEM), pl.BlockSpec(memory_space=pl.ANY)
    total, model_width = rows_in[0].shape
    quarter_rows = keys.shape[0] // 4
    low_rows = jax.ShapeDtypeStruct((total, model_width), jnp.bfloat16)
    return pl.pallas_call(
        functools.partial(backward_kernel, half, layouts, orders, heads),
        out_shape=[low_rows] * 3 + scatter_outs(layouts, rows, columns),
        in_specs=[vmem] * 7 + [hbm] * count,
        out_specs=[vmem] * (3 + count),
        scratch_shapes=[
            pltpu.VMEM((total, model_width), jnp.float32),
            pltpu.VMEM((4 * quarter_rows, model_width), jnp.float32),
            pltpu.VMEM((4 * quarter_rows, model_width), jnp.float32),
            pltpu.VMEM((4, quarter_rows, model_width), jnp.bfloat16),
            pltpu.VMEM((4, quarter_rows, model_width), jnp.bfloat16),
            pltpu.VMEM((2, quarter_rows, model_width), jnp.bfloat16),
            pltpu.VMEM((2, quarter_rows, model_width), jnp.bfloat16),
            pltpu.SemaphoreType.DMA((4,)),
            pltpu.SemaphoreType.DMA((4,)),
        ]
        + scatter_scratch(count, half, rows, columns),
        compiler_params=pltpu.CompilerParams(
            collective_id=number, has_side_effects=True, vmem_limit_bytes=VMEM_BYTES
        ),
        name=f"attention{number}",
    )(*rows_in, keys, values, *gradients)


def product(left, right):
    return jnp.dot(left, right, preferred_element_type=jnp.float32)


def product_tn(left, right):
    return lax.dot_general(
        left, right, (((0,), (0,)), ((), ())), preferred_element_type=jnp.float32
    )


def product_nt(left, right):
    return lax.dot_general(
        left, right, (((1,), (1,)), ((), ())), preferred_element_type=jnp.float32
    )


def spread(per_slot, short_count, len_short, quarter_rows):
    width = per_slot.shape[1]
    short_part = jnp.broadcast_to(
        per_slot[:short_count, None, :], (short_count, len_short, width)
    ).reshape(short_count * len_short, width)
    long_part = jnp.broadcast_to(per_slot[short_count:], (quarter_rows, width))
    return jnp.concatenate([short_part, long_part], 0)


def slot_sum(values, short_count, len_short):
    short_rows = short_count * len_short
    short_part = jnp.sum(
        values[:short_rows].reshape((short_count, len_short) + values.shape[1:]), axis=1
    )
    long_part = jnp.sum(values[short_rows:], axis=0, keepdims=True)
    return jnp.concatenate([short_part, long_part], 0)


def norm_parts(values):
    average = jnp.mean(values, axis=-1, keepdims=True)
    centred = values - average
    variance = jnp.mean(centred * centred, axis=-1, keepdims=True)
    inverse = lax.rsqrt(variance + epsilon)
    return (centred * inverse, inverse)


def norm_back(gradient, normed, inverse):
    return inverse * (
        gradient
        - jnp.mean(gradient, axis=-1, keepdims=True)
        - normed * jnp.mean(gradient * normed, axis=-1, keepdims=True)
    )


def silu_grad(values):
    sigmoid_value = jax.nn.sigmoid(values)
    return sigmoid_value * (1.0 + values * (1.0 - sigmoid_value))


def gelu_tanh(values):
    return jax.nn.gelu(values, approximate=True)


def per_device(
    x_short,
    x_long,
    short_cond,
    long_cond,
    short_heads,
    long_heads,
    short_groups,
    long_groups,
    short_keep,
    long_keep,
    w_ada,
    b_ada,
    w_head_router,
    w_group_router,
    w_qkv,
    w_proj,
    b_proj,
    w_fc1,
    b_fc1,
    w_fc2,
    b_fc2,
    g_short,
    g_long,
):
    short_count, len_short, model_width = x_short.shape
    quarter_rows = x_long.shape[0]
    head_count = w_head_router.shape[1]
    head_width = model_width // head_count
    group_count = w_group_router.shape[1]
    slot_count = short_count + 1
    short_rows = short_count * len_short
    row_count = short_rows + quarter_rows
    fsdp_index = lax.axis_index("fsdp")
    fsdp_count = lax.axis_size("fsdp")
    role = lax.axis_index("dp")
    group_row = fsdp_index // SPLIT
    half = fsdp_count // 2
    shard_rows = w_qkv.shape[0]
    unit_rows = w_fc2.shape[0] // 4
    short_act = low(jax.nn.silu(short_cond))
    long_act = low(jax.nn.silu(long_cond))
    message = exchange(packed([short_act, b_proj, b_fc1, b_fc2], 16), "fsdp", False, 0)
    act_rows, proj_bias, fc1_bias, fc2_bias = unpacked(
        message, [(model_width,), b_proj.shape, b_fc1.shape, b_fc2.shape]
    )
    proj_bias, fc1_bias, fc2_bias = (
        bias.reshape(-1).astype(jnp.float32) for bias in (proj_bias, fc1_bias, fc2_bias)
    )
    item_act = jnp.concatenate([act_rows, long_act], 0)
    own_long_act = lax.dynamic_slice_in_dim(long_act, group_row, 1, 0)
    item_columns = lax.dynamic_slice_in_dim(item_act, fsdp_index * shard_rows, shard_rows, 1)
    bias_row = lax.dynamic_update_slice_in_dim(
        jnp.zeros((fsdp_count * b_ada.shape[0],), jnp.float32),
        b_ada.astype(jnp.float32),
        fsdp_index * b_ada.shape[0],
        0,
    )
    partial = jnp.concatenate(
        [
            product(item_columns, w_ada) + bias_row,
            product(item_columns, w_head_router),
            product(item_columns, w_group_router),
        ],
        1,
    )
    width = partial.shape[1]
    for_device = jnp.stack(
        [partial[:fsdp_count], jnp.repeat(partial[fsdp_count:], SPLIT, axis=0)], 1
    ).reshape(fsdp_count, -1)
    for_device = low(jnp.pad(for_device, ((0, 0), (0, -for_device.shape[1] % 2048))))
    mixed_shard = jnp.concatenate([w_qkv, w_proj], 1)
    attention_piece = lax.dynamic_slice_in_dim(mixed_shard, role * model_width, model_width, 1)
    attention_full, shares = gather(
        [attention_piece],
        (BY_ROLE,),
        ((True, False),),
        for_device.reshape(fsdp_count, -1, 128),
        2,
    )
    conditioned = unpacked(jnp.sum(shares.astype(jnp.float32), axis=0), [(2, width)])[0]
    attention_full = attention_full.reshape(4, -1, model_width)
    mod_width = 6 * model_width
    modulation = conditioned[:, :mod_width]
    head_sigmoid = jax.nn.sigmoid(conditioned[:, mod_width : mod_width + head_count])
    group_sigmoid = jax.nn.sigmoid(conditioned[:, mod_width + head_count :])
    head_mask = jnp.concatenate(
        [short_heads, lax.dynamic_slice_in_dim(long_heads, group_row, 1, 0)], 0
    ).astype(jnp.float32)
    group_mask = jnp.concatenate(
        [short_groups, lax.dynamic_slice_in_dim(long_groups, group_row, 1, 0)], 0
    ).astype(jnp.float32)
    head_gate = head_mask * 2.0 * head_sigmoid
    group_gate = group_mask * 2.0 * group_sigmoid
    shift1, scale1, gate1, shift2, scale2, gate2 = jnp.split(
        spread(modulation, short_count, len_short, quarter_rows), 6, axis=1
    )
    x_rows = jnp.concatenate([x_short.reshape(short_rows, model_width), x_long], 0).astype(
        jnp.float32
    )
    keep_rows = jnp.concatenate([short_keep.reshape(short_rows), long_keep], 0).astype(jnp.float32)[
        :, None
    ]
    normed1, inverse1 = norm_parts(x_rows)
    hidden1 = low(normed1 * (1.0 + scale1) + shift1)
    q_rows, k_rows, v_rows = (low(product(hidden1, attention_full[part])) for part in range(3))

    fc1_piece = lax.dynamic_slice_in_dim(w_fc1, role * model_width, model_width, 1)
    fc2_piece = lax.dynamic_slice_in_dim(w_fc2, role * unit_rows, unit_rows, 0)
    head_rows, log_rows, keys, values, fc1_full, fc2_full = attention_forward(
        q_rows,
        k_rows,
        v_rows,
        [fc1_piece, fc2_piece],
        (BY_COLUMN, BY_SHARD),
        ((True, False), (True, True)),
        head_count,
        quarter_rows,
        3,
    )
    head_rows = head_rows.reshape(row_count, head_count, head_width)
    head_gate_rows = spread(head_gate, short_count, len_short, quarter_rows)[:, :, None]
    attention = low((head_rows * head_gate_rows).reshape(row_count, model_width))
    projected = product(attention, attention_full[3]) + proj_bias
    mixed = x_rows + gate1 * projected
    fc1_full = fc1_full.reshape(model_width, -1)
    fc2_full = fc2_full.reshape(-1, model_width)
    normed2, inverse2 = norm_parts(mixed)
    hidden2 = low(normed2 * (1.0 + scale2) + shift2)
    channel_gate = spread(
        jnp.repeat(group_gate, CHAN, axis=1), short_count, len_short, quarter_rows
    )
    up_rows = product(hidden2, fc1_full) + fc1_bias
    gelu_value, gelu_pull = jax.vjp(gelu_tanh, up_rows)
    activated = low(gelu_value * channel_gate)
    down_rows = product(activated, fc2_full) + fc2_bias
    out_rows = mixed + gate2 * keep_rows * down_rows
    y_short = low(out_rows[:short_rows].reshape(x_short.shape))
    y_long = low(out_rows[short_rows:])
    gradient = jnp.concatenate([g_short.reshape(short_rows, model_width), g_long], 0).astype(
        jnp.float32
    )
    d_down = low(gradient * gate2 * keep_rows)
    slot_gate2 = slot_sum(gradient * keep_rows * down_rows, short_count, len_short)
    grad_fc2 = low(product_tn(activated, d_down)).reshape(half, 2, 4, unit_rows, model_width)
    d_activated = product_nt(d_down, fc2_full)
    d_channel = slot_sum(d_activated * gelu_value, short_count, len_short)
    d_group = jnp.sum(d_channel.reshape(slot_count, group_count, CHAN), axis=-1)
    d_up = low(gelu_pull(d_activated * channel_gate)[0])
    grad_fc1 = low(product_tn(hidden2, d_up)).reshape(half, 2, shard_rows, -1)
    d_hidden2 = product_nt(d_up, fc1_full)

    slot_shift2 = slot_sum(d_hidden2, short_count, len_short)
    slot_scale2 = slot_sum(d_hidden2 * normed2, short_count, len_short)
    d_mixed = gradient + norm_back(d_hidden2 * (1.0 + scale2), normed2, inverse2)
    d_projected = low(d_mixed * gate1)
    slot_gate1 = slot_sum(d_mixed * projected, short_count, len_short)
    d_attention = product_nt(d_projected, attention_full[3]).reshape(
        row_count, head_count, head_width
    )
    d_head = slot_sum(jnp.sum(d_attention * head_rows, axis=-1), short_count, len_short)
    d_heads = low(d_attention * head_gate_rows)
    bias_grad = jnp.concatenate(
        [jnp.sum(part, axis=0, dtype=jnp.float32) for part in (d_projected, d_up, d_down)]
    )
    dq_rows, dk_rows, dv_rows, fc1_sum, fc2_sum = attention_backward(
        [q_rows, k_rows, v_rows, d_heads.reshape(row_count, model_width), log_rows],
        keys,
        values,
        [grad_fc1, grad_fc2],
        (BY_COLUMN, BY_SHARD),
        ((True, False), (True, True)),
        head_count,
        shard_rows,
        model_width,
        4,
    )
    g_w_fc1 = fc1_sum.astype(jnp.float32)
    g_w_fc2 = fc2_sum.reshape(-1, model_width).astype(jnp.float32)
    d_hidden1 = (
        product_nt(dq_rows, attention_full[0])
        + product_nt(dk_rows, attention_full[1])
        + product_nt(dv_rows, attention_full[2])
    )
    slot_shift1 = slot_sum(d_hidden1, short_count, len_short)
    slot_scale1 = slot_sum(d_hidden1 * normed1, short_count, len_short)
    d_rows = d_mixed + norm_back(d_hidden1 * (1.0 + scale1), normed1, inverse1)
    dx_short = low(d_rows[:short_rows].reshape(x_short.shape))
    dx_long = low(d_rows[short_rows:])
    d_head_logit = d_head * head_mask * 2.0 * head_sigmoid * (1.0 - head_sigmoid)
    d_group_logit = d_group * group_mask * 2.0 * group_sigmoid * (1.0 - group_sigmoid)
    d_conditioned = jnp.concatenate(
        [
            slot_shift1,
            slot_scale1,
            slot_gate1,
            slot_shift2,
            slot_scale2,
            slot_gate2,
            d_head_logit,
            d_group_logit,
        ],
        1,
    )
    message = packed([low(d_conditioned), low(bias_grad), short_act, own_long_act], 16)
    attention_sum, all_rows = scatter_products(
        [hidden1, attention],
        [dq_rows, dk_rows, dv_rows, d_projected],
        (False, False),
        message,
        5,
    )
    g_w_qkv = attention_sum[:3].transpose(1, 0, 2).reshape(shard_rows, -1).astype(jnp.float32)
    g_w_proj = attention_sum[3].astype(jnp.float32)
    all_rows, bias_rows, all_short, all_long = unpacked(
        all_rows, [(2, width), bias_grad.shape, (model_width,), (model_width,)]
    )
    long_sum = jnp.sum(
        all_rows[:, :, 1].astype(jnp.float32).reshape(4, -1, SPLIT, width), axis=2
    )
    factors = jnp.concatenate([all_rows[:, :, 0], low(long_sum)], 1)
    d_items = lax.dynamic_index_in_dim(factors, role, 0, keepdims=False)
    d_silu = (
        product_nt(d_items[:, :mod_width], w_ada)
        + product_nt(d_items[:, mod_width : mod_width + head_count], w_head_router)
        + product_nt(d_items[:, mod_width + head_count :], w_group_router)
    )
    d_silu = unpacked(exchange(packed([d_silu], 8), "fsdp", False, 7), [d_silu.shape])[0]
    d_silu = d_silu.transpose(1, 0, 2).reshape(-1, model_width)
    d_short_cond = lax.dynamic_slice_in_dim(d_silu, fsdp_index, 1, 0) * silu_grad(short_cond)
    d_long_cond = d_silu[fsdp_count:] * silu_grad(long_cond)
    act_factors = jnp.concatenate([all_short, all_long[:, ::SPLIT]], 1)
    act_factors = lax.dynamic_slice_in_dim(
        act_factors, fsdp_index * shard_rows, shard_rows, 2
    ).reshape(-1, shard_rows)
    factors = factors.reshape(-1, width)
    g_w_ada = product_tn(act_factors, factors[:, :mod_width])
    g_w_head_router = product_tn(act_factors, factors[:, mod_width : mod_width + head_count])
    g_w_group_router = product_tn(act_factors, factors[:, mod_width + head_count :])
    g_b_ada = lax.dynamic_slice_in_dim(
        jnp.sum(factors[:, :mod_width].astype(jnp.float32), axis=0),
        fsdp_index * b_ada.shape[0],
        b_ada.shape[0],
        0,
    )
    bias_sum = jnp.sum(bias_rows.astype(jnp.float32), axis=(0, 1))

    def own_bias(start, count):
        return lax.dynamic_slice_in_dim(bias_sum, start + fsdp_index * count, count, 0)

    g_b_proj = own_bias(0, shard_rows)
    g_b_fc1 = own_bias(model_width, 4 * shard_rows)
    g_b_fc2 = own_bias(5 * model_width, shard_rows)
    return (
        y_short,
        y_long,
        dx_short,
        dx_long,
        d_short_cond,
        d_long_cond,
        g_w_ada,
        g_b_ada,
        g_w_head_router,
        g_w_group_router,
        g_w_qkv,
        g_w_proj,
        g_b_proj,
        g_w_fc1,
        g_b_fc1,
        g_w_fc2,
        g_b_fc2,
    )


def solution(mesh):
    return jax.shard_map(
        per_device,
        mesh=mesh,
        in_specs=(
            P(("dp", "fsdp"), None, None),
            P(("dp", "fsdp"), None),
            P(("dp", "fsdp"), None),
            P("dp", None),
            P(("dp", "fsdp"), None),
            P("dp", None),
            P(("dp", "fsdp"), None),
            P("dp", None),
            P(("dp", "fsdp"), None),
            P(("dp", "fsdp")),
            P("fsdp", None),
            P("fsdp"),
            P("fsdp", None),
            P("fsdp", None),
            P("fsdp", None),
            P("fsdp", None),
            P("fsdp"),
            P("fsdp", None),
            P("fsdp"),
            P("fsdp", None),
            P("fsdp"),
            P(("dp", "fsdp"), None, None),
            P(("dp", "fsdp"), None),
        ),
        out_specs=(
            P(("dp", "fsdp"), None, None),
            P(("dp", "fsdp"), None),
            P(("dp", "fsdp"), None, None),
            P(("dp", "fsdp"), None),
            P(("dp", "fsdp"), None),
            P("dp", None),
            P("fsdp", None),
            P("fsdp"),
            P("fsdp", None),
            P("fsdp", None),
            P("fsdp", None),
            P("fsdp", None),
            P("fsdp"),
            P("fsdp", None),
            P("fsdp"),
            P("fsdp", None),
            P("fsdp"),
        ),
        check_vma=False,
    )
```

```python
import functools
import math

import jax
import jax.numpy as jnp
from jax import lax
from jax.experimental import pallas as pl
from jax.experimental.pallas import tpu as pltpu
from jax.sharding import PartitionSpec as P

CHAN = 128
SPLIT = 4


epsilon = 1e-06


def low(value):
    return value.astype(jnp.bfloat16)


def packed(parts, unit):
    flat = jnp.concatenate([part.reshape(-1) for part in parts])
    return jnp.pad(flat, (0, -flat.size % (unit * 128))).reshape(-1, 128)


def unpacked(rows, shapes):
    lead = rows.shape[:-2]
    flat = rows.reshape(lead + (-1,))
    parts, start = [], 0
    for shape in shapes:
        size = math.prod(shape)
        parts.append(flat[..., start : start + size].reshape(lead + shape))
        start += size
    return parts


MESH_IDS = pl.DeviceIdType.MESH
VMEM_BYTES = 67_000_000
BY_ROLE, BY_SHARD, BY_COLUMN = range(3)


def flipped(value, step, size):
    total, bit = 0, 1
    while bit < size:
        digit = (value // bit) % 2
        total = total + bit * ((digit + 1) % 2 if step & bit else digit)
        bit *= 2
    return total


def greet(peers):
    barrier = pltpu.get_barrier_semaphore()
    for peer in peers:
        pl.semaphore_signal(barrier, inc=1, device_id=peer, device_id_type=MESH_IDS)
    pl.semaphore_wait(barrier, len(peers))


def remote(source, target, send_sem, recv_sem, peer):
    return pltpu.make_async_remote_copy(
        src_ref=source,
        dst_ref=target,
        send_sem=send_sem,
        recv_sem=recv_sem,
        device_id=peer,
        device_id_type=MESH_IDS,
    )


def exchange_kernel(axis, size, spread_out, rows_ref, out_ref, send_sem, recv_sem):
    me = lax.axis_index(axis)
    greet([{axis: (me + step) % size} for step in range(1, size)])

    def piece(target):
        return rows_ref.at[target] if spread_out else rows_ref

    sent = []
    for step in range(1, size):
        peer = (me + step) % size
        copy = remote(
            piece(peer), out_ref.at[me], send_sem.at[step], recv_sem.at[size - step], {axis: peer}
        )
        copy.start()
        sent.append(copy)
    out_ref[me] = rows_ref[me] if spread_out else rows_ref[...]
    for step in range(1, size):
        peer = (me + step) % size
        remote(
            piece(peer), out_ref.at[peer], send_sem.at[step], recv_sem.at[step], {axis: peer}
        ).wait_recv()
    for copy in sent:
        copy.wait_send()


def exchange(rows, axis, spread_out, number):
    size = lax.axis_size(axis)
    block = rows.shape[1:] if spread_out else rows.shape
    return pl.pallas_call(
        functools.partial(exchange_kernel, axis, size, spread_out),
        out_shape=jax.ShapeDtypeStruct((size,) + block, rows.dtype),
        in_specs=[pl.BlockSpec(memory_space=pltpu.VMEM)],
        out_specs=pl.BlockSpec(memory_space=pltpu.VMEM),
        scratch_shapes=[pltpu.SemaphoreType.DMA((size,)), pltpu.SemaphoreType.DMA((size,))],
        compiler_params=pltpu.CompilerParams(
            collective_id=number, has_side_effects=True, vmem_limit_bytes=VMEM_BYTES
        ),
        cost_estimate=taking(8),
        name=f"exchange{number}",
    )(rows)


def taking(microseconds):
    return pl.CostEstimate(flops=0, transcendentals=0, bytes_accessed=microseconds * 3_000_000)


class Place:
    def __init__(self, half):
        self.half = half
        self.role = lax.axis_index("dp")
        shard = lax.axis_index("fsdp")
        self.shard = shard
        self.line, self.side = shard // 2, shard % 2
        self.other_side = (self.side + 1) % 2
        self.roles = [flipped(self.role, step, 4) for step in range(4)]
        self.lines = [flipped(self.line, step, half) for step in range(half)]
        self.sides = [self.side, self.other_side]
        self.across = {"dp": self.roles[2]}
        self.beside = {"fsdp": self.line * 2 + self.other_side}
        self.core = {"dp": self.roles[1]}
        self.along = [{"fsdp": line * 2 + self.side} for line in self.lines]

    def greet(self, every_shard=False):
        if every_shard:
            shards = [{"fsdp": (self.shard + step) % (2 * self.half)} for step in range(1, 2 * self.half)]
        else:
            shards = [self.beside] + self.along[1:]
        greet([self.across, self.core] + shards)


class Message:
    def __init__(self, at, rows, out, spread_out, send_sem, recv_sem):
        self.at, self.rows, self.out, self.spread_out = at, rows, out, spread_out
        self.send_sem, self.recv_sem, self.sent = send_sem, recv_sem, []
        self.size = 2 * at.half

    def slot(self, shard):
        return self.out.at[shard] if self.spread_out else self.out.at[self.at.role, shard]

    def send(self, number, recv_number, source, target, peer):
        copy = remote(source, target, self.send_sem.at[number], self.recv_sem.at[recv_number], peer)
        copy.start()
        self.sent.append(copy)

    def got(self, number, target):
        remote(
            target, target, self.send_sem.at[number], self.recv_sem.at[number], self.at.core
        ).wait_recv()

    def begin(self):
        me = self.at.shard
        for step in range(1, self.size):
            peer = (me + step) % self.size
            source = self.rows.at[peer] if self.spread_out else self.rows
            self.send(step, self.size - step, source, self.slot(me), {"fsdp": peer})
        self.slot(me)[...] = self.rows[me] if self.spread_out else self.rows[...]

    def arrive(self):
        for step in range(1, self.size):
            self.got(step, self.slot((self.at.shard + step) % self.size))
        if not self.spread_out:
            own = self.out.at[self.at.role]
            self.send(self.size, self.size, own, own, self.at.across)
            self.send(self.size + 1, self.size + 1, own, own, self.at.core)

    def finish(self):
        if not self.spread_out:
            far = self.out.at[self.at.roles[2]]
            self.got(self.size, far)
            self.send(self.size + 2, self.size + 2, far, far, self.at.core)
            self.got(self.size + 1, self.out.at[self.at.roles[1]])
            self.got(self.size + 2, self.out.at[self.at.roles[3]])
        for copy in self.sent:
            copy.wait_send()


def message_scratch(half):
    return [pltpu.SemaphoreType.DMA((2 * half + 3,)), pltpu.SemaphoreType.DMA((2 * half + 3,))]

def cut(rows):
    first = (rows // 2 + 15) // 16 * 16
    return [(0, first), (first, rows - first)]


def block_view(ref, layout, role, line, side, rows):
    if layout == BY_SHARD:
        return ref.at[line, side, role, rows]
    if layout == BY_ROLE:
        return ref.at[role, line, side, rows]
    width = ref.shape[-1] // 4
    return ref.at[line, side, rows, pl.ds(pl.multiple_of(role * width, 128), width)]


def whole_shape(layout, half, rows, columns):
    lead = {BY_ROLE: (4, half, 2), BY_SHARD: (half, 2, 4), BY_COLUMN: (half, 2)}[layout]
    return lead + (rows, 4 * columns if layout == BY_COLUMN else columns)


class GatherUnit:
    def __init__(self, at, line, out, layout, start, count, side_first, send_sem, recv_sem):
        self.at, self.line, self.out, self.layout = at, line, out, layout
        self.rows = pl.ds(start, count)
        self.side_first, self.send_sem, self.recv_sem = side_first, send_sem, recv_sem
        self.sent = []

    def view(self, role, line, side):
        return block_view(self.out, self.layout, role, line, side, self.rows)

    def send(self, number, make):
        self.sent.append((number, make))
        self.copy_of(number, make).start()

    def copy_of(self, number, make):
        source, target, peer = make()
        return remote(source, target, self.send_sem.at[number], self.recv_sem.at[number], peer)

    def got(self, number, target):
        remote(
            target, target, self.send_sem.at[number], self.recv_sem.at[number], self.at.core
        ).wait_recv()

    def numbers(self):
        half = self.at.half
        return half, 2 * half, 3 * half, 3 * half + 1

    def block_to(self, step, peer):
        at = self.at
        where = (at.role, at.lines[step], at.side)
        if step < len(self.line):
            return lambda: (self.line[step].at[self.rows], self.view(*where), peer)
        return lambda: (self.view(*where), self.view(*where), peer)

    def begin(self, to_side):
        beside, across, _, _ = self.numbers()
        for step in range(len(self.line)):
            if to_side:
                self.send(beside + step, self.block_to(step, self.at.beside))
            else:
                self.send(across + step, self.block_to(step, self.at.across))

    def begin_line(self):
        if len(self.line) == 1:
            for step in range(1, self.at.half):
                self.send(step, self.block_to(0, self.at.along[step]))

    def line_step(self, step):
        beside, across, _, _ = self.numbers()
        if step >= len(self.line):
            self.got(step, self.view(self.at.role, self.at.lines[step], self.at.side))
            self.send(across + step, self.block_to(step, self.at.across))
            self.send(beside + step, self.block_to(step, self.at.beside))

    def pass_on(self, number, peer, *where):
        self.send(number, lambda: (self.view(*where), self.view(*where), peer))

    def second(self):
        at, every = self.at, slice(None)
        beside, across, second, core = self.numbers()
        for step in range(at.half):
            if self.side_first:
                self.got(beside + step, self.view(at.role, at.lines[step], at.other_side))
            else:
                self.got(across + step, self.view(at.roles[2], at.lines[step], at.side))
        if self.side_first:
            where = (at.role, every, at.other_side)
            self.pass_on(second, at.across, *where)
        else:
            where = (at.roles[2], every, at.side)
            self.pass_on(second, at.beside, *where)
        self.pass_on(core, at.core, at.role, every, at.side)
        self.pass_on(core + 1, at.core, *where)

    def third(self):
        at, every = self.at, slice(None)
        beside, across, second, core = self.numbers()
        for step in range(at.half):
            if self.side_first:
                self.got(across + step, self.view(at.roles[2], at.lines[step], at.side))
            else:
                self.got(beside + step, self.view(at.role, at.lines[step], at.other_side))
        if self.side_first:
            self.pass_on(core + 2, at.core, at.roles[2], every, at.side)
        else:
            self.pass_on(core + 2, at.core, at.role, every, at.other_side)
        last = (at.roles[2], every, at.other_side)
        self.got(second, self.view(*last))
        self.pass_on(core + 3, at.core, *last)

    def finish(self):
        at, every = self.at, slice(None)
        core = self.numbers()[3]
        near, far = at.roles[1], at.roles[3]
        views = [
            self.view(near, every, at.side),
            self.view(near, every, at.other_side),
            self.view(far, every, at.side),
            self.view(far, every, at.other_side),
        ]
        if not self.side_first:
            views[1], views[2] = views[2], views[1]
        for step, view in enumerate(views):
            self.got(core + step, view)
        for number, make in self.sent:
            self.copy_of(number, make).wait_send()


def gather_start(at, layouts, orders, lines, outs, send_sem, recv_sem, local_sem):
    pairs, local = [], []
    for matrix, layout in enumerate(layouts):
        line = lines[matrix]
        rows = line[0].shape[0]
        pairs.append(
            [
                GatherUnit(
                    at,
                    line,
                    outs[matrix],
                    layout,
                    start,
                    size,
                    orders[matrix][part],
                    send_sem.at[2 * matrix + part],
                    recv_sem.at[2 * matrix + part],
                )
                for part, (start, size) in enumerate(cut(rows))
            ]
        )

        def make(step, matrix=matrix, layout=layout, line=line, rows=rows):
            place = (at.role, at.lines[step], at.side, pl.ds(0, rows))
            return pltpu.make_async_copy(
                line[step], block_view(outs[matrix], layout, *place), local_sem.at[matrix, step]
            )

        for step in range(len(line)):
            make(step).start()
            local.append(functools.partial(make, step))
    for pair in pairs:
        for unit in pair:
            unit.begin(False)
    return pairs, local


def gather_actions(pairs, local):
    count = len(pairs)
    actions = []

    def each(pair, name, *given):
        def act():
            for unit in pair:
                getattr(unit, name)(*given)

        actions.append(act)

    def settle():
        for make in local:
            make().wait()

    half = pairs[0][0].at.half
    for pair in pairs:
        each(pair, "begin_line")
    for pair in pairs:
        each(pair, "begin", True)
    actions.append(settle)
    for matrix in range(count + 1):
        if matrix < count:
            if len(pairs[matrix][0].line) == 1:
                for step in range(1, half):
                    each(pairs[matrix], "line_step", step)
            each(pairs[matrix], "second")
        if matrix:
            each(pairs[matrix - 1], "third")
    for pair in pairs:
        each(pair, "finish")
    return actions


def gather_scratch(count, half):
    return [
        pltpu.SemaphoreType.DMA((2 * count, 3 * half + 5)),
        pltpu.SemaphoreType.DMA((2 * count, 3 * half + 5)),
        pltpu.SemaphoreType.DMA((count, half)),
    ]


class LineCopies:
    def __init__(self, at, block, out, send_sem, recv_sem):
        self.at, self.block, self.out = at, block, out
        self.send_sem, self.recv_sem = send_sem, recv_sem

    def copy_of(self, step):
        return remote(
            self.block,
            self.out.at[step],
            self.send_sem.at[step],
            self.recv_sem.at[step],
            self.at.along[step],
        )

    def begin(self):
        for step in range(1, self.at.half):
            self.copy_of(step).start()

    def finish(self):
        for step in range(1, self.at.half):
            self.copy_of(step).wait_recv()
            self.copy_of(step).wait_send()


def gather_kernel(half, layout, order, *refs):
    piece, next_piece, rows, whole, line, out = refs[:6]
    message_sems, line_sems, scratch = refs[6:8], refs[8:10], refs[10:]
    at = Place(half)
    message = Message(at, rows, out, True, *message_sems)
    copies = LineCopies(at, next_piece, line, *line_sems)
    at.greet(True)
    message.begin()
    pairs, local = gather_start(at, (layout,), (order,), [[piece]], [whole], *scratch)
    actions = gather_actions(pairs, local)
    actions[0]()
    copies.begin()
    for action in actions[1:]:
        action()
    message.arrive()
    message.finish()
    copies.finish()


def gather(piece, layout, order, next_piece, rows, number):
    half = lax.axis_size("fsdp") // 2
    vmem, hbm = pl.BlockSpec(memory_space=pltpu.VMEM), pl.BlockSpec(memory_space=pl.ANY)
    return pl.pallas_call(
        functools.partial(gather_kernel, half, layout, order),
        out_shape=[
            jax.ShapeDtypeStruct(whole_shape(layout, half, *piece.shape), piece.dtype),
            jax.ShapeDtypeStruct((half,) + next_piece.shape, next_piece.dtype),
            jax.ShapeDtypeStruct(rows.shape, rows.dtype),
        ],
        in_specs=[vmem] * 3,
        out_specs=[hbm, vmem, vmem],
        scratch_shapes=message_scratch(half)
        + [pltpu.SemaphoreType.DMA((half,)), pltpu.SemaphoreType.DMA((half,))]
        + gather_scratch(1, half),
        compiler_params=pltpu.CompilerParams(
            collective_id=number, has_side_effects=True, vmem_limit_bytes=VMEM_BYTES
        ),
        name=f"gather{number}",
    )(piece, next_piece, rows)


def accumulate(target, source):
    rows = target.shape[0]
    chunk = 16 if rows % 16 == 0 else rows

    def step(index, carry):
        place_of = pl.ds(pl.multiple_of(index * chunk, chunk), chunk)
        target[place_of] = target[place_of] + source[place_of]
        return carry

    lax.fori_loop(0, rows // chunk, step, 0)


class ScatterUnit:
    def __init__(self, at, terms, out, layout, start, count, across_first, sems, buffers):
        self.at, self.terms, self.out, self.layout = at, terms, out, layout
        self.rows = pl.ds(start, count)
        self.across_first = across_first
        self.send_sem, self.recv_sem, self.stage_sem = sems
        self.core_buf, self.first_buf, self.last_buf, self.stage = buffers
        self.sent = []
        self.base_first, self.base_last = 4, 6
        self.first_peer = at.across if across_first else at.beside
        self.last_peer = at.beside if across_first else at.across

    def own_terms(self, first, last, core):
        role_step, side_step = (first, last) if self.across_first else (last, first)
        role = self.at.roles[2 * role_step + core]
        return block_view(
            self.terms, self.layout, role, slice(None), self.at.sides[side_step], self.rows
        )

    def send(self, number, make):
        self.sent.append((number, make))
        self.copy_of(number, make).start()

    def copy_of(self, number, make):
        source, target, peer = make()
        return remote(source, target, self.send_sem.at[number], self.recv_sem.at[number], peer)

    def got(self, number, target):
        remote(
            target, target, self.send_sem.at[number], self.recv_sem.at[number], self.at.core
        ).wait_recv()

    def add_lines(self, target, source):
        def step(line, carry):
            accumulate(target.at[line], source.at[line])
            return carry

        lax.fori_loop(0, self.at.half, step, 0)

    def begin(self):
        for first in (1, 0):
            for last in (1, 0):
                self.send(
                    2 * first + last,
                    lambda first=first, last=last: (
                        self.own_terms(first, last, 1), self.core_buf.at[first, last], self.at.core
                    ),
                )

    def paired(self, first, last):
        buffer = self.core_buf.at[first, last]
        load = pltpu.make_async_copy(self.own_terms(first, last, 0), self.stage, self.stage_sem)
        load.start()
        self.got(2 * first + last, buffer)
        load.wait()
        self.add_lines(buffer, self.stage)
        if first:
            self.send(
                self.base_first + last,
                lambda: (
                    self.core_buf.at[first, last], self.first_buf.at[last], self.first_peer
                ),
            )

    def joined(self, last):
        buffer = self.first_buf.at[last]
        self.got(self.base_first + last, buffer)
        self.add_lines(buffer, self.core_buf.at[0, last])
        if last:
            for step in list(range(self.at.half - 1, 0, -1)) + [0]:
                self.send(
                    self.base_last + step,
                    lambda line=self.at.lines[step]: (
                        self.first_buf.at[last, line], self.last_buf.at[line], self.last_peer
                    ),
                )

    def lined(self, step):
        line = self.at.lines[step]
        block = self.last_buf.at[line]
        self.got(self.base_last + step, block)
        accumulate(block, self.first_buf.at[0, line])
        self.out[line, self.rows] = block[...]

    def finish(self):
        for number, make in self.sent:
            self.copy_of(number, make).wait_send()


def scatter_actions(pairs):
    half = pairs[0][0].at.half
    steps = list(range(half - 1, 0, -1)) + [0]
    stages = [
        [("paired", 1, 1), ("paired", 1, 0)],
        [("paired", 0, 1), ("paired", 0, 0)],
        [("joined", 1), ("joined", 0)],
        [("lined", step) for step in steps],
    ]
    actions = []

    def each(pair, name, *given):
        def act():
            for unit in pair:
                getattr(unit, name)(*given)

        actions.append(act)

    for turn in range(len(stages) + len(pairs) - 1):
        for index, pair in reversed(list(enumerate(pairs))):
            if 0 <= turn - index < len(stages):
                for call in stages[turn - index]:
                    each(pair, *call)
    for pair in pairs:
        each(pair, "finish")
    return actions


def scatter_start(at, layouts, orders, terms, outs, scratch):
    sems, buffers = scratch[:3], scratch[3:]
    pairs = []
    for matrix, layout in enumerate(layouts):
        pair = []
        for part, (start, size) in enumerate(cut(terms[matrix].shape[-2])):
            unit = 2 * matrix + part
            pair.append(
                ScatterUnit(
                    at,
                    terms[matrix],
                    outs[matrix],
                    layout,
                    start,
                    size,
                    orders[matrix][part],
                    [sem.at[unit] for sem in sems],
                    buffers[4 * unit : 4 * unit + 4],
                )
            )
        pairs.append(pair)
    for pair in pairs:
        for unit in pair:
            unit.begin()
    return pairs


def scatter_scratch(count, half, rows, columns):
    scratch = [pltpu.SemaphoreType.DMA((2 * count, half + 6))] * 2
    scratch += [pltpu.SemaphoreType.DMA((2 * count,))]
    for _ in range(count):
        for _, size in cut(rows):
            for lead in ((2, 2, half), (2, half), (half,), (half,)):
                scratch.append(pltpu.VMEM(lead + (size, columns), jnp.bfloat16))
    return scratch


def scatter_outs(count, half, rows, columns):
    return [jax.ShapeDtypeStruct((half, rows, columns), jnp.bfloat16)] * count


def swap(value, axis, mask):
    size = lax.axis_size(axis)
    return lax.ppermute(value, axis, [(source, source ^ mask) for source in range(size)])


def along_line(near, later):
    line = lax.axis_index("fsdp") // 2

    def at(sums, index):
        return lax.dynamic_index_in_dim(sums, index, 0, keepdims=False)

    return [at(near, line)] + [
        swap(at(near if mask == 2 else later, line ^ (mask // 2)), "fsdp", mask)
        for mask in range(2, lax.axis_size("fsdp"), 2)
    ]


def four_roles(terms):
    role = lax.axis_index("dp")
    total = sum(term.astype(jnp.float32) for term in terms).astype(jnp.bfloat16)
    across = swap(total, "dp", 2)
    blocks = [total, swap(total, "dp", 1), across, swap(across, "dp", 1)]
    whole = jnp.zeros((4,) + total.shape, jnp.float32)
    for step, block in enumerate(blocks):
        whole = lax.dynamic_update_slice(
            whole, block[None].astype(jnp.float32), (role ^ step, 0, 0)
        )
    return whole


class LineSum:
    def __init__(self, at, near, out, buffer, send_sem, recv_sem, local_sem):
        self.at, self.near, self.out, self.buffer = at, near, out, buffer
        self.send_sem, self.recv_sem, self.local_sem = send_sem, recv_sem, local_sem
        self.sent = []

    def send(self, number, source, target, peer):
        copy = remote(source, target, self.send_sem.at[number], self.recv_sem.at[number], peer)
        copy.start()
        self.sent.append(copy)

    def got(self, number, target):
        remote(
            target, target, self.send_sem.at[number], self.recv_sem.at[number], self.at.core
        ).wait_recv()

    def begin(self):
        at = self.at
        for step in range(1, at.half):
            self.send(step, self.near.at[at.lines[step]], self.buffer.at[step], at.along[step])
        self.local = pltpu.make_async_copy(
            self.near.at[at.line], self.buffer.at[0], self.local_sem
        )
        self.local.start()

    def total(self):
        at, own = self.at, self.buffer.at[0]
        self.local.wait()
        for step in range(1, at.half):
            self.got(step, self.buffer.at[step])
            accumulate(own, self.buffer.at[step])
        self.out[at.role] = own[...]
        self.send(at.half, own, self.out.at[at.role], at.across)
        self.send(at.half + 1, own, self.out.at[at.role], at.core)

    def share(self):
        at = self.at
        far = self.out.at[at.roles[2]]
        self.got(at.half, far)
        self.send(at.half + 2, far, far, at.core)

    def finish(self):
        at = self.at
        self.got(at.half + 1, self.out.at[at.roles[1]])
        self.got(at.half + 2, self.out.at[at.roles[3]])
        for copy in self.sent:
            copy.wait_send()


def roles_kernel(half, order, *refs):
    ins, rows, nears = refs[:6], refs[6], refs[7:9]
    out, rows_out, sums = refs[9], refs[10], refs[11:13]
    left, right, terms, local_sem, line_buf, line_send, line_recv, line_local = refs[13:21]
    scratch = refs[21:]
    at = Place(half)
    lines = [
        LineSum(
            at,
            nears[index],
            sums[index],
            line_buf.at[index],
            line_send.at[index],
            line_recv.at[index],
            line_local.at[index],
        )
        for index in range(2)
    ]
    local = []
    for index in range(6):
        target = left.at[index] if index < 2 else right.at[index - 2]
        copy = pltpu.make_async_copy(ins[index], target, local_sem.at[index])
        copy.start()
        local.append(copy)
    message = Message(at, rows, rows_out, False, *scratch[:2])
    at.greet(True)
    message.begin()
    for line in lines:
        line.begin()
    for copy in local:
        copy.wait()
    shard_rows, columns = terms.shape[3:]
    chunks = 3
    width = columns // chunks

    def product_of(role, chunk):
        window = pl.ds(pl.multiple_of(chunk * width, 128), width)
        result = dot_tn(left[role // 3], right[role, :, window]).astype(jnp.bfloat16)
        for shard in range(2 * half):
            terms[role, shard // 2, shard % 2, :, window] = result[
                shard * shard_rows : (shard + 1) * shard_rows
            ]

    def two_roles(first, second):
        def step(index, carry):
            role = jnp.where(index < chunks, first, second)
            product_of(role, index % chunks)
            return carry

        lax.fori_loop(0, 2 * chunks, step, 0)

    two_roles(at.roles[3], at.roles[1])
    pairs = scatter_start(at, (BY_ROLE,), (order,), [terms], [out], scratch[2:])
    two_roles(at.roles[2], at.roles[0])
    actions = scatter_actions(pairs)
    for action in actions[:4]:
        action()
    message.arrive()
    for action in actions[4:6]:
        action()
    lines[0].total()
    for action in actions[6:]:
        action()
    lines[0].share()
    lines[1].total()
    message.finish()
    lines[0].finish()
    lines[1].share()
    lines[1].finish()


def scatter_products(lefts, rights, order, message, nears, number):
    half = lax.axis_size("fsdp") // 2
    model_width = lefts[0].shape[1]
    rows, columns = model_width // (2 * half), rights[0].shape[1]
    vmem, hbm = pl.BlockSpec(memory_space=pltpu.VMEM), pl.BlockSpec(memory_space=pl.ANY)
    return pl.pallas_call(
        functools.partial(roles_kernel, half, order),
        out_shape=scatter_outs(1, half, rows, columns)
        + [jax.ShapeDtypeStruct((4, 2 * half) + message.shape, message.dtype)]
        + [jax.ShapeDtypeStruct((4, rows, columns), jnp.bfloat16)] * 2,
        in_specs=[hbm] * 6 + [vmem] + [hbm] * 2,
        out_specs=[vmem] * 4,
        scratch_shapes=[
            pltpu.VMEM((2,) + lefts[0].shape, jnp.bfloat16),
            pltpu.VMEM((4,) + rights[0].shape, jnp.bfloat16),
            pltpu.VMEM((4, half, 2, rows, columns), jnp.bfloat16),
            pltpu.SemaphoreType.DMA((6,)),
            pltpu.VMEM((2, half, rows, columns), jnp.bfloat16),
            pltpu.SemaphoreType.DMA((2, half + 3)),
            pltpu.SemaphoreType.DMA((2, half + 3)),
            pltpu.SemaphoreType.DMA((2,)),
        ]
        + message_scratch(half)
        + scatter_scratch(1, half, rows, columns),
        compiler_params=pltpu.CompilerParams(
            collective_id=number, has_side_effects=True, vmem_limit_bytes=VMEM_BYTES
        ),
        cost_estimate=taking(90),
        name=f"scatter{number}",
    )(*lefts, *rights, message, *nears)


def head_window(head, width, columns):
    tile = jnp.minimum(head * width // 128, columns // 128 - 2)
    lane = lax.broadcasted_iota(jnp.int32, (1, 256), 1) + tile * 128
    inside = jnp.logical_and(lane >= head * width, lane < (head + 1) * width)
    return pl.ds(pl.multiple_of(tile * 128, 128), 256), jnp.where(inside, 1.0, 0.0)


def dot_nt(left, right):
    return lax.dot_general(
        left, right, (((1,), (1,)), ((), ())), preferred_element_type=jnp.float32
    )


def dot_tn(left, right):
    return lax.dot_general(
        left, right, (((0,), (0,)), ((), ())), preferred_element_type=jnp.float32
    )


def attend_head(head, width, q_ref, k_ref, v_ref, o_ref, log_ref):
    scaling = width ** (-0.5)
    window, inside = head_window(head, width, q_ref.shape[1])
    queries = q_ref[:, window] * inside.astype(jnp.bfloat16)
    scores = dot_nt(queries, k_ref[:, window]) * scaling
    row_max = jnp.max(scores, axis=-1, keepdims=True)
    exponent = jnp.exp(scores - row_max)
    row_total = jnp.sum(exponent, axis=-1, keepdims=True)
    weights = (exponent * (1.0 / row_total)).astype(jnp.bfloat16)
    result = jnp.dot(weights, v_ref[:, window], preferred_element_type=jnp.float32)
    o_ref[:, window] += result * inside
    lane = lax.broadcasted_iota(jnp.int32, (1, log_ref.shape[1]), 1)
    log_ref[...] = jnp.where(lane == head, row_max + jnp.log(row_total), log_ref[...])


def attend_back_head(head, width, q_ref, k_ref, v_ref, g_ref, log_ref, dq_ref, dk_ref, dv_ref):
    scaling = width ** (-0.5)
    window, inside = head_window(head, width, q_ref.shape[1])
    inside_low = inside.astype(jnp.bfloat16)
    queries, grads = q_ref[:, window] * inside_low, g_ref[:, window] * inside_low
    key_rows = k_ref[:, window]
    lane = lax.broadcasted_iota(jnp.int32, (1, log_ref.shape[1]), 1)
    log_total = jnp.sum(jnp.where(lane == head, log_ref[...], 0.0), axis=-1, keepdims=True)
    weights = jnp.exp(dot_nt(queries, key_rows) * scaling - log_total)
    dv_ref[:, window] += dot_tn(weights.astype(jnp.bfloat16), grads)
    d_weights = dot_nt(grads, v_ref[:, window])
    inner = jnp.sum(weights * d_weights, axis=-1, keepdims=True)
    d_scores = (weights * (d_weights - inner)).astype(jnp.bfloat16)
    dq_ref[:, window] += jnp.dot(d_scores, key_rows, preferred_element_type=jnp.float32) * (
        inside * scaling
    )
    dk_ref[:, window] += dot_tn(d_scores, queries) * scaling


def run_heads(head_count, attend_one, actions):
    spread_over = {}
    for index, action in enumerate(actions):
        spread_over.setdefault(index * head_count // len(actions), []).append(action)

    def step(head, carry):
        attend_one(head)
        for when, group in spread_over.items():

            @pl.when(head == when)
            def _(group=group):
                for action in group:
                    action()

        return carry

    lax.fori_loop(0, head_count, step, 0)


def forward_kernel(half, layouts, orders, heads, *refs):
    count = len(layouts)
    q_ref, k_ref, v_ref = refs[:3]
    fc1_piece, fc1_line, fc2_piece = refs[3:6]
    lines = [[fc1_piece] + [fc1_line.at[step] for step in range(1, half)], [fc2_piece]]
    refs = refs[6:]
    o_ref, log_ref, keys, values = refs[:4]
    outs = refs[4 : 4 + count]
    send_sem, recv_sem = refs[4 + count : 6 + count]
    at = Place(half)
    width = q_ref.shape[1] // heads
    rows = keys.shape[0] // 4
    short = q_ref.shape[0] - rows
    own = pl.ds(short, rows)
    beside, along = at.beside, at.along[1]

    def quarter(buffer, index):
        return buffer.at[pl.ds(index * rows, rows)]

    at.greet()
    sent = []

    def send(number, source, target, peer):
        copy = remote(source, target, send_sem.at[number], recv_sem.at[number], peer)
        copy.start()
        sent.append(copy)

    def got(number, target):
        remote(target, target, send_sem.at[number], recv_sem.at[number], along).wait_recv()

    send(0, k_ref.at[own], quarter(keys, 1), beside)
    send(1, v_ref.at[own], quarter(values, 2), along)
    send(2, v_ref.at[own], quarter(values, 1), beside)
    send(3, k_ref.at[own], quarter(keys, 2), along)
    pairs, local = gather_start(at, layouts, orders, lines, outs, *refs[6 + count :])
    actions = gather_actions(pairs, local)
    beside_first, settle, second, line_steps = count, 2 * count, 2 * count + 1, 2 * count + 2
    late = line_steps + half - 1
    for action in actions[:beside_first]:
        action()
    quarter(keys, 0)[...] = k_ref[own]
    quarter(values, 0)[...] = v_ref[own]
    o_ref[...] = jnp.zeros_like(o_ref)
    log_ref[...] = jnp.zeros_like(log_ref)

    def pass_on():
        got(0, quarter(keys, 1))
        send(4, quarter(keys, 1), quarter(keys, 3), along)
        got(1, quarter(values, 2))
        send(5, quarter(values, 2), quarter(values, 3), beside)

    first = pl.ds(0, short)
    run_heads(
        heads,
        lambda head: attend_head(
            head,
            width,
            q_ref.at[first],
            k_ref.at[first],
            v_ref.at[first],
            o_ref.at[first],
            log_ref.at[first],
        ),
        [],
    )
    pass_on()
    for action in (
        actions[beside_first : settle + 1] + actions[line_steps:late] + actions[second:line_steps]
    ):
        action()
    got(2, quarter(values, 1))
    got(3, quarter(keys, 2))
    got(4, quarter(keys, 3))
    got(5, quarter(values, 3))
    run_heads(
        heads,
        lambda head: attend_head(
            head, width, q_ref.at[own], keys, values, o_ref.at[own], log_ref.at[own]
        ),
        actions[late:-count],
    )
    for action in actions[-count:]:
        action()
    for copy in sent:
        copy.wait_send()


def attention_forward(q_rows, k_rows, v_rows, blocks, layouts, orders, heads, rows, number):
    half = lax.axis_size("fsdp") // 2
    count = len(layouts)
    vmem, hbm = pl.BlockSpec(memory_space=pltpu.VMEM), pl.BlockSpec(memory_space=pl.ANY)
    total, columns = q_rows.shape
    outs = [
        jax.ShapeDtypeStruct((total, columns), jnp.float32),
        jax.ShapeDtypeStruct((total, 128), jnp.float32),
        jax.ShapeDtypeStruct((4 * rows, columns), jnp.bfloat16),
        jax.ShapeDtypeStruct((4 * rows, columns), jnp.bfloat16),
    ] + [
        jax.ShapeDtypeStruct(whole_shape(layout, half, *blocks[0].shape), blocks[0].dtype)
        for layout in layouts
    ]
    return pl.pallas_call(
        functools.partial(forward_kernel, half, layouts, orders, heads),
        out_shape=outs,
        in_specs=[vmem] * (3 + len(blocks)),
        out_specs=[vmem] * 4 + [hbm] * count,
        scratch_shapes=[pltpu.SemaphoreType.DMA((6,)), pltpu.SemaphoreType.DMA((6,))]
        + gather_scratch(count, half),
        compiler_params=pltpu.CompilerParams(
            collective_id=number, has_side_effects=True, vmem_limit_bytes=VMEM_BYTES
        ),
        cost_estimate=taking(120),
        name=f"attention{number}",
    )(q_rows, k_rows, v_rows, *blocks)


def backward_kernel(half, layouts, orders, heads, *refs):
    count = len(layouts)
    q_ref, k_ref, v_ref, g_ref, log_ref, keys, values = refs[:7]
    terms = refs[7 : 7 + count]
    dq_out, dk_out, dv_out = refs[7 + count : 10 + count]
    outs = refs[10 + count : 10 + 2 * count]
    rest = refs[10 + 2 * count :]
    dq, dk, dv, wide, wide_got, slim, slim_got, send_sem, recv_sem = rest[:9]
    at = Place(half)
    width = q_ref.shape[1] // heads
    rows = keys.shape[0] // 4
    short = q_ref.shape[0] - rows
    own, first = pl.ds(short, rows), pl.ds(0, short)
    beside, along = at.beside, at.along[1]
    at.greet()
    pairs = scatter_start(at, layouts, orders, terms, outs, rest[9:])
    actions = scatter_actions(pairs)
    dq[...] = jnp.zeros_like(dq)
    dk[...] = jnp.zeros_like(dk)
    dv[...] = jnp.zeros_like(dv)
    sent = []

    def send(number, source, target, peer):
        copy = remote(source, target, send_sem.at[number], recv_sem.at[number], peer)
        copy.start()
        sent.append(copy)

    def got(number, target):
        remote(target, target, send_sem.at[number], recv_sem.at[number], along).wait_recv()

    def quarter(index):
        return pl.ds(index * rows, rows)

    split = 2 * count
    run_heads(
        heads,
        lambda head: attend_back_head(
            head,
            width,
            q_ref.at[own],
            keys,
            values,
            g_ref.at[own],
            log_ref.at[own],
            dq.at[own],
            dk,
            dv,
        ),
        actions[:split],
    )
    for part, (source, index) in enumerate([(dk, 2), (dk, 3), (dv, 1), (dv, 3)]):
        wide[part] = source[quarter(index)].astype(jnp.bfloat16)
    send(0, wide.at[pl.ds(0, 2)], wide_got.at[pl.ds(0, 2)], along)
    send(1, wide.at[pl.ds(2, 2)], wide_got.at[pl.ds(2, 2)], beside)
    short_dk, short_dv = dk.at[pl.ds(2 * rows, short)], dv.at[pl.ds(rows, short)]
    short_dk[...] = jnp.zeros_like(short_dk)
    short_dv[...] = jnp.zeros_like(short_dv)
    run_heads(
        heads,
        lambda head: attend_back_head(
            head,
            width,
            q_ref.at[first],
            k_ref.at[first],
            v_ref.at[first],
            g_ref.at[first],
            log_ref.at[first],
            dq.at[first],
            short_dk,
            short_dv,
        ),
        actions[split : split + 2],
    )
    dq_out[...] = dq[...].astype(jnp.bfloat16)
    dk_out[first] = short_dk[...].astype(jnp.bfloat16)
    dv_out[first] = short_dv[...].astype(jnp.bfloat16)
    got(0, wide_got.at[pl.ds(0, 2)])
    slim[0] = (dk[quarter(1)] + wide_got[1].astype(jnp.float32)).astype(jnp.bfloat16)
    send(2, slim.at[0], slim_got.at[0], beside)
    got(1, wide_got.at[pl.ds(2, 2)])
    slim[1] = (dv[quarter(2)] + wide_got[3].astype(jnp.float32)).astype(jnp.bfloat16)
    send(3, slim.at[1], slim_got.at[1], along)
    for action in actions[split + 2 : -count]:
        action()
    got(2, slim_got.at[0])
    total = dk[quarter(0)] + wide_got[0].astype(jnp.float32) + slim_got[0].astype(jnp.float32)
    dk_out[own] = total.astype(jnp.bfloat16)
    got(3, slim_got.at[1])
    total = dv[quarter(0)] + wide_got[2].astype(jnp.float32) + slim_got[1].astype(jnp.float32)
    dv_out[own] = total.astype(jnp.bfloat16)
    for action in actions[-count:]:
        action()
    for copy in sent:
        copy.wait_send()


def attention_backward(
    rows_in, keys, values, gradients, layouts, orders, heads, rows, columns, number
):
    half = lax.axis_size("fsdp") // 2
    count = len(gradients)
    vmem, hbm = pl.BlockSpec(memory_space=pltpu.VMEM), pl.BlockSpec(memory_space=pl.ANY)
    total, model_width = rows_in[0].shape
    quarter_rows = keys.shape[0] // 4
    low_rows = jax.ShapeDtypeStruct((total, model_width), jnp.bfloat16)
    return pl.pallas_call(
        functools.partial(backward_kernel, half, layouts, orders, heads),
        out_shape=[low_rows] * 3 + scatter_outs(count, half, rows, columns),
        in_specs=[vmem] * 7 + [hbm] * count,
        out_specs=[vmem] * (3 + count),
        scratch_shapes=[
            pltpu.VMEM((total, model_width), jnp.float32),
            pltpu.VMEM((4 * quarter_rows, model_width), jnp.float32),
            pltpu.VMEM((4 * quarter_rows, model_width), jnp.float32),
            pltpu.VMEM((4, quarter_rows, model_width), jnp.bfloat16),
            pltpu.VMEM((4, quarter_rows, model_width), jnp.bfloat16),
            pltpu.VMEM((2, quarter_rows, model_width), jnp.bfloat16),
            pltpu.VMEM((2, quarter_rows, model_width), jnp.bfloat16),
            pltpu.SemaphoreType.DMA((4,)),
            pltpu.SemaphoreType.DMA((4,)),
        ]
        + scatter_scratch(count, half, rows, columns),
        compiler_params=pltpu.CompilerParams(
            collective_id=number, has_side_effects=True, vmem_limit_bytes=VMEM_BYTES
        ),
        cost_estimate=taking(150),
        name=f"attention{number}",
    )(*rows_in, keys, values, *gradients)


def product(left, right):
    return jnp.dot(left, right, preferred_element_type=jnp.float32)


def product_tn(left, right):
    return lax.dot_general(
        left, right, (((0,), (0,)), ((), ())), preferred_element_type=jnp.float32
    )


def product_nt(left, right):
    return lax.dot_general(
        left, right, (((1,), (1,)), ((), ())), preferred_element_type=jnp.float32
    )


def spread(per_slot, short_count, len_short, quarter_rows):
    short_rows = short_count * len_short
    row = lax.broadcasted_iota(jnp.int32, (short_rows + quarter_rows, 1), 0)
    result = per_slot[short_count][None]
    for slot in range(short_count):
        result = jnp.where(row < (short_count - slot) * len_short, per_slot[short_count - 1 - slot][None], result)
    return result


def slot_sum(values, short_count, len_short):
    short_rows = short_count * len_short
    short_part = jnp.sum(
        values[:short_rows].reshape((short_count, len_short) + values.shape[1:]), axis=1
    )
    long_part = jnp.sum(values[short_rows:], axis=0, keepdims=True)
    return jnp.concatenate([short_part, long_part], 0)


def norm_parts(values):
    average = jnp.mean(values, axis=-1, keepdims=True)
    centred = values - average
    variance = jnp.mean(centred * centred, axis=-1, keepdims=True)
    inverse = lax.rsqrt(variance + epsilon)
    return (centred * inverse, inverse)


def norm_back(gradient, normed, inverse):
    return inverse * (
        gradient
        - jnp.mean(gradient, axis=-1, keepdims=True)
        - normed * jnp.mean(gradient * normed, axis=-1, keepdims=True)
    )


def silu_grad(values):
    sigmoid_value = jax.nn.sigmoid(values)
    return sigmoid_value * (1.0 + values * (1.0 - sigmoid_value))


def gelu_tanh(values):
    return jax.nn.gelu(values, approximate=True)


def per_device(
    x_short,
    x_long,
    short_cond,
    long_cond,
    short_heads,
    long_heads,
    short_groups,
    long_groups,
    short_keep,
    long_keep,
    w_ada,
    b_ada,
    w_head_router,
    w_group_router,
    w_qkv,
    w_proj,
    b_proj,
    w_fc1,
    b_fc1,
    w_fc2,
    b_fc2,
    g_short,
    g_long,
):
    short_count, len_short, model_width = x_short.shape
    quarter_rows = x_long.shape[0]
    head_count = w_head_router.shape[1]
    head_width = model_width // head_count
    group_count = w_group_router.shape[1]
    slot_count = short_count + 1
    short_rows = short_count * len_short
    row_count = short_rows + quarter_rows
    fsdp_index = lax.axis_index("fsdp")
    fsdp_count = lax.axis_size("fsdp")
    role = lax.axis_index("dp")
    group_row = fsdp_index // SPLIT
    half = fsdp_count // 2
    shard_rows = w_qkv.shape[0]
    unit_rows = w_fc2.shape[0] // 4
    mixed_shard = jnp.concatenate([w_qkv, w_proj], 1)
    attention_piece = lax.dynamic_slice_in_dim(mixed_shard, role * model_width, model_width, 1)
    fc1_piece = lax.dynamic_slice_in_dim(w_fc1, role * model_width, model_width, 1)
    fc2_piece = lax.dynamic_slice_in_dim(w_fc2, role * unit_rows, unit_rows, 0)
    short_act = low(jax.nn.silu(short_cond))
    long_act = low(jax.nn.silu(long_cond))
    message = exchange(packed([short_act, b_proj, b_fc1, b_fc2], 16), "fsdp", False, 0)
    act_rows, proj_bias, fc1_bias, fc2_bias = unpacked(
        message, [(model_width,), b_proj.shape, b_fc1.shape, b_fc2.shape]
    )
    proj_bias, fc1_bias, fc2_bias = (
        bias.reshape(-1).astype(jnp.float32) for bias in (proj_bias, fc1_bias, fc2_bias)
    )
    item_act = jnp.concatenate([act_rows, long_act], 0)
    own_long_act = lax.dynamic_slice_in_dim(long_act, group_row, 1, 0)
    item_columns = lax.dynamic_slice_in_dim(item_act, fsdp_index * shard_rows, shard_rows, 1)
    bias_row = lax.dynamic_update_slice_in_dim(
        jnp.zeros((fsdp_count * b_ada.shape[0],), jnp.float32),
        b_ada.astype(jnp.float32),
        fsdp_index * b_ada.shape[0],
        0,
    )
    partial = jnp.concatenate(
        [
            product(item_columns, w_ada) + bias_row,
            product(item_columns, w_head_router),
            product(item_columns, w_group_router),
        ],
        1,
    )
    width = partial.shape[1]
    for_device = jnp.stack(
        [partial[:fsdp_count], jnp.repeat(partial[fsdp_count:], SPLIT, axis=0)], 1
    ).reshape(fsdp_count, -1)
    for_device = low(jnp.pad(for_device, ((0, 0), (0, -for_device.shape[1] % 2048))))
    attention_full, fc1_line, shares = gather(
        attention_piece,
        BY_ROLE,
        (True, False),
        fc1_piece,
        for_device.reshape(fsdp_count, -1, 128),
        2,
    )
    conditioned = unpacked(jnp.sum(shares.astype(jnp.float32), axis=0), [(2, width)])[0]
    attention_full = attention_full.reshape(4, -1, model_width)
    mod_width = 6 * model_width
    modulation = conditioned[:, :mod_width]
    head_sigmoid = jax.nn.sigmoid(conditioned[:, mod_width : mod_width + head_count])
    group_sigmoid = jax.nn.sigmoid(conditioned[:, mod_width + head_count :])
    head_mask = jnp.concatenate(
        [short_heads, lax.dynamic_slice_in_dim(long_heads, group_row, 1, 0)], 0
    ).astype(jnp.float32)
    group_mask = jnp.concatenate(
        [short_groups, lax.dynamic_slice_in_dim(long_groups, group_row, 1, 0)], 0
    ).astype(jnp.float32)
    head_gate = head_mask * 2.0 * head_sigmoid
    group_gate = group_mask * 2.0 * group_sigmoid
    shift1, scale1, gate1, shift2, scale2, gate2 = jnp.split(
        spread(modulation, short_count, len_short, quarter_rows), 6, axis=1
    )
    x_rows = jnp.concatenate([x_short.reshape(short_rows, model_width), x_long], 0).astype(
        jnp.float32
    )
    keep_rows = jnp.concatenate([short_keep.reshape(short_rows), long_keep], 0).astype(jnp.float32)[
        :, None
    ]
    normed1, inverse1 = norm_parts(x_rows)
    hidden1 = low(normed1 * (1.0 + scale1) + shift1)
    q_rows, k_rows, v_rows = (low(product(hidden1, attention_full[part])) for part in range(3))

    head_rows, log_rows, keys, values, fc1_full, fc2_full = attention_forward(
        q_rows,
        k_rows,
        v_rows,
        [fc1_piece, fc1_line, fc2_piece],
        (BY_COLUMN, BY_SHARD),
        ((True, False), (True, False)),
        head_count,
        quarter_rows,
        3,
    )
    head_gate_rows = spread(
        jnp.repeat(head_gate, head_width, axis=1), short_count, len_short, quarter_rows
    )
    attention = low(head_rows * head_gate_rows)
    projected = product(attention, attention_full[3]) + proj_bias
    mixed = x_rows + gate1 * projected
    fc1_full = fc1_full.reshape(model_width, -1)
    fc2_full = fc2_full.reshape(-1, model_width)
    normed2, inverse2 = norm_parts(mixed)
    hidden2 = low(normed2 * (1.0 + scale2) + shift2)
    channel_gate = spread(
        jnp.repeat(group_gate, CHAN, axis=1), short_count, len_short, quarter_rows
    )
    up_rows = product(hidden2, fc1_full) + fc1_bias
    gelu_value, gelu_pull = jax.vjp(gelu_tanh, up_rows)
    activated = low(gelu_value * channel_gate)
    down_rows = product(activated, fc2_full) + fc2_bias
    out_rows = mixed + gate2 * keep_rows * down_rows
    y_short = low(out_rows[:short_rows].reshape(x_short.shape))
    y_long = low(out_rows[short_rows:])
    gradient = jnp.concatenate([g_short.reshape(short_rows, model_width), g_long], 0).astype(
        jnp.float32
    )
    d_down = low(gradient * gate2 * keep_rows)
    slot_gate2 = slot_sum(gradient * keep_rows * down_rows, short_count, len_short)
    grad_fc2 = low(product_tn(activated, d_down)).reshape(half, 2, 4, unit_rows, model_width)
    d_activated = product_nt(d_down, fc2_full)
    d_channel = slot_sum(d_activated * gelu_value, short_count, len_short)
    d_group = jnp.sum(d_channel.reshape(slot_count, group_count, CHAN), axis=-1)
    d_up = low(gelu_pull(d_activated * channel_gate)[0])
    grad_fc1 = low(product_tn(hidden2, d_up)).reshape(half, 2, shard_rows, -1)
    d_hidden2 = product_nt(d_up, fc1_full)

    slot_shift2 = slot_sum(d_hidden2, short_count, len_short)
    slot_scale2 = slot_sum(d_hidden2 * normed2, short_count, len_short)
    d_mixed = gradient + norm_back(d_hidden2 * (1.0 + scale2), normed2, inverse2)
    d_projected = low(d_mixed * gate1)
    slot_gate1 = slot_sum(d_mixed * projected, short_count, len_short)
    d_attention = product_nt(d_projected, attention_full[3])
    d_head = slot_sum(d_attention * head_rows, short_count, len_short)
    d_head = jnp.sum(d_head.reshape(slot_count, head_count, head_width), axis=-1)
    d_heads = low(d_attention * head_gate_rows)
    bias_grad = jnp.concatenate(
        [jnp.sum(part, axis=0, dtype=jnp.float32) for part in (d_projected, d_up, d_down)]
    )
    dq_rows, dk_rows, dv_rows, fc1_near, fc2_near = attention_backward(
        [q_rows, k_rows, v_rows, d_heads, log_rows],
        keys,
        values,
        [grad_fc1, grad_fc2],
        (BY_COLUMN, BY_SHARD),
        ((True, False), (True, True)),
        head_count,
        shard_rows,
        model_width,
        4,
    )
    d_hidden1 = (
        product_nt(dq_rows, attention_full[0])
        + product_nt(dk_rows, attention_full[1])
        + product_nt(dv_rows, attention_full[2])
    )
    slot_shift1 = slot_sum(d_hidden1, short_count, len_short)
    slot_scale1 = slot_sum(d_hidden1 * normed1, short_count, len_short)
    d_rows = d_mixed + norm_back(d_hidden1 * (1.0 + scale1), normed1, inverse1)
    dx_short = low(d_rows[:short_rows].reshape(x_short.shape))
    dx_long = low(d_rows[short_rows:])
    d_head_logit = d_head * head_mask * 2.0 * head_sigmoid * (1.0 - head_sigmoid)
    d_group_logit = d_group * group_mask * 2.0 * group_sigmoid * (1.0 - group_sigmoid)
    d_conditioned = jnp.concatenate(
        [
            slot_shift1,
            slot_scale1,
            slot_gate1,
            slot_shift2,
            slot_scale2,
            slot_gate2,
            d_head_logit,
            d_group_logit,
        ],
        1,
    )
    message = packed([low(d_conditioned), low(bias_grad), short_act, own_long_act], 16)
    attention_sum, all_rows, fc1_sum, fc2_sum = scatter_products(
        [hidden1, attention],
        [dq_rows, dk_rows, dv_rows, d_projected],
        (True, False),
        message,
        [fc1_near, fc2_near],
        5,
    )
    g_w_fc1 = fc1_sum.transpose(1, 0, 2).reshape(shard_rows, -1).astype(jnp.float32)
    g_w_fc2 = fc2_sum.reshape(-1, model_width).astype(jnp.float32)
    all_rows, bias_rows, all_short, all_long = unpacked(
        all_rows, [(2, width), bias_grad.shape, (model_width,), (model_width,)]
    )
    long_sum = jnp.sum(
        all_rows[:, :, 1].astype(jnp.float32).reshape(4, -1, SPLIT, width), axis=2
    )
    factors = jnp.concatenate([all_rows[:, :, 0], low(long_sum)], 1)
    d_items = lax.dynamic_index_in_dim(factors, role, 0, keepdims=False)
    d_silu = (
        product_nt(d_items[:, :mod_width], w_ada)
        + product_nt(d_items[:, mod_width : mod_width + head_count], w_head_router)
        + product_nt(d_items[:, mod_width + head_count :], w_group_router)
    )
    gathered = exchange(packed([d_silu], 8), "fsdp", False, 7)
    gathered, later_sum = lax.optimization_barrier((gathered, attention_sum))
    attention_grad = four_roles(along_line(attention_sum, later_sum))
    g_w_qkv = attention_grad[:3].transpose(1, 0, 2).reshape(shard_rows, -1)
    g_w_proj = attention_grad[3]
    d_silu = unpacked(gathered, [d_silu.shape])[0]
    d_silu = d_silu.transpose(1, 0, 2).reshape(-1, model_width)
    d_short_cond = lax.dynamic_slice_in_dim(d_silu, fsdp_index, 1, 0) * silu_grad(short_cond)
    d_long_cond = d_silu[fsdp_count:] * silu_grad(long_cond)
    act_factors = jnp.concatenate([all_short, all_long[:, ::SPLIT]], 1)
    act_factors = lax.dynamic_slice_in_dim(
        act_factors, fsdp_index * shard_rows, shard_rows, 2
    ).reshape(-1, shard_rows)
    factors = factors.reshape(-1, width)
    g_w_ada = product_tn(act_factors, factors[:, :mod_width])
    g_w_head_router = product_tn(act_factors, factors[:, mod_width : mod_width + head_count])
    g_w_group_router = product_tn(act_factors, factors[:, mod_width + head_count :])
    g_b_ada = lax.dynamic_slice_in_dim(
        jnp.sum(factors[:, :mod_width].astype(jnp.float32), axis=0),
        fsdp_index * b_ada.shape[0],
        b_ada.shape[0],
        0,
    )
    bias_sum = jnp.sum(bias_rows.astype(jnp.float32), axis=(0, 1))

    def own_bias(start, count):
        return lax.dynamic_slice_in_dim(bias_sum, start + fsdp_index * count, count, 0)

    g_b_proj = own_bias(0, shard_rows)
    g_b_fc1 = own_bias(model_width, 4 * shard_rows)
    g_b_fc2 = own_bias(5 * model_width, shard_rows)
    return (
        y_short,
        y_long,
        dx_short,
        dx_long,
        d_short_cond,
        d_long_cond,
        g_w_ada,
        g_b_ada,
        g_w_head_router,
        g_w_group_router,
        g_w_qkv,
        g_w_proj,
        g_b_proj,
        g_w_fc1,
        g_b_fc1,
        g_w_fc2,
        g_b_fc2,
    )


def solution(mesh):
    return jax.shard_map(
        per_device,
        mesh=mesh,
        in_specs=(
            P(("dp", "fsdp"), None, None),
            P(("dp", "fsdp"), None),
            P(("dp", "fsdp"), None),
            P("dp", None),
            P(("dp", "fsdp"), None),
            P("dp", None),
            P(("dp", "fsdp"), None),
            P("dp", None),
            P(("dp", "fsdp"), None),
            P(("dp", "fsdp")),
            P("fsdp", None),
            P("fsdp"),
            P("fsdp", None),
            P("fsdp", None),
            P("fsdp", None),
            P("fsdp", None),
            P("fsdp"),
            P("fsdp", None),
            P("fsdp"),
            P("fsdp", None),
            P("fsdp"),
            P(("dp", "fsdp"), None, None),
            P(("dp", "fsdp"), None),
        ),
        out_specs=(
            P(("dp", "fsdp"), None, None),
            P(("dp", "fsdp"), None),
            P(("dp", "fsdp"), None, None),
            P(("dp", "fsdp"), None),
            P(("dp", "fsdp"), None),
            P("dp", None),
            P("fsdp", None),
            P("fsdp"),
            P("fsdp", None),
            P("fsdp", None),
            P("fsdp", None),
            P("fsdp", None),
            P("fsdp"),
            P("fsdp", None),
            P("fsdp"),
            P("fsdp", None),
            P("fsdp"),
        ),
        check_vma=False,
    )
```

```python
import functools
import math

import jax
import jax.numpy as jnp
from jax import lax
from jax.experimental import pallas as pl
from jax.experimental.pallas import tpu as pltpu
from jax.sharding import PartitionSpec as P

CHAN = 128
SPLIT = 4


epsilon = 1e-06


def low(value):
    return value.astype(jnp.bfloat16)


def packed(parts, unit):
    flat = jnp.concatenate([part.reshape(-1) for part in parts])
    return jnp.pad(flat, (0, -flat.size % (unit * 128))).reshape(-1, 128)


def unpacked(rows, shapes):
    lead = rows.shape[:-2]
    flat = rows.reshape(lead + (-1,))
    parts, start = [], 0
    for shape in shapes:
        size = math.prod(shape)
        parts.append(flat[..., start : start + size].reshape(lead + shape))
        start += size
    return parts


MESH_IDS = pl.DeviceIdType.MESH
VMEM_BYTES = 67_000_000
BY_ROLE, BY_SHARD, BY_COLUMN = range(3)


def flipped(value, step, size):
    total, bit = 0, 1
    while bit < size:
        digit = (value // bit) % 2
        total = total + bit * ((digit + 1) % 2 if step & bit else digit)
        bit *= 2
    return total


def greet(peers):
    barrier = pltpu.get_barrier_semaphore()
    for peer in peers:
        pl.semaphore_signal(barrier, inc=1, device_id=peer, device_id_type=MESH_IDS)
    pl.semaphore_wait(barrier, len(peers))


def remote(source, target, send_sem, recv_sem, peer):
    return pltpu.make_async_remote_copy(
        src_ref=source,
        dst_ref=target,
        send_sem=send_sem,
        recv_sem=recv_sem,
        device_id=peer,
        device_id_type=MESH_IDS,
    )


def exchange_kernel(axis, size, spread_out, rows_ref, out_ref, send_sem, recv_sem):
    me = lax.axis_index(axis)
    greet([{axis: (me + step) % size} for step in range(1, size)])

    def piece(target):
        return rows_ref.at[target] if spread_out else rows_ref

    sent = []
    for step in range(1, size):
        peer = (me + step) % size
        copy = remote(
            piece(peer), out_ref.at[me], send_sem.at[step], recv_sem.at[size - step], {axis: peer}
        )
        copy.start()
        sent.append(copy)
    out_ref[me] = rows_ref[me] if spread_out else rows_ref[...]
    for step in range(1, size):
        peer = (me + step) % size
        remote(
            piece(peer), out_ref.at[peer], send_sem.at[step], recv_sem.at[step], {axis: peer}
        ).wait_recv()
    for copy in sent:
        copy.wait_send()


def exchange(rows, axis, spread_out, number):
    size = lax.axis_size(axis)
    block = rows.shape[1:] if spread_out else rows.shape
    return pl.pallas_call(
        functools.partial(exchange_kernel, axis, size, spread_out),
        out_shape=jax.ShapeDtypeStruct((size,) + block, rows.dtype),
        in_specs=[pl.BlockSpec(memory_space=pltpu.VMEM)],
        out_specs=pl.BlockSpec(memory_space=pltpu.VMEM),
        scratch_shapes=[pltpu.SemaphoreType.DMA((size,)), pltpu.SemaphoreType.DMA((size,))],
        compiler_params=pltpu.CompilerParams(
            collective_id=number, has_side_effects=True, vmem_limit_bytes=VMEM_BYTES
        ),
        cost_estimate=taking(8),
        name=f"exchange{number}",
    )(rows)


def taking(microseconds):
    return pl.CostEstimate(flops=0, transcendentals=0, bytes_accessed=microseconds * 3_000_000)


class Place:
    def __init__(self, half):
        self.half = half
        self.role = lax.axis_index("dp")
        shard = lax.axis_index("fsdp")
        self.shard = shard
        self.line, self.side = shard // 2, shard % 2
        self.other_side = (self.side + 1) % 2
        self.roles = [flipped(self.role, step, 4) for step in range(4)]
        self.lines = [flipped(self.line, step, half) for step in range(half)]
        self.sides = [self.side, self.other_side]
        self.across = {"dp": self.roles[2]}
        self.beside = {"fsdp": self.line * 2 + self.other_side}
        self.core = {"dp": self.roles[1]}
        self.along = [{"fsdp": line * 2 + self.side} for line in self.lines]

    def greet(self, every_shard=False):
        if every_shard:
            shards = [{"fsdp": (self.shard + step) % (2 * self.half)} for step in range(1, 2 * self.half)]
        else:
            shards = [self.beside] + self.along[1:]
        greet([self.across, self.core] + shards)


class Message:
    def __init__(self, at, rows, out, spread_out, send_sem, recv_sem):
        self.at, self.rows, self.out, self.spread_out = at, rows, out, spread_out
        self.send_sem, self.recv_sem, self.sent = send_sem, recv_sem, []
        self.size = 2 * at.half

    def slot(self, shard):
        return self.out.at[shard] if self.spread_out else self.out.at[self.at.role, shard]

    def send(self, number, recv_number, source, target, peer):
        copy = remote(source, target, self.send_sem.at[number], self.recv_sem.at[recv_number], peer)
        copy.start()
        self.sent.append(copy)

    def got(self, number, target):
        remote(
            target, target, self.send_sem.at[number], self.recv_sem.at[number], self.at.core
        ).wait_recv()

    def begin(self):
        me = self.at.shard
        for step in range(1, self.size):
            peer = (me + step) % self.size
            source = self.rows.at[peer] if self.spread_out else self.rows
            self.send(step, self.size - step, source, self.slot(me), {"fsdp": peer})
        self.slot(me)[...] = self.rows[me] if self.spread_out else self.rows[...]

    def arrive(self):
        for step in range(1, self.size):
            self.got(step, self.slot((self.at.shard + step) % self.size))
        if not self.spread_out:
            own = self.out.at[self.at.role]
            self.send(self.size, self.size, own, own, self.at.across)
            self.send(self.size + 1, self.size + 1, own, own, self.at.core)

    def finish(self):
        if not self.spread_out:
            far = self.out.at[self.at.roles[2]]
            self.got(self.size, far)
            self.send(self.size + 2, self.size + 2, far, far, self.at.core)
            self.got(self.size + 1, self.out.at[self.at.roles[1]])
            self.got(self.size + 2, self.out.at[self.at.roles[3]])
        for copy in self.sent:
            copy.wait_send()


def message_scratch(half):
    return [pltpu.SemaphoreType.DMA((2 * half + 3,)), pltpu.SemaphoreType.DMA((2 * half + 3,))]

def cut(rows):
    first = (rows // 2 + 15) // 16 * 16
    return [(0, first), (first, rows - first)]


def block_view(ref, layout, role, line, side, rows):
    if layout == BY_SHARD:
        return ref.at[line, side, role, rows]
    if layout == BY_ROLE:
        return ref.at[role, line, side, rows]
    width = ref.shape[-1] // 4
    return ref.at[line, side, rows, pl.ds(pl.multiple_of(role * width, 128), width)]


def whole_shape(layout, half, rows, columns):
    lead = {BY_ROLE: (4, half, 2), BY_SHARD: (half, 2, 4), BY_COLUMN: (half, 2)}[layout]
    return lead + (rows, 4 * columns if layout == BY_COLUMN else columns)


class GatherUnit:
    def __init__(self, at, line, out, layout, start, count, side_first, send_sem, recv_sem):
        self.at, self.line, self.out, self.layout = at, line, out, layout
        self.rows = pl.ds(start, count)
        self.side_first, self.send_sem, self.recv_sem = side_first, send_sem, recv_sem
        self.sent = []

    def view(self, role, line, side):
        return block_view(self.out, self.layout, role, line, side, self.rows)

    def send(self, number, make):
        self.sent.append((number, make))
        self.copy_of(number, make).start()

    def copy_of(self, number, make):
        source, target, peer = make()
        return remote(source, target, self.send_sem.at[number], self.recv_sem.at[number], peer)

    def got(self, number, target):
        remote(
            target, target, self.send_sem.at[number], self.recv_sem.at[number], self.at.core
        ).wait_recv()

    def numbers(self):
        half = self.at.half
        return half, 2 * half, 3 * half, 3 * half + 1

    def block_to(self, step, peer):
        at = self.at
        where = (at.role, at.lines[step], at.side)
        if step < len(self.line):
            return lambda: (self.line[step].at[self.rows], self.view(*where), peer)
        return lambda: (self.view(*where), self.view(*where), peer)

    def begin(self, to_side):
        beside, across, _, _ = self.numbers()
        for step in range(len(self.line)):
            if to_side:
                self.send(beside + step, self.block_to(step, self.at.beside))
            else:
                self.send(across + step, self.block_to(step, self.at.across))

    def begin_line(self):
        if len(self.line) == 1:
            for step in range(1, self.at.half):
                self.send(step, self.block_to(0, self.at.along[step]))

    def line_step(self, step):
        beside, across, _, _ = self.numbers()
        if step >= len(self.line):
            self.got(step, self.view(self.at.role, self.at.lines[step], self.at.side))
            self.send(across + step, self.block_to(step, self.at.across))
            self.send(beside + step, self.block_to(step, self.at.beside))

    def pass_on(self, number, peer, *where):
        self.send(number, lambda: (self.view(*where), self.view(*where), peer))

    def second(self):
        at, every = self.at, slice(None)
        beside, across, second, core = self.numbers()
        for step in range(at.half):
            if self.side_first:
                self.got(beside + step, self.view(at.role, at.lines[step], at.other_side))
            else:
                self.got(across + step, self.view(at.roles[2], at.lines[step], at.side))
        if self.side_first:
            where = (at.role, every, at.other_side)
            self.pass_on(second, at.across, *where)
        else:
            where = (at.roles[2], every, at.side)
            self.pass_on(second, at.beside, *where)
        self.pass_on(core, at.core, at.role, every, at.side)
        self.pass_on(core + 1, at.core, *where)

    def third(self):
        at, every = self.at, slice(None)
        beside, across, second, core = self.numbers()
        for step in range(at.half):
            if self.side_first:
                self.got(across + step, self.view(at.roles[2], at.lines[step], at.side))
            else:
                self.got(beside + step, self.view(at.role, at.lines[step], at.other_side))
        if self.side_first:
            self.pass_on(core + 2, at.core, at.roles[2], every, at.side)
        else:
            self.pass_on(core + 2, at.core, at.role, every, at.other_side)
        last = (at.roles[2], every, at.other_side)
        self.got(second, self.view(*last))
        self.pass_on(core + 3, at.core, *last)

    def finish(self):
        at, every = self.at, slice(None)
        core = self.numbers()[3]
        near, far = at.roles[1], at.roles[3]
        views = [
            self.view(near, every, at.side),
            self.view(near, every, at.other_side),
            self.view(far, every, at.side),
            self.view(far, every, at.other_side),
        ]
        if not self.side_first:
            views[1], views[2] = views[2], views[1]
        for step, view in enumerate(views):
            self.got(core + step, view)
        for number, make in self.sent:
            self.copy_of(number, make).wait_send()


def gather_start(at, layouts, orders, lines, outs, send_sem, recv_sem, local_sem):
    pairs, local = [], []
    for matrix, layout in enumerate(layouts):
        line = lines[matrix]
        rows = line[0].shape[0]
        pairs.append(
            [
                GatherUnit(
                    at,
                    line,
                    outs[matrix],
                    layout,
                    start,
                    size,
                    orders[matrix][part],
                    send_sem.at[2 * matrix + part],
                    recv_sem.at[2 * matrix + part],
                )
                for part, (start, size) in enumerate(cut(rows))
            ]
        )

        def make(step, matrix=matrix, layout=layout, line=line, rows=rows):
            place = (at.role, at.lines[step], at.side, pl.ds(0, rows))
            return pltpu.make_async_copy(
                line[step], block_view(outs[matrix], layout, *place), local_sem.at[matrix, step]
            )

        for step in range(len(line)):
            make(step).start()
            local.append(functools.partial(make, step))
    for pair in pairs:
        for unit in pair:
            unit.begin(False)
    return pairs, local


def gather_actions(pairs, local):
    count = len(pairs)
    actions = []

    def each(pair, name, *given):
        def act():
            for unit in pair:
                getattr(unit, name)(*given)

        actions.append(act)

    def settle():
        for make in local:
            make().wait()

    half = pairs[0][0].at.half
    for pair in pairs:
        each(pair, "begin_line")
    for pair in pairs:
        each(pair, "begin", True)
    actions.append(settle)
    for matrix in range(count + 1):
        if matrix < count:
            if len(pairs[matrix][0].line) == 1:
                for step in range(1, half):
                    each(pairs[matrix], "line_step", step)
            each(pairs[matrix], "second")
        if matrix:
            each(pairs[matrix - 1], "third")
    for pair in pairs:
        each(pair, "finish")
    return actions


def gather_scratch(count, half):
    return [
        pltpu.SemaphoreType.DMA((2 * count, 3 * half + 5)),
        pltpu.SemaphoreType.DMA((2 * count, 3 * half + 5)),
        pltpu.SemaphoreType.DMA((count, half)),
    ]


class LineCopies:
    def __init__(self, at, block, out, send_sem, recv_sem):
        self.at, self.block, self.out = at, block, out
        self.send_sem, self.recv_sem = send_sem, recv_sem

    def copy_of(self, step):
        return remote(
            self.block,
            self.out.at[step],
            self.send_sem.at[step],
            self.recv_sem.at[step],
            self.at.along[step],
        )

    def begin(self):
        for step in range(1, self.at.half):
            self.copy_of(step).start()

    def finish(self):
        for step in range(1, self.at.half):
            self.copy_of(step).wait_recv()
            self.copy_of(step).wait_send()


def gather_kernel(half, layout, order, *refs):
    piece, next_piece, rows, whole, line, out = refs[:6]
    message_sems, line_sems, scratch = refs[6:8], refs[8:10], refs[10:]
    at = Place(half)
    message = Message(at, rows, out, True, *message_sems)
    copies = LineCopies(at, next_piece, line, *line_sems)
    at.greet(True)
    message.begin()
    pairs, local = gather_start(at, (layout,), (order,), [[piece]], [whole], *scratch)
    actions = gather_actions(pairs, local)
    actions[0]()
    copies.begin()
    for action in actions[1:]:
        action()
    message.arrive()
    message.finish()
    copies.finish()


def gather(piece, layout, order, next_piece, rows, number):
    half = lax.axis_size("fsdp") // 2
    vmem, hbm = pl.BlockSpec(memory_space=pltpu.VMEM), pl.BlockSpec(memory_space=pl.ANY)
    return pl.pallas_call(
        functools.partial(gather_kernel, half, layout, order),
        out_shape=[
            jax.ShapeDtypeStruct(whole_shape(layout, half, *piece.shape), piece.dtype),
            jax.ShapeDtypeStruct((half,) + next_piece.shape, next_piece.dtype),
            jax.ShapeDtypeStruct(rows.shape, rows.dtype),
        ],
        in_specs=[vmem] * 3,
        out_specs=[hbm, vmem, vmem],
        scratch_shapes=message_scratch(half)
        + [pltpu.SemaphoreType.DMA((half,)), pltpu.SemaphoreType.DMA((half,))]
        + gather_scratch(1, half),
        compiler_params=pltpu.CompilerParams(
            collective_id=number, has_side_effects=True, vmem_limit_bytes=VMEM_BYTES
        ),
        name=f"gather{number}",
    )(piece, next_piece, rows)


def accumulate(target, source):
    rows = target.shape[0]
    chunk = 16 if rows % 16 == 0 else rows

    def step(index, carry):
        place_of = pl.ds(pl.multiple_of(index * chunk, chunk), chunk)
        target[place_of] = target[place_of] + source[place_of]
        return carry

    lax.fori_loop(0, rows // chunk, step, 0)


class ScatterUnit:
    def __init__(self, at, terms, out, layout, start, count, across_first, sems, buffers):
        self.at, self.terms, self.out, self.layout = at, terms, out, layout
        self.rows = pl.ds(start, count)
        self.across_first = across_first
        self.send_sem, self.recv_sem, self.stage_sem = sems
        self.core_buf, self.first_buf, self.last_buf, self.stage = buffers
        self.sent = []
        self.base_first, self.base_last = 4, 6
        self.first_peer = at.across if across_first else at.beside
        self.last_peer = at.beside if across_first else at.across

    def own_terms(self, first, last, core):
        role_step, side_step = (first, last) if self.across_first else (last, first)
        role = self.at.roles[2 * role_step + core]
        return block_view(
            self.terms, self.layout, role, slice(None), self.at.sides[side_step], self.rows
        )

    def send(self, number, make):
        self.sent.append((number, make))
        self.copy_of(number, make).start()

    def copy_of(self, number, make):
        source, target, peer = make()
        return remote(source, target, self.send_sem.at[number], self.recv_sem.at[number], peer)

    def got(self, number, target):
        remote(
            target, target, self.send_sem.at[number], self.recv_sem.at[number], self.at.core
        ).wait_recv()

    def add_lines(self, target, source):
        def step(line, carry):
            accumulate(target.at[line], source.at[line])
            return carry

        lax.fori_loop(0, self.at.half, step, 0)

    def begin(self):
        for first in (1, 0):
            for last in (1, 0):
                self.send(
                    2 * first + last,
                    lambda first=first, last=last: (
                        self.own_terms(first, last, 1), self.core_buf.at[first, last], self.at.core
                    ),
                )

    def paired(self, first, last):
        buffer = self.core_buf.at[first, last]
        load = pltpu.make_async_copy(self.own_terms(first, last, 0), self.stage, self.stage_sem)
        load.start()
        self.got(2 * first + last, buffer)
        load.wait()
        self.add_lines(buffer, self.stage)
        if first:
            self.send(
                self.base_first + last,
                lambda: (
                    self.core_buf.at[first, last], self.first_buf.at[last], self.first_peer
                ),
            )

    def joined(self, last):
        buffer = self.first_buf.at[last]
        self.got(self.base_first + last, buffer)
        self.add_lines(buffer, self.core_buf.at[0, last])
        if last:
            for step in list(range(self.at.half - 1, 0, -1)) + [0]:
                self.send(
                    self.base_last + step,
                    lambda line=self.at.lines[step]: (
                        self.first_buf.at[last, line], self.last_buf.at[line], self.last_peer
                    ),
                )

    def lined(self, step):
        line = self.at.lines[step]
        block = self.last_buf.at[line]
        self.got(self.base_last + step, block)
        accumulate(block, self.first_buf.at[0, line])
        self.out[line, self.rows] = block[...]

    def finish(self):
        for number, make in self.sent:
            self.copy_of(number, make).wait_send()


def scatter_actions(pairs):
    half = pairs[0][0].at.half
    steps = list(range(half - 1, 0, -1)) + [0]
    stages = [
        [("paired", 1, 1), ("paired", 1, 0)],
        [("paired", 0, 1), ("paired", 0, 0)],
        [("joined", 1), ("joined", 0)],
        [("lined", step) for step in steps],
    ]
    actions = []

    def each(pair, name, *given):
        def act():
            for unit in pair:
                getattr(unit, name)(*given)

        actions.append(act)

    for turn in range(len(stages) + len(pairs) - 1):
        for index, pair in reversed(list(enumerate(pairs))):
            if 0 <= turn - index < len(stages):
                for call in stages[turn - index]:
                    each(pair, *call)
    for pair in pairs:
        each(pair, "finish")
    return actions


def scatter_start(at, layouts, orders, terms, outs, scratch):
    sems, buffers = scratch[:3], scratch[3:]
    pairs = []
    for matrix, layout in enumerate(layouts):
        pair = []
        for part, (start, size) in enumerate(cut(terms[matrix].shape[-2])):
            unit = 2 * matrix + part
            pair.append(
                ScatterUnit(
                    at,
                    terms[matrix],
                    outs[matrix],
                    layout,
                    start,
                    size,
                    orders[matrix][part],
                    [sem.at[unit] for sem in sems],
                    buffers[4 * unit : 4 * unit + 4],
                )
            )
        pairs.append(pair)
    for pair in pairs:
        for unit in pair:
            unit.begin()
    return pairs


def scatter_scratch(count, half, rows, columns):
    scratch = [pltpu.SemaphoreType.DMA((2 * count, half + 6))] * 2
    scratch += [pltpu.SemaphoreType.DMA((2 * count,))]
    for _ in range(count):
        for _, size in cut(rows):
            for lead in ((2, 2, half), (2, half), (half,), (half,)):
                scratch.append(pltpu.VMEM(lead + (size, columns), jnp.bfloat16))
    return scratch


def scatter_outs(count, half, rows, columns):
    return [jax.ShapeDtypeStruct((half, rows, columns), jnp.bfloat16)] * count


def swap(value, axis, mask):
    size = lax.axis_size(axis)
    return lax.ppermute(value, axis, [(source, source ^ mask) for source in range(size)])


def along_line(near, later):
    line = lax.axis_index("fsdp") // 2

    def at(sums, index):
        return lax.dynamic_index_in_dim(sums, index, 0, keepdims=False)

    return [at(near, line)] + [
        swap(at(near if mask == 2 else later, line ^ (mask // 2)), "fsdp", mask)
        for mask in range(2, lax.axis_size("fsdp"), 2)
    ]


def four_roles(terms):
    role = lax.axis_index("dp")
    total = sum(term.astype(jnp.float32) for term in terms).astype(jnp.bfloat16)
    across = swap(total, "dp", 2)
    blocks = [total, swap(total, "dp", 1), across, swap(across, "dp", 1)]
    whole = jnp.zeros((4,) + total.shape, jnp.float32)
    for step, block in enumerate(blocks):
        whole = lax.dynamic_update_slice(
            whole, block[None].astype(jnp.float32), (role ^ step, 0, 0)
        )
    return whole


class LineSum:
    def __init__(self, at, near, out, buffer, send_sem, recv_sem, local_sem):
        self.at, self.near, self.out, self.buffer = at, near, out, buffer
        self.send_sem, self.recv_sem, self.local_sem = send_sem, recv_sem, local_sem
        self.sent = []

    def send(self, number, source, target, peer):
        copy = remote(source, target, self.send_sem.at[number], self.recv_sem.at[number], peer)
        copy.start()
        self.sent.append(copy)

    def got(self, number, target):
        remote(
            target, target, self.send_sem.at[number], self.recv_sem.at[number], self.at.core
        ).wait_recv()

    def begin(self):
        at = self.at
        for step in range(1, at.half):
            self.send(step, self.near.at[at.lines[step]], self.buffer.at[step], at.along[step])
        self.local = pltpu.make_async_copy(
            self.near.at[at.line], self.buffer.at[0], self.local_sem
        )
        self.local.start()

    def total(self):
        at, own = self.at, self.buffer.at[0]
        self.local.wait()
        for step in range(1, at.half):
            self.got(step, self.buffer.at[step])
            accumulate(own, self.buffer.at[step])
        self.out[at.role] = own[...]
        self.send(at.half, own, self.out.at[at.role], at.across)
        self.send(at.half + 1, own, self.out.at[at.role], at.core)

    def share(self):
        at = self.at
        far = self.out.at[at.roles[2]]
        self.got(at.half, far)
        self.send(at.half + 2, far, far, at.core)

    def finish(self):
        at = self.at
        self.got(at.half + 1, self.out.at[at.roles[1]])
        self.got(at.half + 2, self.out.at[at.roles[3]])
        for copy in self.sent:
            copy.wait_send()


def roles_kernel(half, order, *refs):
    ins, rows, nears = refs[:6], refs[6], refs[7:9]
    out, rows_out, sums = refs[9], refs[10], refs[11:13]
    left, right, terms, local_sem, line_buf, line_send, line_recv, line_local = refs[13:21]
    scratch = refs[21:]
    at = Place(half)
    lines = [
        LineSum(
            at,
            nears[index],
            sums[index],
            line_buf.at[index],
            line_send.at[index],
            line_recv.at[index],
            line_local.at[index],
        )
        for index in range(2)
    ]
    local = []
    for index in range(6):
        target = left.at[index] if index < 2 else right.at[index - 2]
        copy = pltpu.make_async_copy(ins[index], target, local_sem.at[index])
        copy.start()
        local.append(copy)
    message = Message(at, rows, rows_out, False, *scratch[:2])
    at.greet(True)
    message.begin()
    for line in lines:
        line.begin()
    for copy in local:
        copy.wait()
    shard_rows, columns = terms.shape[3:]
    chunks = 3
    width = columns // chunks

    def product_of(role, chunk):
        window = pl.ds(pl.multiple_of(chunk * width, 128), width)
        result = dot_tn(left[role // 3], right[role, :, window]).astype(jnp.bfloat16)
        for shard in range(2 * half):
            terms[role, shard // 2, shard % 2, :, window] = result[
                shard * shard_rows : (shard + 1) * shard_rows
            ]

    def two_roles(first, second):
        def step(index, carry):
            role = jnp.where(index < chunks, first, second)
            product_of(role, index % chunks)
            return carry

        lax.fori_loop(0, 2 * chunks, step, 0)

    two_roles(at.roles[3], at.roles[1])
    pairs = scatter_start(at, (BY_ROLE,), (order,), [terms], [out], scratch[2:])
    two_roles(at.roles[2], at.roles[0])
    actions = scatter_actions(pairs)
    for action in actions[:4]:
        action()
    message.arrive()
    for action in actions[4:6]:
        action()
    lines[0].total()
    for action in actions[6:]:
        action()
    lines[0].share()
    lines[1].total()
    message.finish()
    lines[0].finish()
    lines[1].share()
    lines[1].finish()


def scatter_products(lefts, rights, order, message, nears, number):
    half = lax.axis_size("fsdp") // 2
    model_width = lefts[0].shape[1]
    rows, columns = model_width // (2 * half), rights[0].shape[1]
    vmem, hbm = pl.BlockSpec(memory_space=pltpu.VMEM), pl.BlockSpec(memory_space=pl.ANY)
    return pl.pallas_call(
        functools.partial(roles_kernel, half, order),
        out_shape=scatter_outs(1, half, rows, columns)
        + [jax.ShapeDtypeStruct((4, 2 * half) + message.shape, message.dtype)]
        + [jax.ShapeDtypeStruct((4, rows, columns), jnp.bfloat16)] * 2,
        in_specs=[hbm] * 6 + [vmem] + [hbm] * 2,
        out_specs=[vmem] * 4,
        scratch_shapes=[
            pltpu.VMEM((2,) + lefts[0].shape, jnp.bfloat16),
            pltpu.VMEM((4,) + rights[0].shape, jnp.bfloat16),
            pltpu.VMEM((4, half, 2, rows, columns), jnp.bfloat16),
            pltpu.SemaphoreType.DMA((6,)),
            pltpu.VMEM((2, half, rows, columns), jnp.bfloat16),
            pltpu.SemaphoreType.DMA((2, half + 3)),
            pltpu.SemaphoreType.DMA((2, half + 3)),
            pltpu.SemaphoreType.DMA((2,)),
        ]
        + message_scratch(half)
        + scatter_scratch(1, half, rows, columns),
        compiler_params=pltpu.CompilerParams(
            collective_id=number, has_side_effects=True, vmem_limit_bytes=VMEM_BYTES
        ),
        cost_estimate=taking(90),
        name=f"scatter{number}",
    )(*lefts, *rights, message, *nears)


def head_window(head, width, columns):
    tile = jnp.minimum(head * width // 128, columns // 128 - 2)
    lane = lax.broadcasted_iota(jnp.int32, (1, 256), 1) + tile * 128
    inside = jnp.logical_and(lane >= head * width, lane < (head + 1) * width)
    return pl.ds(pl.multiple_of(tile * 128, 128), 256), jnp.where(inside, 1.0, 0.0)


def dot_nt(left, right):
    return lax.dot_general(
        left, right, (((1,), (1,)), ((), ())), preferred_element_type=jnp.float32
    )


def dot_tn(left, right):
    return lax.dot_general(
        left, right, (((0,), (0,)), ((), ())), preferred_element_type=jnp.float32
    )


def attend_head(head, width, q_ref, k_ref, v_ref, o_ref, log_ref):
    scaling = width ** (-0.5)
    window, inside = head_window(head, width, q_ref.shape[1])
    queries = q_ref[:, window] * inside.astype(jnp.bfloat16)
    scores = dot_nt(queries, k_ref[:, window]) * scaling
    row_max = jnp.max(scores, axis=-1, keepdims=True)
    exponent = jnp.exp(scores - row_max)
    row_total = jnp.sum(exponent, axis=-1, keepdims=True)
    weights = (exponent * (1.0 / row_total)).astype(jnp.bfloat16)
    result = jnp.dot(weights, v_ref[:, window], preferred_element_type=jnp.float32)
    o_ref[:, window] += result * inside
    lane = lax.broadcasted_iota(jnp.int32, (1, log_ref.shape[1]), 1)
    log_ref[...] = jnp.where(lane == head, row_max + jnp.log(row_total), log_ref[...])


def attend_back_head(head, width, q_ref, k_ref, v_ref, g_ref, log_ref, dq_ref, dk_ref, dv_ref):
    scaling = width ** (-0.5)
    window, inside = head_window(head, width, q_ref.shape[1])
    inside_low = inside.astype(jnp.bfloat16)
    queries, grads = q_ref[:, window] * inside_low, g_ref[:, window] * inside_low
    key_rows = k_ref[:, window]
    lane = lax.broadcasted_iota(jnp.int32, (1, log_ref.shape[1]), 1)
    log_total = jnp.sum(jnp.where(lane == head, log_ref[...], 0.0), axis=-1, keepdims=True)
    weights = jnp.exp(dot_nt(queries, key_rows) * scaling - log_total)
    dv_ref[:, window] += dot_tn(weights.astype(jnp.bfloat16), grads)
    d_weights = dot_nt(grads, v_ref[:, window])
    inner = jnp.sum(weights * d_weights, axis=-1, keepdims=True)
    d_scores = (weights * (d_weights - inner)).astype(jnp.bfloat16)
    dq_ref[:, window] += jnp.dot(d_scores, key_rows, preferred_element_type=jnp.float32) * (
        inside * scaling
    )
    dk_ref[:, window] += dot_tn(d_scores, queries) * scaling


def run_heads(head_count, attend_one, actions):
    spread_over = {}
    for index, action in enumerate(actions):
        spread_over.setdefault(index * head_count // len(actions), []).append(action)

    def step(head, carry):
        attend_one(head)
        for when, group in spread_over.items():

            @pl.when(head == when)
            def _(group=group):
                for action in group:
                    action()

        return carry

    lax.fori_loop(0, head_count, step, 0)


def mix_rows(
    x_ref, start, length, first_slot, o_ref, slot_values, weights, attention, projected, mixed, hidden
):
    size = 128 if length % 128 == 0 else length

    def step(index, carry):
        own = pl.ds(pl.multiple_of(index * size, size), size)
        place = pl.ds(pl.multiple_of(start + index * size, size), size)
        values = slot_values[first_slot + index * size // length]
        head_gate, gate1, shift2, scale2, bias = (values[row : row + 1] for row in range(5))
        gated = (o_ref[place] * head_gate).astype(jnp.bfloat16)
        attention[place] = gated
        result = jnp.dot(gated, weights[...], preferred_element_type=jnp.float32) + bias
        projected[place] = result
        total = x_ref[own].astype(jnp.float32) + gate1 * result
        mixed[place] = total
        centred = total - jnp.mean(total, axis=-1, keepdims=True)
        variance = jnp.mean(centred * centred, axis=-1, keepdims=True)
        normed = centred * lax.rsqrt(variance + epsilon)
        hidden[place] = (normed * (1.0 + scale2) + shift2).astype(jnp.bfloat16)
        return carry

    lax.fori_loop(0, x_ref.shape[0] // size, step, 0)


def forward_kernel(half, layouts, orders, heads, *refs):
    count = len(layouts)
    q_ref, k_ref, v_ref = refs[:3]
    fc1_piece, fc1_line, fc2_piece = refs[3:6]
    lines = [[fc1_piece] + [fc1_line.at[step] for step in range(1, half)], [fc2_piece]]
    x_short, x_long, slot_values, weights = refs[6:10]
    refs = refs[10:]
    o_ref, log_ref, keys, values, *mixing = refs[:8]
    outs = refs[8 : 8 + count]
    send_sem, recv_sem, projection, projection_sem = refs[8 + count : 12 + count]
    at = Place(half)
    width = q_ref.shape[1] // heads
    rows = keys.shape[0] // 4
    short = q_ref.shape[0] - rows
    own = pl.ds(short, rows)
    beside, along = at.beside, at.along[1]

    def quarter(buffer, index):
        return buffer.at[pl.ds(index * rows, rows)]

    at.greet()
    sent = []

    def send(number, source, target, peer):
        copy = remote(source, target, send_sem.at[number], recv_sem.at[number], peer)
        copy.start()
        sent.append(copy)

    def got(number, target):
        remote(target, target, send_sem.at[number], recv_sem.at[number], along).wait_recv()

    send(0, k_ref.at[own], quarter(keys, 1), beside)
    send(1, v_ref.at[own], quarter(values, 2), along)
    send(2, v_ref.at[own], quarter(values, 1), beside)
    send(3, k_ref.at[own], quarter(keys, 2), along)
    pairs, local = gather_start(at, layouts, orders, lines, outs, *refs[12 + count :])
    load = pltpu.make_async_copy(weights.at[3], projection, projection_sem)
    load.start()
    actions = gather_actions(pairs, local)
    beside_first, settle, second, line_steps = count, 2 * count, 2 * count + 1, 2 * count + 2
    late = line_steps + half - 1
    for action in actions[:beside_first]:
        action()
    quarter(keys, 0)[...] = k_ref[own]
    quarter(values, 0)[...] = v_ref[own]
    o_ref[...] = jnp.zeros_like(o_ref)
    log_ref[...] = jnp.zeros_like(log_ref)

    def pass_on():
        got(0, quarter(keys, 1))
        send(4, quarter(keys, 1), quarter(keys, 3), along)
        got(1, quarter(values, 2))
        send(5, quarter(values, 2), quarter(values, 3), beside)

    first = pl.ds(0, short)
    run_heads(
        heads,
        lambda head: attend_head(
            head,
            width,
            q_ref.at[first],
            k_ref.at[first],
            v_ref.at[first],
            o_ref.at[first],
            log_ref.at[first],
        ),
        [],
    )
    pass_on()
    for action in (
        actions[beside_first : settle + 1] + actions[line_steps:late] + actions[second:line_steps]
    ):
        action()
    got(2, quarter(values, 1))
    got(3, quarter(keys, 2))
    got(4, quarter(keys, 3))
    got(5, quarter(values, 3))
    run_heads(
        heads,
        lambda head: attend_head(
            head, width, q_ref.at[own], keys, values, o_ref.at[own], log_ref.at[own]
        ),
        actions[late : late + 2],
    )
    for action in actions[late + 2 : -count]:
        action()
    load.wait()
    slots = slot_values.shape[0]
    mix_rows(x_short, 0, short // (slots - 1), 0, o_ref, slot_values, projection, *mixing)
    mix_rows(x_long, short, rows, slots - 1, o_ref, slot_values, projection, *mixing)
    for action in actions[-count:]:
        action()
    for copy in sent:
        copy.wait_send()


def attention_forward(q_rows, k_rows, v_rows, blocks, mixing, layouts, orders, heads, rows, number):
    half = lax.axis_size("fsdp") // 2
    count = len(layouts)
    vmem, hbm = pl.BlockSpec(memory_space=pltpu.VMEM), pl.BlockSpec(memory_space=pl.ANY)
    total, columns = q_rows.shape
    outs = [
        jax.ShapeDtypeStruct((total, columns), jnp.float32),
        jax.ShapeDtypeStruct((total, 128), jnp.float32),
        jax.ShapeDtypeStruct((4 * rows, columns), jnp.bfloat16),
        jax.ShapeDtypeStruct((4 * rows, columns), jnp.bfloat16),
        jax.ShapeDtypeStruct((total, columns), jnp.bfloat16),
        jax.ShapeDtypeStruct((total, columns), jnp.float32),
        jax.ShapeDtypeStruct((total, columns), jnp.float32),
        jax.ShapeDtypeStruct((total, columns), jnp.bfloat16),
    ] + [
        jax.ShapeDtypeStruct(whole_shape(layout, half, *blocks[0].shape), blocks[0].dtype)
        for layout in layouts
    ]
    return pl.pallas_call(
        functools.partial(forward_kernel, half, layouts, orders, heads),
        out_shape=outs,
        in_specs=[vmem] * (6 + len(blocks)) + [hbm],
        out_specs=[vmem] * 8 + [hbm] * count,
        scratch_shapes=[
            pltpu.SemaphoreType.DMA((6,)),
            pltpu.SemaphoreType.DMA((6,)),
            pltpu.VMEM((columns, columns), jnp.bfloat16),
            pltpu.SemaphoreType.DMA,
        ]
        + gather_scratch(count, half),
        compiler_params=pltpu.CompilerParams(
            collective_id=number, has_side_effects=True, vmem_limit_bytes=VMEM_BYTES
        ),
        cost_estimate=taking(120),
        name=f"attention{number}",
    )(q_rows, k_rows, v_rows, *blocks, *mixing)


def backward_kernel(half, layouts, orders, heads, *refs):
    count = len(layouts)
    q_ref, k_ref, v_ref, g_ref, log_ref, keys, values = refs[:7]
    terms = refs[7 : 7 + count]
    dq_out, dk_out, dv_out = refs[7 + count : 10 + count]
    outs = refs[10 + count : 10 + 2 * count]
    rest = refs[10 + 2 * count :]
    dq, dk, dv, wide, wide_got, slim, slim_got, send_sem, recv_sem = rest[:9]
    at = Place(half)
    width = q_ref.shape[1] // heads
    rows = keys.shape[0] // 4
    short = q_ref.shape[0] - rows
    own, first = pl.ds(short, rows), pl.ds(0, short)
    beside, along = at.beside, at.along[1]
    at.greet()
    pairs = scatter_start(at, layouts, orders, terms, outs, rest[9:])
    actions = scatter_actions(pairs)
    dq[...] = jnp.zeros_like(dq)
    dk[...] = jnp.zeros_like(dk)
    dv[...] = jnp.zeros_like(dv)
    sent = []

    def send(number, source, target, peer):
        copy = remote(source, target, send_sem.at[number], recv_sem.at[number], peer)
        copy.start()
        sent.append(copy)

    def got(number, target):
        remote(target, target, send_sem.at[number], recv_sem.at[number], along).wait_recv()

    def quarter(index):
        return pl.ds(index * rows, rows)

    split = 2 * count
    run_heads(
        heads,
        lambda head: attend_back_head(
            head,
            width,
            q_ref.at[own],
            keys,
            values,
            g_ref.at[own],
            log_ref.at[own],
            dq.at[own],
            dk,
            dv,
        ),
        actions[:split],
    )
    for part, (source, index) in enumerate([(dk, 2), (dk, 3), (dv, 1), (dv, 3)]):
        wide[part] = source[quarter(index)].astype(jnp.bfloat16)
    send(0, wide.at[pl.ds(0, 2)], wide_got.at[pl.ds(0, 2)], along)
    send(1, wide.at[pl.ds(2, 2)], wide_got.at[pl.ds(2, 2)], beside)
    short_dk, short_dv = dk.at[pl.ds(2 * rows, short)], dv.at[pl.ds(rows, short)]
    short_dk[...] = jnp.zeros_like(short_dk)
    short_dv[...] = jnp.zeros_like(short_dv)
    run_heads(
        heads,
        lambda head: attend_back_head(
            head,
            width,
            q_ref.at[first],
            k_ref.at[first],
            v_ref.at[first],
            g_ref.at[first],
            log_ref.at[first],
            dq.at[first],
            short_dk,
            short_dv,
        ),
        actions[split : split + 2],
    )
    dq_out[...] = dq[...].astype(jnp.bfloat16)
    dk_out[first] = short_dk[...].astype(jnp.bfloat16)
    dv_out[first] = short_dv[...].astype(jnp.bfloat16)
    got(0, wide_got.at[pl.ds(0, 2)])
    slim[0] = (dk[quarter(1)] + wide_got[1].astype(jnp.float32)).astype(jnp.bfloat16)
    send(2, slim.at[0], slim_got.at[0], beside)
    got(1, wide_got.at[pl.ds(2, 2)])
    slim[1] = (dv[quarter(2)] + wide_got[3].astype(jnp.float32)).astype(jnp.bfloat16)
    send(3, slim.at[1], slim_got.at[1], along)
    for action in actions[split + 2 : -count]:
        action()
    got(2, slim_got.at[0])
    total = dk[quarter(0)] + wide_got[0].astype(jnp.float32) + slim_got[0].astype(jnp.float32)
    dk_out[own] = total.astype(jnp.bfloat16)
    got(3, slim_got.at[1])
    total = dv[quarter(0)] + wide_got[2].astype(jnp.float32) + slim_got[1].astype(jnp.float32)
    dv_out[own] = total.astype(jnp.bfloat16)
    for action in actions[-count:]:
        action()
    for copy in sent:
        copy.wait_send()


def attention_backward(
    rows_in, keys, values, gradients, layouts, orders, heads, rows, columns, number
):
    half = lax.axis_size("fsdp") // 2
    count = len(gradients)
    vmem, hbm = pl.BlockSpec(memory_space=pltpu.VMEM), pl.BlockSpec(memory_space=pl.ANY)
    total, model_width = rows_in[0].shape
    quarter_rows = keys.shape[0] // 4
    low_rows = jax.ShapeDtypeStruct((total, model_width), jnp.bfloat16)
    return pl.pallas_call(
        functools.partial(backward_kernel, half, layouts, orders, heads),
        out_shape=[low_rows] * 3 + scatter_outs(count, half, rows, columns),
        in_specs=[vmem] * 7 + [hbm] * count,
        out_specs=[vmem] * (3 + count),
        scratch_shapes=[
            pltpu.VMEM((total, model_width), jnp.float32),
            pltpu.VMEM((4 * quarter_rows, model_width), jnp.float32),
            pltpu.VMEM((4 * quarter_rows, model_width), jnp.float32),
            pltpu.VMEM((4, quarter_rows, model_width), jnp.bfloat16),
            pltpu.VMEM((4, quarter_rows, model_width), jnp.bfloat16),
            pltpu.VMEM((2, quarter_rows, model_width), jnp.bfloat16),
            pltpu.VMEM((2, quarter_rows, model_width), jnp.bfloat16),
            pltpu.SemaphoreType.DMA((4,)),
            pltpu.SemaphoreType.DMA((4,)),
        ]
        + scatter_scratch(count, half, rows, columns),
        compiler_params=pltpu.CompilerParams(
            collective_id=number, has_side_effects=True, vmem_limit_bytes=VMEM_BYTES
        ),
        cost_estimate=taking(150),
        name=f"attention{number}",
    )(*rows_in, keys, values, *gradients)


def product(left, right):
    return jnp.dot(left, right, preferred_element_type=jnp.float32)


def product_tn(left, right):
    return lax.dot_general(
        left, right, (((0,), (0,)), ((), ())), preferred_element_type=jnp.float32
    )


def product_nt(left, right):
    return lax.dot_general(
        left, right, (((1,), (1,)), ((), ())), preferred_element_type=jnp.float32
    )


def spread(per_slot, short_count, len_short, quarter_rows):
    short_rows = short_count * len_short
    row = lax.broadcasted_iota(jnp.int32, (short_rows + quarter_rows, 1), 0)
    result = per_slot[short_count][None]
    for slot in range(short_count):
        result = jnp.where(row < (short_count - slot) * len_short, per_slot[short_count - 1 - slot][None], result)
    return result


def slot_sum(values, short_count, len_short):
    short_rows = short_count * len_short
    short_part = jnp.sum(
        values[:short_rows].reshape((short_count, len_short) + values.shape[1:]), axis=1
    )
    long_part = jnp.sum(values[short_rows:], axis=0, keepdims=True)
    return jnp.concatenate([short_part, long_part], 0)


def norm_parts(values):
    average = jnp.mean(values, axis=-1, keepdims=True)
    centred = values - average
    variance = jnp.mean(centred * centred, axis=-1, keepdims=True)
    inverse = lax.rsqrt(variance + epsilon)
    return (centred * inverse, inverse)


def norm_back(gradient, normed, inverse):
    return inverse * (
        gradient
        - jnp.mean(gradient, axis=-1, keepdims=True)
        - normed * jnp.mean(gradient * normed, axis=-1, keepdims=True)
    )


def silu_grad(values):
    sigmoid_value = jax.nn.sigmoid(values)
    return sigmoid_value * (1.0 + values * (1.0 - sigmoid_value))


def gelu_tanh(values):
    return jax.nn.gelu(values, approximate=True)


def per_device(
    x_short,
    x_long,
    short_cond,
    long_cond,
    short_heads,
    long_heads,
    short_groups,
    long_groups,
    short_keep,
    long_keep,
    w_ada,
    b_ada,
    w_head_router,
    w_group_router,
    w_qkv,
    w_proj,
    b_proj,
    w_fc1,
    b_fc1,
    w_fc2,
    b_fc2,
    g_short,
    g_long,
):
    short_count, len_short, model_width = x_short.shape
    quarter_rows = x_long.shape[0]
    head_count = w_head_router.shape[1]
    head_width = model_width // head_count
    group_count = w_group_router.shape[1]
    slot_count = short_count + 1
    short_rows = short_count * len_short
    row_count = short_rows + quarter_rows
    fsdp_index = lax.axis_index("fsdp")
    fsdp_count = lax.axis_size("fsdp")
    role = lax.axis_index("dp")
    group_row = fsdp_index // SPLIT
    half = fsdp_count // 2
    shard_rows = w_qkv.shape[0]
    unit_rows = w_fc2.shape[0] // 4
    mixed_shard = jnp.concatenate([w_qkv, w_proj], 1)
    attention_piece = lax.dynamic_slice_in_dim(mixed_shard, role * model_width, model_width, 1)
    fc1_piece = lax.dynamic_slice_in_dim(w_fc1, role * model_width, model_width, 1)
    fc2_piece = lax.dynamic_slice_in_dim(w_fc2, role * unit_rows, unit_rows, 0)
    short_act = low(jax.nn.silu(short_cond))
    long_act = low(jax.nn.silu(long_cond))
    message = exchange(packed([short_act, b_proj, b_fc1, b_fc2], 16), "fsdp", False, 0)
    act_rows, proj_bias, fc1_bias, fc2_bias = unpacked(
        message, [(model_width,), b_proj.shape, b_fc1.shape, b_fc2.shape]
    )
    proj_bias, fc1_bias, fc2_bias = (
        bias.reshape(-1).astype(jnp.float32) for bias in (proj_bias, fc1_bias, fc2_bias)
    )
    item_act = jnp.concatenate([act_rows, long_act], 0)
    own_long_act = lax.dynamic_slice_in_dim(long_act, group_row, 1, 0)
    item_columns = lax.dynamic_slice_in_dim(item_act, fsdp_index * shard_rows, shard_rows, 1)
    bias_row = lax.dynamic_update_slice_in_dim(
        jnp.zeros((fsdp_count * b_ada.shape[0],), jnp.float32),
        b_ada.astype(jnp.float32),
        fsdp_index * b_ada.shape[0],
        0,
    )
    partial = jnp.concatenate(
        [
            product(item_columns, w_ada) + bias_row,
            product(item_columns, w_head_router),
            product(item_columns, w_group_router),
        ],
        1,
    )
    width = partial.shape[1]
    for_device = jnp.stack(
        [partial[:fsdp_count], jnp.repeat(partial[fsdp_count:], SPLIT, axis=0)], 1
    ).reshape(fsdp_count, -1)
    for_device = low(jnp.pad(for_device, ((0, 0), (0, -for_device.shape[1] % 2048))))
    attention_full, fc1_line, shares = gather(
        attention_piece,
        BY_ROLE,
        (True, False),
        fc1_piece,
        for_device.reshape(fsdp_count, -1, 128),
        2,
    )
    conditioned = unpacked(jnp.sum(shares.astype(jnp.float32), axis=0), [(2, width)])[0]
    attention_full = attention_full.reshape(4, -1, model_width)
    mod_width = 6 * model_width
    modulation = conditioned[:, :mod_width]
    head_sigmoid = jax.nn.sigmoid(conditioned[:, mod_width : mod_width + head_count])
    group_sigmoid = jax.nn.sigmoid(conditioned[:, mod_width + head_count :])
    head_mask = jnp.concatenate(
        [short_heads, lax.dynamic_slice_in_dim(long_heads, group_row, 1, 0)], 0
    ).astype(jnp.float32)
    group_mask = jnp.concatenate(
        [short_groups, lax.dynamic_slice_in_dim(long_groups, group_row, 1, 0)], 0
    ).astype(jnp.float32)
    head_gate = head_mask * 2.0 * head_sigmoid
    group_gate = group_mask * 2.0 * group_sigmoid
    shift1, scale1, gate1, shift2, scale2, gate2 = jnp.split(
        spread(modulation, short_count, len_short, quarter_rows), 6, axis=1
    )
    x_rows = jnp.concatenate([x_short.reshape(short_rows, model_width), x_long], 0).astype(
        jnp.float32
    )
    keep_rows = jnp.concatenate([short_keep.reshape(short_rows), long_keep], 0).astype(jnp.float32)[
        :, None
    ]
    normed1, inverse1 = norm_parts(x_rows)
    hidden1 = low(normed1 * (1.0 + scale1) + shift1)
    q_rows, k_rows, v_rows = (low(product(hidden1, attention_full[part])) for part in range(3))

    head_columns = jnp.repeat(head_gate, head_width, axis=1)
    pieces = modulation.reshape(slot_count, 6, model_width)
    slot_values = jnp.stack(
        [
            head_columns,
            pieces[:, 2],
            pieces[:, 3],
            pieces[:, 4],
            jnp.broadcast_to(proj_bias, (slot_count, model_width)),
        ],
        1,
    )
    slot_values = jnp.pad(slot_values, ((0, 0), (0, 3), (0, 0)))
    (
        head_rows,
        log_rows,
        keys,
        values,
        attention,
        projected,
        mixed,
        hidden2,
        fc1_full,
        fc2_full,
    ) = attention_forward(
        q_rows,
        k_rows,
        v_rows,
        [fc1_piece, fc1_line, fc2_piece],
        [x_short.reshape(short_rows, model_width), x_long, slot_values, attention_full],
        (BY_COLUMN, BY_SHARD),
        ((True, False), (True, False)),
        head_count,
        quarter_rows,
        3,
    )
    head_gate_rows = spread(head_columns, short_count, len_short, quarter_rows)
    fc1_full = fc1_full.reshape(model_width, -1)
    fc2_full = fc2_full.reshape(-1, model_width)
    normed2, inverse2 = norm_parts(mixed)
    channel_gate = spread(
        jnp.repeat(group_gate, CHAN, axis=1), short_count, len_short, quarter_rows
    )
    up_rows = product(hidden2, fc1_full) + fc1_bias
    gelu_value, gelu_pull = jax.vjp(gelu_tanh, up_rows)
    activated = low(gelu_value * channel_gate)
    down_rows = product(activated, fc2_full) + fc2_bias
    out_rows = mixed + gate2 * keep_rows * down_rows
    y_short = low(out_rows[:short_rows].reshape(x_short.shape))
    y_long = low(out_rows[short_rows:])
    gradient = jnp.concatenate([g_short.reshape(short_rows, model_width), g_long], 0).astype(
        jnp.float32
    )
    d_down = low(gradient * gate2 * keep_rows)
    slot_gate2 = slot_sum(gradient * keep_rows * down_rows, short_count, len_short)
    grad_fc2 = low(product_tn(activated, d_down)).reshape(half, 2, 4, unit_rows, model_width)
    d_activated = product_nt(d_down, fc2_full)
    d_channel = slot_sum(d_activated * gelu_value, short_count, len_short)
    d_group = jnp.sum(d_channel.reshape(slot_count, group_count, CHAN), axis=-1)
    d_up = low(gelu_pull(d_activated * channel_gate)[0])
    grad_fc1 = low(product_tn(hidden2, d_up)).reshape(half, 2, shard_rows, -1)
    d_hidden2 = product_nt(d_up, fc1_full)

    slot_shift2 = slot_sum(d_hidden2, short_count, len_short)
    slot_scale2 = slot_sum(d_hidden2 * normed2, short_count, len_short)
    d_mixed = gradient + norm_back(d_hidden2 * (1.0 + scale2), normed2, inverse2)
    d_projected = low(d_mixed * gate1)
    slot_gate1 = slot_sum(d_mixed * projected, short_count, len_short)
    d_attention = product_nt(d_projected, attention_full[3])
    d_head = slot_sum(d_attention * head_rows, short_count, len_short)
    d_head = jnp.sum(d_head.reshape(slot_count, head_count, head_width), axis=-1)
    d_heads = low(d_attention * head_gate_rows)
    bias_grad = jnp.concatenate(
        [jnp.sum(part, axis=0, dtype=jnp.float32) for part in (d_projected, d_up, d_down)]
    )
    dq_rows, dk_rows, dv_rows, fc1_near, fc2_near = attention_backward(
        [q_rows, k_rows, v_rows, d_heads, log_rows],
        keys,
        values,
        [grad_fc1, grad_fc2],
        (BY_COLUMN, BY_SHARD),
        ((True, False), (True, True)),
        head_count,
        shard_rows,
        model_width,
        4,
    )
    d_hidden1 = (
        product_nt(dq_rows, attention_full[0])
        + product_nt(dk_rows, attention_full[1])
        + product_nt(dv_rows, attention_full[2])
    )
    slot_shift1 = slot_sum(d_hidden1, short_count, len_short)
    slot_scale1 = slot_sum(d_hidden1 * normed1, short_count, len_short)
    d_rows = d_mixed + norm_back(d_hidden1 * (1.0 + scale1), normed1, inverse1)
    dx_short = low(d_rows[:short_rows].reshape(x_short.shape))
    dx_long = low(d_rows[short_rows:])
    d_head_logit = d_head * head_mask * 2.0 * head_sigmoid * (1.0 - head_sigmoid)
    d_group_logit = d_group * group_mask * 2.0 * group_sigmoid * (1.0 - group_sigmoid)
    d_conditioned = jnp.concatenate(
        [
            slot_shift1,
            slot_scale1,
            slot_gate1,
            slot_shift2,
            slot_scale2,
            slot_gate2,
            d_head_logit,
            d_group_logit,
        ],
        1,
    )
    message = packed([low(d_conditioned), low(bias_grad), short_act, own_long_act], 16)
    attention_sum, all_rows, fc1_sum, fc2_sum = scatter_products(
        [hidden1, attention],
        [dq_rows, dk_rows, dv_rows, d_projected],
        (True, False),
        message,
        [fc1_near, fc2_near],
        5,
    )
    g_w_fc1 = fc1_sum.transpose(1, 0, 2).reshape(shard_rows, -1).astype(jnp.float32)
    g_w_fc2 = fc2_sum.reshape(-1, model_width).astype(jnp.float32)
    all_rows, bias_rows, all_short, all_long = unpacked(
        all_rows, [(2, width), bias_grad.shape, (model_width,), (model_width,)]
    )
    long_sum = jnp.sum(
        all_rows[:, :, 1].astype(jnp.float32).reshape(4, -1, SPLIT, width), axis=2
    )
    factors = jnp.concatenate([all_rows[:, :, 0], low(long_sum)], 1)
    d_items = lax.dynamic_index_in_dim(factors, role, 0, keepdims=False)
    d_silu = (
        product_nt(d_items[:, :mod_width], w_ada)
        + product_nt(d_items[:, mod_width : mod_width + head_count], w_head_router)
        + product_nt(d_items[:, mod_width + head_count :], w_group_router)
    )
    gathered = exchange(packed([d_silu], 8), "fsdp", False, 7)
    gathered, later_sum = lax.optimization_barrier((gathered, attention_sum))
    attention_grad = four_roles(along_line(attention_sum, later_sum))
    g_w_qkv = attention_grad[:3].transpose(1, 0, 2).reshape(shard_rows, -1)
    g_w_proj = attention_grad[3]
    d_silu = unpacked(gathered, [d_silu.shape])[0]
    d_silu = d_silu.transpose(1, 0, 2).reshape(-1, model_width)
    d_short_cond = lax.dynamic_slice_in_dim(d_silu, fsdp_index, 1, 0) * silu_grad(short_cond)
    d_long_cond = d_silu[fsdp_count:] * silu_grad(long_cond)
    act_factors = jnp.concatenate([all_short, all_long[:, ::SPLIT]], 1)
    act_factors = lax.dynamic_slice_in_dim(
        act_factors, fsdp_index * shard_rows, shard_rows, 2
    ).reshape(-1, shard_rows)
    factors = factors.reshape(-1, width)
    g_w_ada = product_tn(act_factors, factors[:, :mod_width])
    g_w_head_router = product_tn(act_factors, factors[:, mod_width : mod_width + head_count])
    g_w_group_router = product_tn(act_factors, factors[:, mod_width + head_count :])
    g_b_ada = lax.dynamic_slice_in_dim(
        jnp.sum(factors[:, :mod_width].astype(jnp.float32), axis=0),
        fsdp_index * b_ada.shape[0],
        b_ada.shape[0],
        0,
    )
    bias_sum = jnp.sum(bias_rows.astype(jnp.float32), axis=(0, 1))

    def own_bias(start, count):
        return lax.dynamic_slice_in_dim(bias_sum, start + fsdp_index * count, count, 0)

    g_b_proj = own_bias(0, shard_rows)
    g_b_fc1 = own_bias(model_width, 4 * shard_rows)
    g_b_fc2 = own_bias(5 * model_width, shard_rows)
    return (
        y_short,
        y_long,
        dx_short,
        dx_long,
        d_short_cond,
        d_long_cond,
        g_w_ada,
        g_b_ada,
        g_w_head_router,
        g_w_group_router,
        g_w_qkv,
        g_w_proj,
        g_b_proj,
        g_w_fc1,
        g_b_fc1,
        g_w_fc2,
        g_b_fc2,
    )


def solution(mesh):
    return jax.shard_map(
        per_device,
        mesh=mesh,
        in_specs=(
            P(("dp", "fsdp"), None, None),
            P(("dp", "fsdp"), None),
            P(("dp", "fsdp"), None),
            P("dp", None),
            P(("dp", "fsdp"), None),
            P("dp", None),
            P(("dp", "fsdp"), None),
            P("dp", None),
            P(("dp", "fsdp"), None),
            P(("dp", "fsdp")),
            P("fsdp", None),
            P("fsdp"),
            P("fsdp", None),
            P("fsdp", None),
            P("fsdp", None),
            P("fsdp", None),
            P("fsdp"),
            P("fsdp", None),
            P("fsdp"),
            P("fsdp", None),
            P("fsdp"),
            P(("dp", "fsdp"), None, None),
            P(("dp", "fsdp"), None),
        ),
        out_specs=(
            P(("dp", "fsdp"), None, None),
            P(("dp", "fsdp"), None),
            P(("dp", "fsdp"), None, None),
            P(("dp", "fsdp"), None),
            P(("dp", "fsdp"), None),
            P("dp", None),
            P("fsdp", None),
            P("fsdp"),
            P("fsdp", None),
            P("fsdp", None),
            P("fsdp", None),
            P("fsdp", None),
            P("fsdp"),
            P("fsdp", None),
            P("fsdp"),
            P("fsdp", None),
            P("fsdp"),
        ),
        check_vma=False,
    )
```
